128 devices in a mesh: lev: 4 (over z), lat: 4 (over y_hi, core), lon: 8 (over y_lo, x).
Axes of the slice: x: 4, y: 4 (y_hi: 2, y_lo: 2; y = y_hi * 2 + y_lo), z: 4, core: 2. Of those that a mesh axis runs over, the one named last changes fastest.
Arguments:
- latent: bfloat16 [256, 128, 1024], P(None, 'lat', 'lon'), may hold values from -6 to 6
- conv_weight: bfloat16 [16, 128, 9, 256], P('lev'), may hold values from -0.125 to 0.125
- mid_weight: bfloat16 [16, 128, 128], P('lev'), may hold values from -0.5 to 0.5
- out_weight: bfloat16 [16, 48, 128], P('lev'), may hold values from -0.5 to 0.5
- vertical_inner_matrix: bfloat16 [1024, 768], replicated, may hold values from -0.21875 to 0.21875
- vertical_outer_matrix: bfloat16 [768, 1024], replicated, may hold values from -0.1875 to 0.1875
- obs_values: float32 [4, 8, 256, 768], P('lat', 'lon'), may hold values from -6 to 6
- obs_weight: float32 [768], replicated, may hold values from 0.25 to 4
- obs_index: int32 [4, 8, 256], P('lat', 'lon'), may hold values from 0 to 4095
- obs_count: int32 [4, 8], P('lat', 'lon'), may hold values from 64 to 256
Outputs:
- latent_grad: float32 [256, 128, 1024], P('lev', 'lat', 'lon')
The draws below stay inside these ranges and needn't reach their ends.
Inputs may be any that keep to these rules, and one draw needn't show every extreme that they name: `obs_index`: row-major index of a cell within its tile of 32 x 128 cells; indices may repeat. `obs_count`: slots from this number on hold no observation.
All inputs are finite; a program needn't handle non-finite values.
Results may differ from the reference program's by a relative error of at most 0.007.
Values may be sent and summed in bfloat16 or wider, within the bound.
A program may use at most 192 MiB of HBM per device.

```python
import math
import jax
import jax.numpy as jnp
from jax import lax

LATENT = 256
DEC_HID = 128
LEVCH = 48
MLP_HID = 1024
LAT_DEV = 32
LON_DEV = 128
OBS = 256
GROUPS = 16
VERTICAL_QUANTA = 768
LAT = 128
LON = 1024
N_LAT = 4
N_LON = 8


def set_ends(drawn, rng, least, high):
    index_at = [jax.random.randint(jax.random.fold_in(rng, axis), (), 0, length) for axis, length in enumerate(drawn.shape)]
    longest = drawn.shape.index(max(drawn.shape))
    next_to = index_at[:longest] + [(index_at[longest] + 1) % drawn.shape[longest]] + index_at[longest + 1:]
    return drawn.at[tuple(index_at)].set(least).at[tuple(next_to)].set(high)


def steps_of(own_key, dims, cuts, smallest, high):
    level, own = 1.0, jax.random.fold_in(own_key, 6)
    for dim, blocks in cuts:
        steps = jnp.exp(jax.random.uniform(jax.random.fold_in(own, dim), (blocks,), jnp.float32, smallest / len(cuts), high / len(cuts)))
        level = level * jnp.repeat(steps, dims[dim] // blocks).reshape([-1 if axis == dim else 1 for axis in range(len(dims))])
    return level


def noise(key, extent, spread, limit, split=(), kind=jnp.bfloat16):
    array = spread * jax.random.normal(key, extent, jnp.float32)
    if split:
        array = array * steps_of(key, extent, split, -0.22, 0.18)
    return jnp.clip(array, -limit, limit).astype(kind)


def setup_inputs(seed: int = 0) -> dict:
    streams_of = jax.random.split(jax.random.key(seed), 11)
    return {
        "latent": noise(streams_of[0], (LATENT, LAT, LON), 1.0, 6.0, ((1, 4), (2, 8))),
        "conv_weight": noise(streams_of[1], (GROUPS, DEC_HID, 9, LATENT), (9 * LATENT) ** -0.5, 0.125, ((0, 4),)),
        "mid_weight": noise(streams_of[2], (GROUPS, DEC_HID, DEC_HID), DEC_HID ** -0.5, 0.5, ((0, 4),)),
        "out_weight": noise(streams_of[3], (GROUPS, LEVCH, DEC_HID), DEC_HID ** -0.5, 0.5, ((0, 4),)),
        "vertical_inner_matrix": noise(streams_of[4], (MLP_HID, VERTICAL_QUANTA), VERTICAL_QUANTA ** -0.5, 0.21875),
        "vertical_outer_matrix": noise(streams_of[5], (VERTICAL_QUANTA, MLP_HID), MLP_HID ** -0.5, 0.1875),
        "obs_values": noise(streams_of[6], (N_LAT, N_LON, OBS, VERTICAL_QUANTA), 1.0, 6.0, ((0, 4), (1, 8)), jnp.float32),
        "obs_weight": jnp.clip(jnp.exp(jax.random.uniform(streams_of[7], (VERTICAL_QUANTA,), jnp.float32, math.log(0.25), math.log(4.0))), 0.25, 4.0),
        "obs_index": set_ends(jax.random.randint(streams_of[8], (N_LAT, N_LON, OBS), 0, LAT_DEV * LON_DEV), jax.random.fold_in(streams_of[8], 1), 0, (LAT_DEV * LON_DEV) - 1).astype(jnp.int32),
        "obs_count": set_ends(jax.random.randint(streams_of[9], (N_LAT, N_LON), OBS // 4, OBS + 1), jax.random.fold_in(streams_of[9], 1), OBS // 4, OBS).astype(jnp.int32),
    }


KAPPA = 0.7978845608028654
CUBIC = 0.044715


def gelu_slope(pre):
    tanh_v = jnp.tanh(KAPPA * (pre + CUBIC * pre * pre * pre))
    value = 0.5 * pre * (1.0 + tanh_v)
    slope = 0.5 * (1.0 + tanh_v) + 0.5 * pre * (1.0 - tanh_v * tanh_v) * KAPPA * (1.0 + 3.0 * CUBIC * pre * pre)
    return value, slope


def extend(field):
    wrapped = jnp.concatenate([field[..., -1:], field, field[..., :1]], -1)
    zero_fill = jnp.zeros(wrapped.shape[:-2] + (1, wrapped.shape[-1]), wrapped.dtype)
    return jnp.concatenate([zero_fill, wrapped, zero_fill], -2)


def reference(latent, conv_weight, mid_weight, out_weight, vertical_inner_matrix, vertical_outer_matrix, obs_values, obs_weight, obs_index, obs_count):
    objective_amount = LAT * LON
    padded = extend(latent)
    stacked = jnp.stack([padded[:, a:a + LAT, b:b + LON] for a in range(3) for b in range(3)], 0).reshape(9 * LATENT, objective_amount)

    def forward(weights):
        kernel, middle, outer = weights
        pre_one = jnp.dot(kernel.reshape(DEC_HID, 9 * LATENT), stacked, preferred_element_type=jnp.float32)
        act_one, slope_one = gelu_slope(pre_one)
        pre_two = jnp.dot(middle, act_one.astype(jnp.bfloat16), preferred_element_type=jnp.float32)
        act_two, slope_two = gelu_slope(pre_two)
        decoded_layers = jnp.dot(outer, act_two.astype(jnp.bfloat16), preferred_element_type=jnp.float32).astype(jnp.bfloat16)
        return decoded_layers, slope_one, slope_two

    decoded_layers = lax.map(lambda w: forward(w)[0], (conv_weight, mid_weight, out_weight)).reshape(VERTICAL_QUANTA, objective_amount)
    pre_col = jnp.dot(vertical_inner_matrix, decoded_layers, preferred_element_type=jnp.float32)
    vertical_hidden_response, vertical_derivative_factor = gelu_slope(pre_col)
    predicted_vector = decoded_layers.astype(jnp.float32) + jnp.dot(vertical_outer_matrix, vertical_hidden_response.astype(jnp.bfloat16), preferred_element_type=jnp.float32)

    tile_row = lax.broadcasted_iota(jnp.int32, (N_LAT, N_LON, OBS), 0)
    tile_col = lax.broadcasted_iota(jnp.int32, (N_LAT, N_LON, OBS), 1)
    slot = lax.broadcasted_iota(jnp.int32, (N_LAT, N_LON, OBS), 2)
    measurement_sites = ((tile_row * LAT_DEV + obs_index // LON_DEV) * LON + tile_col * LON_DEV + obs_index % LON_DEV).reshape(-1).astype(jnp.int32)
    live = (slot < obs_count[:, :, None]).astype(jnp.float32).reshape(-1)
    measurement_entries = jnp.take(predicted_vector, measurement_sites, axis=1)
    measurement_residual = (measurement_entries - obs_values.reshape(-1, VERTICAL_QUANTA).T) * live[None, :] * obs_weight[:, None]
    prediction_adjoint = jnp.zeros((VERTICAL_QUANTA, objective_amount), jnp.float32).at[:, measurement_sites].add(measurement_residual)

    hidden_response_adjoint = (jnp.dot(vertical_outer_matrix.T, prediction_adjoint.astype(jnp.bfloat16), preferred_element_type=jnp.float32) * vertical_derivative_factor).astype(jnp.bfloat16)
    gridded_adjoint = (prediction_adjoint + jnp.dot(vertical_inner_matrix.T, hidden_response_adjoint, preferred_element_type=jnp.float32)).astype(jnp.bfloat16)
    grad_groups = gridded_adjoint.reshape(GROUPS, LEVCH, objective_amount)

    def backward(carry, items):
        kernel, middle, outer, grad_f = items
        fields_g, slope_one, slope_two = forward((kernel, middle, outer))
        grad_two = (jnp.dot(outer.T, grad_f, preferred_element_type=jnp.float32) * slope_two).astype(jnp.bfloat16)
        grad_one = (jnp.dot(middle.T, grad_two, preferred_element_type=jnp.float32) * slope_one).astype(jnp.bfloat16)
        rim = extend(grad_one.reshape(DEC_HID, LAT, LON))
        taps = jnp.stack([rim[:, 2 - a:2 - a + LAT, 2 - b:2 - b + LON] for a in range(3) for b in range(3)], 1).reshape(DEC_HID, 9, objective_amount)
        term = jnp.einsum("okc,okp->cp", kernel.astype(jnp.float32), taps.astype(jnp.float32))
        return carry + term, None

    summed, _ = lax.scan(backward, jnp.zeros((LATENT, objective_amount), jnp.float32), (conv_weight, mid_weight, out_weight, grad_groups))
    return (latent.astype(jnp.float32).reshape(LATENT, objective_amount) + summed).reshape(LATENT, LAT, LON)
```

```python
import jax
import jax.numpy as jnp
from jax import lax
from jax.sharding import PartitionSpec as P

KAPPA = 0.7978845608028654
CUBIC = 0.044715


def ring(shard, axis, up):
    size = lax.axis_size(axis)
    step = 1 if up else -1
    return lax.ppermute(shard, axis, [(i, (i + step) % size) for i in range(size)])


def extended(shard, sides):
    for axis, dim in sides:
        length = shard.shape[dim]
        before = ring(lax.slice_in_dim(shard, length - 1, length, axis=dim), axis, True)
        after = ring(lax.slice_in_dim(shard, 0, 1, axis=dim), axis, False)
        if axis == "lat":
            index = lax.axis_index("lat")
            before = jnp.where(index == 0, jnp.zeros_like(before), before)
            after = jnp.where(index == lax.axis_size("lat") - 1, jnp.zeros_like(after), after)
        shard = jnp.concatenate([before, shard, after], axis=dim)
    return shard


def gelu_slope(pre):
    tanh_v = jnp.tanh(KAPPA * (pre + CUBIC * pre * pre * pre))
    value = 0.5 * pre * (1.0 + tanh_v)
    slope = 0.5 * (1.0 + tanh_v) + 0.5 * pre * (1.0 - tanh_v * tanh_v) * KAPPA * (
        1.0 + 3.0 * CUBIC * pre * pre
    )
    return (value, slope)


def dot(spec, *args):
    return jnp.einsum(spec, *args, preferred_element_type=jnp.float32)


def per_device(
    latent,
    conv_weight,
    mid_weight,
    out_weight,
    vertical_inner_matrix,
    vertical_outer_matrix,
    obs_values,
    obs_weight,
    obs_index,
    obs_count,
):
    bf16 = jnp.bfloat16
    chans, rows, cols = latent.shape
    groups, hidden = conv_weight.shape[:2]
    levels = out_weight.shape[1]
    slots = obs_index.shape[-1]
    lev = lax.axis_index("lev")
    lev_count = lax.axis_size("lev")
    wide = cols + 2
    padded = extended(latent, (("lat", 1), ("lon", 2))).reshape(chans, (rows + 2) * wide)
    span = (rows - 1) * wide + cols
    index = obs_index[0, 0]
    place = (index // cols) * wide + index % cols
    live = (lax.broadcasted_iota(jnp.int32, (slots,), 0) < obs_count[0, 0]).astype(jnp.float32)
    pick = (place[:, None] == lax.broadcasted_iota(jnp.int32, (slots, span), 1)).astype(bf16)
    offsets = [a * wide + b for a in range(3) for b in range(3)]
    patches = jnp.stack(
        [dot("kp,cp->kc", pick, padded[:, o : o + span]).astype(bf16) for o in offsets], 1
    )
    pre_one = dot("ktc,gotc->kgo", patches, conv_weight)
    act_one, slope_one = gelu_slope(pre_one)
    pre_two = dot("kgi,goi->kgo", act_one.astype(bf16), mid_weight)
    act_two, slope_two = gelu_slope(pre_two)
    own = dot("kgi,goi->kgo", act_two.astype(bf16), out_weight).astype(bf16)
    fields = lax.all_gather(own.reshape(slots, groups * levels), "lev", axis=1, tiled=True)
    pre_col = dot("kf,hf->kh", fields, vertical_inner_matrix)
    act_col, slope_col = gelu_slope(pre_col)
    forecast = fields.astype(jnp.float32) + dot("kh,fh->kf", act_col.astype(bf16), vertical_outer_matrix)
    misfit = (forecast - obs_values[0, 0]) * live[:, None] * obs_weight[None, :]
    grad_act = (dot("kf,fh->kh", misfit.astype(bf16), vertical_outer_matrix) * slope_col).astype(bf16)
    grad_fields = (misfit + dot("kh,hf->kf", grad_act, vertical_inner_matrix)).astype(bf16)
    grad_own = lax.dynamic_slice_in_dim(grad_fields, lev * groups * levels, groups * levels, 1)
    grad_own = grad_own.reshape(slots, groups, levels)
    grad_two = (dot("kgo,goi->kgi", grad_own, out_weight) * slope_two).astype(bf16)
    grad_one = (dot("kgo,goi->kgi", grad_two, mid_weight) * slope_one).astype(bf16)
    taps = dot("kgo,gotc->ctk", grad_one, conv_weight).astype(bf16)
    taps = lax.psum_scatter(taps, "lev", scatter_dimension=0, tiled=True)
    portion = chans // lev_count
    result = jnp.zeros((portion, (rows + 2) * wide), jnp.float32)
    for t, o in enumerate(offsets):
        result = result.at[:, o : o + span].add(dot("ck,kp->cp", taps[:, t, :], pick))
    result = result.reshape(portion, rows + 2, wide)
    left, right = result[:, :, :1].astype(bf16), result[:, :, -1:].astype(bf16)
    result = result[:, :, 1:-1]
    result = result.at[:, :, :1].add(ring(right, "lon", True).astype(jnp.float32))
    result = result.at[:, :, -1:].add(ring(left, "lon", False).astype(jnp.float32))
    top, bottom = result[:, :1].astype(bf16), result[:, -1:].astype(bf16)
    from_north = ring(bottom, "lat", True).astype(jnp.float32)
    from_south = ring(top, "lat", False).astype(jnp.float32)
    lat = lax.axis_index("lat")
    from_north = jnp.where(lat == 0, 0.0, from_north)
    from_south = jnp.where(lat == lax.axis_size("lat") - 1, 0.0, from_south)
    result = result[:, 1:-1].at[:, :1].add(from_north).at[:, -1:].add(from_south)
    mine = lax.dynamic_slice_in_dim(latent, lev * portion, portion, 0).astype(jnp.float32)
    return mine + result


def solution(mesh):
    return jax.shard_map(
        per_device,
        mesh=mesh,
        in_specs=(
            P(None, "lat", "lon"),
            P("lev", None, None, None),
            P("lev", None, None),
            P("lev", None, None),
            P(),
            P(),
            P("lat", "lon", None, None),
            P(),
            P("lat", "lon", None),
            P("lat", "lon"),
        ),
        out_specs=P("lev", "lat", "lon"),
        check_vma=False,
    )
```

```python
import functools

import jax
import jax.numpy as jnp
from jax import lax
from jax.experimental import pallas as pl
from jax.experimental.pallas import tpu as pltpu
from jax.sharding import PartitionSpec as P

KAPPA = 0.7978845608028654
CUBIC = 0.044715
F32 = jnp.float32
BF16 = jnp.bfloat16
MESH = pl.DeviceIdType.MESH


def gelu_slope(pre):
    tanh_v = jnp.tanh(KAPPA * (pre + CUBIC * pre * pre * pre))
    half = 0.5 * (1.0 + tanh_v)
    value = pre * half
    slope = half + 0.5 * pre * (1.0 - tanh_v * tanh_v) * (KAPPA + 3.0 * KAPPA * CUBIC * pre * pre)
    return (value, slope)


def dot_nn(x, y):
    return lax.dot_general(x, y, (((1,), (0,)), ((), ())), preferred_element_type=F32)


def dot_nt(x, y):
    return lax.dot_general(x, y, (((1,), (1,)), ((), ())), preferred_element_type=F32)


def iota(shape, dim):
    return lax.broadcasted_iota(jnp.int32, shape, dim)


def loop(count, body, unroll=1):
    def step(i, carry):
        body(i)
        return carry

    lax.fori_loop(0, count, step, 0, unroll=unroll)


def kernel(
    latent_hbm,
    conv_hbm,
    mid_ref,
    out_ref,
    inner_hbm,
    outer_hbm,
    obs_hbm,
    weight_ref,
    index_ref,
    count_ref,
    grad_ref,
    raw,
    wide,
    slab,
    conv,
    inner,
    outer,
    obs,
    pick,
    edge,
    side_pick,
    side_send,
    side,
    north,
    south,
    pre,
    act,
    slope_one,
    slope_two,
    slope_col,
    fields,
    fields_t,
    cast,
    misfit,
    out_pad,
    eye,
    taps,
    taps_in,
    summed,
    up_part,
    mid_part,
    down_part,
    row_send,
    row_in,
    side_out,
    side_in,
    load_sem,
    halo_send,
    halo_recv,
    field_send,
    field_recv,
    taps_send,
    taps_recv,
    back_send,
    back_recv,
):
    lev, lat, lon = lax.axis_index("lev"), lax.axis_index("lat"), lax.axis_index("lon")
    n_lev, n_lat, n_lon = lax.axis_size("lev"), lax.axis_size("lat"), lax.axis_size("lon")
    slots = pick.shape[1]
    cells = pick.shape[2]
    chans = slab.shape[0]
    rows = cells // 128
    groups, hidden = mid_ref.shape[:2]
    levels = out_ref.shape[1]
    own = groups * levels
    portion = chans // n_lev

    loads = [
        pltpu.make_async_copy(src, dst, load_sem.at[n])
        for n, (src, dst) in enumerate(
            ((latent_hbm, raw), (conv_hbm, conv), (inner_hbm, inner), (outer_hbm, outer), (obs_hbm, obs))
        )
    ]
    for load in loads:
        load.start()

    def tile(dlat, dlon):
        return (lev, lax.rem(lat + dlat + n_lat, n_lat), lax.rem(lon + dlon + n_lon, n_lon))

    def peer(d):
        return (lax.rem(lev + d, n_lev), lat, lon)

    around = [(x, y) for x in (-1, 0, 1) for y in (-1, 0, 1) if (x, y) != (0, 0)]
    barrier = pltpu.get_barrier_semaphore()
    for x, y in around:
        pl.semaphore_signal(barrier, inc=1, device_id=tile(x, y), device_id_type=MESH)
    for d in range(1, n_lev):
        pl.semaphore_signal(barrier, inc=1, device_id=peer(d), device_id_type=MESH)

    square = iota((slots, slots), 0) == iota((slots, slots), 1)
    eye[...] = jnp.where(square, 1.0, 0.0).astype(BF16)
    spread = jnp.broadcast_to(index_ref[...].astype(F32), (slots, slots))
    index = jnp.sum(jnp.where(square, spread, 0.0), axis=1, keepdims=True).astype(jnp.int32)
    row = lax.shift_right_logical(index, 7)
    col = lax.bitwise_and(index, 127)
    live = jnp.where(iota((slots, 1), 0) < count_ref[...], 1.0, 0.0)

    j = iota((128, 1), 0)
    last = (rows - 1) * 128
    spot = jnp.where(j < 32, j * 128 + 127, (j - 32) * 128)
    for at, cell in ((64, last + 127), (80, last), (96, 127), (112, 0)):
        spot = jnp.where(j == at, cell, jnp.where(j > at, -1, spot))

    def cast_rows(i):
        part = pl.ds(pl.multiple_of(i * 256, 256), 256)
        wide[part, :] = raw[part, :].astype(F32)

    def slab_row(r):
        slab[:, pl.ds(pl.multiple_of((r + 1) * 128, 128), 128)] = wide[
            pl.ds(r, chans, stride=rows), :
        ].astype(BF16)

    def edge_block(i):
        start = pl.multiple_of(i * 512, 512)
        edge[:, pl.ds(start, 512)] = jnp.where(iota((128, 512), 1) + start == spot, 1.0, 0.0).astype(BF16)

    loop(cells // 512, edge_block)
    loads[0].wait()
    loop(raw.shape[0] // 256, cast_rows)
    loop(rows, slab_row, 2)
    side_send[...] = dot_nt(edge[...], slab[:, 128 : 128 + cells]).astype(BF16)

    pl.semaphore_wait(barrier, len(around) + n_lev - 1)
    halo = [
        (slab.at[:, 128:256], south, (-1, 0)),
        (slab.at[:, cells : cells + 128], north, (1, 0)),
    ]
    sides = [(0, 32, (0, 1)), (32, 32, (0, -1)), (64, 16, (1, 1)), (80, 16, (1, -1)), (96, 16, (-1, 1)), (112, 16, (-1, -1))]
    for first, length, where in sides:
        halo.append((side_send.at[pl.ds(first, length)], side.at[pl.ds(first, length)], where))
    halo = [
        pltpu.make_async_remote_copy(
            src_ref=src,
            dst_ref=dst,
            send_sem=halo_send.at[n],
            recv_sem=halo_recv.at[n],
            device_id=tile(*where),
            device_id_type=MESH,
        )
        for n, (src, dst, where) in enumerate(halo)
    ]
    for copy in halo:
        copy.start()

    for b in range(3):
        there = col + (b - 1)
        target = jnp.where((there >= 0) & (there < 128), index + (b - 1), -1)

        def pick_block(i, b=b, target=target):
            start = pl.multiple_of(i * 256, 256)
            hit = iota((slots, 256), 1) + start == target
            pick[b, :, pl.ds(start, 256)] = jnp.where(hit, 1.0, 0.0).astype(BF16)

        loop(cells // 256, pick_block)

    for a in range(3):
        line = row + (a - 1)
        above = (line < 0) & (lat > 0)
        below = (line >= rows) & (lat < n_lat - 1)
        inside = (line >= 0) & (line < rows)
        for b in (0, 2):
            first, upper, lower = (0, 64, 96) if b == 0 else (32, 80, 112)
            out = (col == 0) if b == 0 else (col == 127)
            target = jnp.where(inside, first + line, jnp.where(above, upper, jnp.where(below, lower, -1)))
            target = jnp.where(out, target, -1)
            side_pick[a * 3 + b] = jnp.where(iota((slots, 128), 1) == target, 1.0, 0.0).astype(BF16)
        side_pick[a * 3 + 1] = jnp.zeros((slots, 128), BF16)

    out_pad[...] = jnp.zeros(out_pad.shape, BF16)
    for g in range(groups):
        part = pl.ds(pl.multiple_of(lev * own + g * levels, 16), levels)
        out_pad[part, g * hidden : (g + 1) * hidden] = out_ref[g]

    for copy in halo:
        copy.wait_recv()
    has_north = jnp.where(lat > 0, 1.0, 0.0)
    has_south = jnp.where(lat < n_lat - 1, 1.0, 0.0)
    slab[:, 0:128] = (north[...].astype(F32) * has_north).astype(BF16)
    slab[:, 128 + cells : 256 + cells] = (south[...].astype(F32) * has_south).astype(BF16)
    loads[1].wait()
    pre[...] = jnp.zeros(pre.shape, F32)

    def tap(t):
        a, b = t // 3, t % 3
        patch = dot_nt(pick[b], slab[:, pl.ds(pl.multiple_of(a * 128, 128), cells)])
        patch = patch + dot_nn(side_pick[t], side[...])
        kernel_t = conv[:, t].reshape(groups * hidden, chans)
        pre[...] += dot_nt(patch.astype(BF16), kernel_t)

    loop(9, tap)

    step = 32

    def gelu_one(i):
        part = pl.ds(pl.multiple_of(i * step, step), step)
        value, slope = gelu_slope(pre[part, :])
        act[part, :] = value.astype(BF16)
        slope_one[part, :] = slope

    def gelu_two(i):
        part = pl.ds(pl.multiple_of(i * step, step), step)
        value, slope = gelu_slope(pre[part, :])
        act[part, :] = value.astype(BF16)
        slope_two[part, :] = slope

    loop(slots // step, gelu_one)
    for g in range(groups):
        part = slice(g * hidden, (g + 1) * hidden)
        pre[:, part] = dot_nt(act[:, part], mid_ref[g])
    loop(slots // step, gelu_two)
    for g in range(groups):
        part = slice(g * hidden, (g + 1) * hidden)
        fields[pl.ds(pl.multiple_of(lev * own + g * levels, 16), levels), :] = dot_nt(
            out_ref[g], act[:, part]
        ).astype(BF16)

    def field_copy(d, source):
        part = pl.ds(pl.multiple_of(source * own, 16), own)
        return pltpu.make_async_remote_copy(
            src_ref=fields.at[part],
            dst_ref=fields.at[part],
            send_sem=field_send.at[d - 1],
            recv_sem=field_recv.at[d - 1],
            device_id=peer(d),
            device_id_type=MESH,
        )

    field_out = [field_copy(d, lev) for d in range(1, n_lev)]
    for copy in field_out:
        copy.start()
    for load in loads[2:]:
        load.wait()
    for d in range(1, n_lev):
        field_copy(d, lax.rem(lev + n_lev - d, n_lev)).wait_recv()

    for i in range(fields.shape[0] // 256):
        part = slice(i * 256, (i + 1) * 256)
        fields_t[:, part] = dot_nt(eye[...], fields[part, :]).astype(BF16)
    misfit[...] = fields_t[...].astype(F32)

    def column(i):
        part = pl.ds(pl.multiple_of(i * 256, 256), 256)
        value, slope = gelu_slope(dot_nt(fields_t[...], inner[part, :]))
        slope_col[:, part] = slope
        misfit[...] += dot_nt(value.astype(BF16), outer[:, part])

    loop(inner.shape[0] // 256, column)
    misfit[...] = (misfit[...] - obs[...]) * live * weight_ref[...]
    cast[...] = misfit[...].astype(BF16)

    def column_back(i):
        part = pl.ds(pl.multiple_of(i * 256, 256), 256)
        grad_act = (dot_nn(cast[...], outer[:, part]) * slope_col[:, part]).astype(BF16)
        misfit[...] += dot_nn(grad_act, inner[part, :])

    loop(inner.shape[0] // 256, column_back)
    grad_fields = misfit[...].astype(BF16)
    act[...] = (dot_nn(grad_fields, out_pad[...]) * slope_two[...]).astype(BF16)
    for g in range(groups):
        part = slice(g * hidden, (g + 1) * hidden)
        slope_one[:, part] = slope_one[:, part] * dot_nn(act[:, part], mid_ref[g])
    act[...] = slope_one[...].astype(BF16)

    def taps_copy(b, d, target):
        return pltpu.make_async_remote_copy(
            src_ref=taps.at[b, target],
            dst_ref=taps_in.at[b, d - 1],
            send_sem=taps_send.at[b, d - 1],
            recv_sem=taps_recv.at[b, d - 1],
            device_id=peer(d),
            device_id_type=MESH,
        )

    taps_out = []
    for b in range(3):

        def back(a, b=b):
            kernel_t = conv[:, a * 3 + b].reshape(groups * hidden, chans)
            part = dot_nn(act[...], kernel_t).astype(BF16)
            part = dot_nt(eye[...], part).astype(BF16)
            for d in range(n_lev):
                taps[b, d, pl.ds(pl.multiple_of(a * portion, 16), portion), :] = part[
                    d * portion : (d + 1) * portion
                ]

        loop(3, back)
        for d in range(1, n_lev):
            copy = taps_copy(b, d, lax.rem(lev + d, n_lev))
            copy.start()
            taps_out.append(copy)

    for b in range(3):
        for d in range(1, n_lev):
            taps_copy(b, d, lax.rem(lev + d, n_lev)).wait_recv()
        total = taps[b, lev].astype(F32)
        for d in range(1, n_lev):
            total = total + taps_in[b, d - 1].astype(F32)
        summed[b] = total.astype(BF16)

    upper = jnp.zeros((portion, 128), F32)
    lower = jnp.zeros((portion, 128), F32)
    beside = jnp.zeros((portion, 128), F32)
    for b in range(3):
        upper = upper + dot_nn(summed[b, 0:portion], pick[b, :, 0:128])
        lower = lower + dot_nn(summed[b, 2 * portion : 3 * portion], pick[b, :, last : last + 128])
        if b != 1:
            for a in range(3):
                beside = beside + dot_nn(summed[b, a * portion : (a + 1) * portion], side_pick[a * 3 + b])
    row_send[0] = (upper * has_north).astype(BF16)
    row_send[1] = (lower * has_south).astype(BF16)
    side_out[...] = beside.astype(BF16)
    back_copies = [(row_send.at[0], row_in.at[0], (-1, 0)), (row_send.at[1], row_in.at[1], (1, 0))]
    back_sides = [(0, -1), (0, 1), (-1, -1), (-1, 1), (1, -1), (1, 1)]
    for n, where in enumerate(back_sides):
        back_copies.append((side_out, side_in.at[n], where))
    back_copies = [
        pltpu.make_async_remote_copy(
            src_ref=src,
            dst_ref=dst,
            send_sem=back_send.at[n],
            recv_sem=back_recv.at[n],
            device_id=tile(*where),
            device_id_type=MESH,
        )
        for n, (src, dst, where) in enumerate(back_copies)
    ]
    for copy in back_copies:
        copy.start()

    def scatter(i):
        start = pl.multiple_of(i * 512, 512)
        part = dot_nn(summed[0], pick[0, :, pl.ds(start, 512)])
        part = part + dot_nn(summed[1], pick[1, :, pl.ds(start, 512)])
        part = part + dot_nn(summed[2], pick[2, :, pl.ds(start, 512)])
        up_part[:, pl.ds(start, 512)] = part[0:portion]
        mid_part[:, pl.ds(start, 512)] = part[portion : 2 * portion]
        down_part[:, pl.ds(pl.multiple_of(start + 128, 128), 512)] = part[2 * portion :]

    loop(cells // 512, scatter)
    for copy in back_copies:
        copy.wait_recv()
    up_part[:, cells : cells + 128] = row_in[0].astype(F32)
    down_part[:, 0:128] = row_in[1].astype(F32)
    lane = iota((portion, 128), 1)
    block = side_in[0].astype(F32)
    for n, start in ((1, 32), (2, 64), (3, 80), (4, 96), (5, 112)):
        block = jnp.where(lane >= start, side_in[n].astype(F32), block)
    block = block.astype(BF16)

    def finish(r):
        here = pl.ds(pl.multiple_of(r * 128, 128), 128)
        below = pl.ds(pl.multiple_of((r + 1) * 128, 128), 128)
        total = up_part[:, below] + mid_part[:, here] + down_part[:, here] + dot_nn(block, edge[:, here])
        grad_ref[pl.ds(r, portion, stride=rows), :] = total

    loop(rows, finish, 2)
    for copy in halo + field_out + taps_out + back_copies:
        copy.wait_send()


def per_device(
    latent,
    conv_weight,
    mid_weight,
    out_weight,
    vertical_inner_matrix,
    vertical_outer_matrix,
    obs_values,
    obs_weight,
    obs_index,
    obs_count,
):
    chans, rows, cols = latent.shape
    groups, hidden = conv_weight.shape[:2]
    slots, channels = obs_values.shape[2:]
    n_lev = lax.axis_size("lev")
    cells = rows * cols
    portion = chans // n_lev
    width = groups * hidden
    column = vertical_inner_matrix.shape[0]
    conv = conv_weight.transpose(0, 2, 1, 3)
    vmem = pltpu.VMEM
    dma = pltpu.SemaphoreType.DMA
    anywhere = pl.BlockSpec(memory_space=pl.ANY)
    near = pl.BlockSpec(memory_space=pltpu.VMEM)
    grad = pl.pallas_call(
        kernel,
        out_shape=jax.ShapeDtypeStruct((portion * rows, cols), F32),
        in_specs=[anywhere, anywhere, near, near, anywhere, anywhere, anywhere, near, near, near],
        out_specs=near,
        scratch_shapes=[
            vmem((chans * rows, cols), BF16),
            vmem((chans * rows, cols), F32),
            vmem((chans, cells + 2 * cols), BF16),
            vmem(conv.shape, BF16),
            vmem(vertical_inner_matrix.shape, BF16),
            vmem(vertical_outer_matrix.shape, BF16),
            vmem((slots, channels), F32),
            vmem((3, slots, cells), BF16),
            vmem((128, cells), BF16),
            vmem((9, slots, 128), BF16),
            vmem((128, chans), BF16),
            vmem((128, chans), BF16),
            vmem((chans, 128), BF16),
            vmem((chans, 128), BF16),
            vmem((slots, width), F32),
            vmem((slots, width), BF16),
            vmem((slots, width), F32),
            vmem((slots, width), F32),
            vmem((slots, column), F32),
            vmem((channels, slots), BF16),
            vmem((slots, channels), BF16),
            vmem((slots, channels), BF16),
            vmem((slots, channels), F32),
            vmem((channels, width), BF16),
            vmem((slots, slots), BF16),
            vmem((3, n_lev, 3 * portion, slots), BF16),
            vmem((3, n_lev - 1, 3 * portion, slots), BF16),
            vmem((3, 3 * portion, slots), BF16),
            vmem((portion, cells + cols), F32),
            vmem((portion, cells), F32),
            vmem((portion, cells + cols), F32),
            vmem((2, portion, cols), BF16),
            vmem((2, portion, cols), BF16),
            vmem((portion, 128), BF16),
            vmem((6, portion, 128), BF16),
            dma((5,)),
            dma((8,)),
            dma((8,)),
            dma((n_lev - 1,)),
            dma((n_lev - 1,)),
            dma((3, n_lev - 1)),
            dma((3, n_lev - 1)),
            dma((8,)),
            dma((8,)),
        ],
        compiler_params=pltpu.CompilerParams(
            collective_id=0, has_side_effects=True, vmem_limit_bytes=50 * 1024 * 1024
        ),
        name="slots_step",
    )(
        latent.reshape(chans * rows, cols),
        conv,
        mid_weight,
        out_weight,
        vertical_inner_matrix,
        vertical_outer_matrix,
        obs_values.reshape(slots, channels),
        obs_weight.reshape(1, channels),
        obs_index.reshape(1, slots),
        obs_count,
    )
    mine = lax.dynamic_slice_in_dim(latent, lax.axis_index("lev") * portion, portion, 0)
    return mine.astype(F32) + grad.reshape(portion, rows, cols)


def solution(mesh):
    return jax.shard_map(
        per_device,
        mesh=mesh,
        in_specs=(
            P(None, "lat", "lon"),
            P("lev", None, None, None),
            P("lev", None, None),
            P("lev", None, None),
            P(),
            P(),
            P("lat", "lon", None, None),
            P(),
            P("lat", "lon", None),
            P("lat", "lon"),
        ),
        out_specs=P("lev", "lat", "lon"),
        check_vma=False,
    )
```

```python
import functools

import jax
import jax.numpy as jnp
from jax import lax
from jax.experimental import pallas as pl
from jax.experimental.pallas import tpu as pltpu
from jax.sharding import PartitionSpec as P

KAPPA = 0.7978845608028654
CUBIC = 0.044715
F32 = jnp.float32
BF16 = jnp.bfloat16
MESH = pl.DeviceIdType.MESH


def gelu_slope(pre):
    tanh_v = jnp.tanh(KAPPA * (pre + CUBIC * pre * pre * pre))
    half = 0.5 * (1.0 + tanh_v)
    value = pre * half
    slope = half + 0.5 * pre * (1.0 - tanh_v * tanh_v) * (KAPPA + 3.0 * KAPPA * CUBIC * pre * pre)
    return (value, slope)


def dot_nn(x, y):
    return lax.dot_general(x, y, (((1,), (0,)), ((), ())), preferred_element_type=F32)


def dot_nt(x, y):
    return lax.dot_general(x, y, (((1,), (1,)), ((), ())), preferred_element_type=F32)


def iota(shape, dim):
    return lax.broadcasted_iota(jnp.int32, shape, dim)


def loop(count, body, unroll=1):
    def step(i, carry):
        body(i)
        return carry

    lax.fori_loop(0, count, step, 0, unroll=unroll)


def kernel(
    latent_hbm,
    conv_hbm,
    mid_hbm,
    out_hbm,
    inner_hbm,
    outer_hbm,
    obs_hbm,
    weight_hbm,
    index_hbm,
    count_hbm,
    grad_ref,
    raw,
    conv,
    mid_ref,
    out_ref,
    inner,
    outer,
    obs,
    weight_ref,
    index_ref,
    count_ref,
    index_smem,
    slab,
    table,
    patch,
    pick,
    edge,
    side_pick,
    side_send,
    side,
    row_out,
    north,
    south,
    pre,
    act,
    slope_one,
    slope_two,
    act_col,
    slope_col,
    fields,
    fields_t,
    cast,
    misfit,
    out_pad,
    eye,
    taps,
    relay_in,
    relay_out,
    taps_in,
    up_part,
    mid_part,
    down_part,
    row_send,
    row_in,
    side_out,
    side_in,
    load_sem,
    halo_send,
    halo_recv,
    field_send,
    field_recv,
    relay_send,
    relay_recv,
    taps_send,
    taps_recv,
    back_send,
    back_recv,
):
    lev, lat, lon = lax.axis_index("lev"), lax.axis_index("lat"), lax.axis_index("lon")
    n_lev, n_lat, n_lon = lax.axis_size("lev"), lax.axis_size("lat"), lax.axis_size("lon")
    slots = pick.shape[1]
    cells = pick.shape[2]
    chans = slab.shape[1]
    rows = cells // 128
    groups, hidden = mid_ref.shape[:2]
    levels = out_ref.shape[1]
    own = groups * levels
    portion = chans // n_lev
    pitch = table.shape[0] // (rows + 2)

    pairs = (
        (latent_hbm, raw),
        (index_hbm, index_smem),
        (index_hbm, index_ref),
        (count_hbm, count_ref),
        (conv_hbm, conv),
        (mid_hbm, mid_ref),
        (out_hbm, out_ref),
        (inner_hbm, inner),
        (outer_hbm, outer),
        (obs_hbm, obs),
        (weight_hbm, weight_ref.at[0]),
    )
    loads = [pltpu.make_async_copy(src, dst, load_sem.at[n]) for n, (src, dst) in enumerate(pairs)]
    for load in loads:
        load.start()

    def tile(dlat, dlon):
        return (lev, lax.rem(lat + dlat + n_lat, n_lat), lax.rem(lon + dlon + n_lon, n_lon))

    def peer(d):
        return (lax.rem(lev + d, n_lev), lat, lon)

    around = [(x, y) for x in (-1, 0, 1) for y in (-1, 0, 1) if (x, y) != (0, 0)]
    barrier = pltpu.get_barrier_semaphore()
    for x, y in around:
        pl.semaphore_signal(barrier, inc=1, device_id=tile(x, y), device_id_type=MESH)
    for d in range(1, n_lev):
        pl.semaphore_signal(barrier, inc=1, device_id=peer(d), device_id_type=MESH)

    square = iota((slots, slots), 0) == iota((slots, slots), 1)
    eye[...] = jnp.where(square, 1.0, 0.0).astype(BF16)
    order = iota((slots, 1), 0)
    order = lax.bitwise_and(order, 7) * rows + lax.shift_right_logical(order, 3)
    order = jnp.where(iota((slots, slots), 1) == order, 1.0, 0.0).astype(BF16)
    loads[0].wait()

    def relayout(i):
        start = pl.multiple_of(i * 16 * rows, 16 * rows)
        parts = [
            dot_nn(order, raw[pl.ds(start + h * 8 * rows, 8 * rows), :]).reshape(rows, 8, 128) for h in range(2)
        ]
        slab[:, pl.ds(pl.multiple_of(i * 16, 16), 16), :] = jnp.concatenate(parts, axis=1).astype(BF16)

    loop(chans // 16, relayout, 2)

    def put_row(line, value):
        start = line * pitch + 2
        table[pl.ds(start, 128, stride=2), :] = value[:, 0:128]
        table[pl.ds(start + 1, 128, stride=2), :] = value[:, 128:256]

    def table_row(r):
        put_row(r + 1, dot_nt(eye[0:128, 0:128], slab[r]))

    loop(rows, table_row, 2)

    for n, line in ((0, 0), (1, rows - 1)):
        row_out[n] = dot_nt(eye[0:128, 0:128], slab[line]).astype(BF16)
    for h in range(2):
        part = slice(h * 128, (h + 1) * 128)
        side_send[0:rows, part] = table[pl.ds(pitch + 256 + h, rows, stride=pitch), :]
        side_send[rows : 2 * rows, part] = table[pl.ds(pitch + 2 + h, rows, stride=pitch), :]
        for n, at in enumerate(
            (rows * pitch + 256, rows * pitch + 2, pitch + 256, pitch + 2)
        ):
            first = 2 * rows + 8 * n
            side_send[first : first + 8, part] = jnp.broadcast_to(table[at + h : at + h + 1, :], (8, 128))

    pl.semaphore_wait(barrier, len(around) + n_lev - 1)
    halo = [(row_out.at[0], south, (-1, 0)), (row_out.at[1], north, (1, 0))]
    sides = [(0, 32, (0, 1)), (32, 32, (0, -1)), (64, 8, (1, 1)), (72, 8, (1, -1)), (80, 8, (-1, 1)), (88, 8, (-1, -1))]
    for first, length, where in sides:
        halo.append((side_send.at[pl.ds(first, length)], side.at[pl.ds(first, length)], where))
    halo = [
        pltpu.make_async_remote_copy(
            src_ref=src,
            dst_ref=dst,
            send_sem=halo_send.at[n],
            recv_sem=halo_recv.at[n],
            device_id=tile(*where),
            device_id_type=MESH,
        )
        for n, (src, dst, where) in enumerate(halo)
    ]
    for copy in halo:
        copy.start()

    out_pad[...] = jnp.zeros(out_pad.shape, BF16)
    pre[...] = jnp.zeros(pre.shape, F32)
    for load in loads[1:7]:
        load.wait()
    for g in range(groups):
        part = pl.ds(pl.multiple_of(lev * own + g * levels, 16), levels)
        out_pad[part, g * hidden : (g + 1) * hidden] = out_ref[g]

    for copy in halo:
        copy.wait_recv()
    has_north = jnp.where(lat > 0, 1.0, 0.0)
    has_south = jnp.where(lat < n_lat - 1, 1.0, 0.0)
    put_row(0, north[...].astype(F32) * has_north)
    put_row(rows + 1, south[...].astype(F32) * has_south)
    for h in range(2):
        part = slice(h * 128, (h + 1) * 128)
        table[pl.ds(pitch + h, rows, stride=pitch), :] = side[0:rows, part]
        table[pl.ds(pitch + 258 + h, rows, stride=pitch), :] = side[rows : 2 * rows, part]
        low = (rows + 1) * pitch
        for n, (at, scale) in enumerate(((0, has_north), (258, has_north), (low, has_south), (low + 258, has_south))):
            first = 2 * rows + 8 * n
            table[at + h : at + h + 1, :] = side[first : first + 1, part] * scale

    def slot_patch(k):
        where = index_smem[0, k]
        start = lax.shift_right_logical(where, 7) * pitch + lax.bitwise_and(where, 127) * 2
        for a in range(3):
            patch[pl.ds(pl.multiple_of(k * 24 + a * 8, 8), 8), :] = table[pl.ds(start + a * pitch, 8), :]

    loop(slots, slot_patch, 8)

    def tap(a):
        for b in range(3):
            parts = [patch[pl.ds(a * 8 + b * 2 + h, slots, stride=24), :] for h in range(2)]
            cells_t = jnp.concatenate(parts, axis=1).astype(BF16)
            pre[...] += dot_nt(cells_t, conv[:, a * 3 + b].reshape(groups * hidden, chans))

    loop(3, tap)

    step = 32

    def gelu_one(i):
        part = pl.ds(pl.multiple_of(i * step, step), step)
        value, slope = gelu_slope(pre[part, :])
        act[part, :] = value.astype(BF16)
        slope_one[part, :] = slope

    def gelu_two(i):
        part = pl.ds(pl.multiple_of(i * step, step), step)
        value, slope = gelu_slope(pre[part, :])
        act[part, :] = value.astype(BF16)
        slope_two[part, :] = slope

    loop(slots // step, gelu_one)
    for g in range(groups):
        part = slice(g * hidden, (g + 1) * hidden)
        pre[:, part] = dot_nt(act[:, part], mid_ref[g])
    loop(slots // step, gelu_two)
    for g in range(groups):
        part = slice(g * hidden, (g + 1) * hidden)
        fields[pl.ds(pl.multiple_of(lev * own + g * levels, 16), levels), :] = dot_nt(
            out_ref[g], act[:, part]
        ).astype(BF16)

    def field_copy(d, source):
        part = pl.ds(pl.multiple_of(source * own, 16), own)
        return pltpu.make_async_remote_copy(
            src_ref=fields.at[part],
            dst_ref=fields.at[part],
            send_sem=field_send.at[d - 1],
            recv_sem=field_recv.at[d - 1],
            device_id=peer(d),
            device_id_type=MESH,
        )

    field_out = [field_copy(d, lev) for d in range(1, n_lev)]
    for copy in field_out:
        copy.start()

    spread = jnp.broadcast_to(index_ref[...].astype(F32), (slots, slots))
    index = jnp.sum(jnp.where(square, spread, 0.0), axis=1, keepdims=True).astype(jnp.int32)
    row = lax.shift_right_logical(index, 7)
    col = lax.bitwise_and(index, 127)
    live = jnp.where(iota((slots, 1), 0) < count_ref[...], 1.0, 0.0)
    row_wide = jnp.broadcast_to(row, (slots, 128))
    lane_wide = iota((slots, 128), 1)
    last = (rows - 1) * 128
    for b in range(3):
        cast[:, b * 128 : (b + 1) * 128] = jnp.where(lane_wide == col + (b - 1), 1.0, 0.0).astype(BF16)

    def pick_row(r):
        hit = row_wide == r
        for b in range(3):
            column_b = cast[:, b * 128 : (b + 1) * 128].astype(F32)
            pick[b, :, pl.ds(pl.multiple_of(r * 128, 128), 128)] = jnp.where(hit, column_b, 0.0).astype(BF16)

    loop(rows, pick_row)

    for a in range(3):
        line = row + (a - 1)
        above = (line < 0) & (lat > 0)
        below = (line >= rows) & (lat < n_lat - 1)
        inside = (line >= 0) & (line < rows)
        for n, b in enumerate((0, 2)):
            first, upper, lower = (0, 64, 96) if b == 0 else (32, 80, 112)
            out = (col == 0) if b == 0 else (col == 127)
            target = jnp.where(inside, first + line, jnp.where(above, upper, jnp.where(below, lower, -1)))
            target = jnp.where(out, target, -1)
            side_pick[n * 3 + a] = jnp.where(lane_wide == target, 1.0, 0.0).astype(BF16)

    j = iota((128, 1), 0)
    spot = jnp.where(j < 32, j * 128 + 127, (j - 32) * 128)
    for at, cell in ((64, last + 127), (80, last), (96, 127), (112, 0)):
        spot = jnp.where(j == at, cell, jnp.where(j > at, -1, spot))

    def edge_block(i):
        start = pl.multiple_of(i * 512, 512)
        edge[:, pl.ds(start, 512)] = jnp.where(iota((128, 512), 1) + start == spot, 1.0, 0.0).astype(BF16)

    loop(cells // 512, edge_block)

    for load in loads[7:]:
        load.wait()
    for d in range(1, n_lev):
        field_copy(d, lax.rem(lev + n_lev - d, n_lev)).wait_recv()

    blocks = fields.shape[0] // 256
    for i in range(blocks):
        part = slice(i * 256, (i + 1) * 256)
        fields_t[:, part] = dot_nt(eye[...], fields[part, :]).astype(BF16)

    def column(i):
        part = pl.ds(pl.multiple_of(i * 256, 256), 256)
        value, slope = gelu_slope(dot_nt(fields_t[...], inner[part, :]))
        slope_col[:, part] = slope
        act_col[:, part] = value.astype(BF16)

    loop(inner.shape[0] // 256, column)

    def compare(i):
        part = pl.ds(pl.multiple_of(i * 256, 256), 256)
        forecast = fields_t[:, part].astype(F32) + dot_nt(act_col[...], outer[part, :])
        value = (forecast - obs[:, part]) * live * weight_ref[:, part]
        misfit[:, part] = value
        cast[:, part] = value.astype(BF16)

    loop(blocks, compare)

    def column_back(i):
        part = pl.ds(pl.multiple_of(i * 256, 256), 256)
        act_col[:, part] = (dot_nn(cast[...], outer[:, part]) * slope_col[:, part]).astype(BF16)

    loop(inner.shape[0] // 256, column_back)

    def fields_back(i):
        part = pl.ds(pl.multiple_of(i * 256, 256), 256)
        fields_t[:, part] = (misfit[:, part] + dot_nn(act_col[...], inner[:, part])).astype(BF16)

    loop(blocks, fields_back)
    act[...] = (dot_nn(fields_t[...], out_pad[...]) * slope_two[...]).astype(BF16)
    for g in range(groups):
        part = slice(g * hidden, (g + 1) * hidden)
        slope_one[:, part] = slope_one[:, part] * dot_nn(act[:, part], mid_ref[g])
    act[...] = slope_one[...].astype(BF16)

    above_lev, below_lev, across = lax.rem(lev + 1, n_lev), lax.rem(lev + 3, n_lev), lax.rem(lev + 2, n_lev)
    half = 3 * portion // 2
    low_half, high_half = pl.ds(0, half), pl.ds(half, half)

    def send(src, dst, sems, device):
        return pltpu.make_async_remote_copy(
            src_ref=src,
            dst_ref=dst,
            send_sem=sems[0],
            recv_sem=sems[1],
            device_id=(device, lat, lon),
            device_id_type=MESH,
        )

    def relay_copies(b):
        return [
            send(taps.at[b, across, low_half], relay_in.at[b, 0], (relay_send.at[b, 0], relay_recv.at[b, 0]), above_lev),
            send(taps.at[b, across, high_half], relay_in.at[b, 1], (relay_send.at[b, 1], relay_recv.at[b, 1]), below_lev),
        ]

    def taps_copies(b):
        sources = (
            (relay_out.at[b, 0], above_lev),
            (taps.at[b, above_lev, high_half], above_lev),
            (taps.at[b, below_lev, low_half], below_lev),
            (relay_out.at[b, 1], below_lev),
        )
        return [
            send(src, taps_in.at[b, n], (taps_send.at[b, n], taps_recv.at[b, n]), device)
            for n, (src, device) in enumerate(sources)
        ]

    relays = [relay_copies(b) for b in range(3)]
    shares = [taps_copies(b) for b in range(3)]
    for b in range(3):

        def back(a, b=b):
            kernel_t = conv[:, a * 3 + b].reshape(groups * hidden, chans)
            part = dot_nn(act[...], kernel_t).astype(BF16)
            part = dot_nt(eye[...], part).astype(BF16)
            for d in range(n_lev):
                taps[b, d, pl.ds(pl.multiple_of(a * portion, 16), portion), :] = part[
                    d * portion : (d + 1) * portion
                ]

        loop(3, back)
        for copy in relays[b] + shares[b][1:3]:
            copy.start()
    for b in range(3):
        for copy in relays[b]:
            copy.wait_recv()
        for n, (device, part) in enumerate(((above_lev, low_half), (below_lev, high_half))):
            mine = taps[b, device, part, :].astype(F32)
            relay_out[b, n] = (mine + relay_in[b, n].astype(F32)).astype(BF16)
        shares[b][0].start()
        shares[b][3].start()

    upper = jnp.zeros((portion, 128), F32)
    lower = jnp.zeros((portion, 128), F32)
    beside = jnp.zeros((portion, 128), F32)
    for b in range(3):
        for copy in shares[b]:
            copy.wait_recv()
        halves = []
        for part, first, second in ((low_half, 0, 2), (high_half, 1, 3)):
            total = taps[b, lev, part, :].astype(F32)
            halves.append(total + taps_in[b, first].astype(F32) + taps_in[b, second].astype(F32))
        summed = jnp.concatenate(halves, axis=0).astype(BF16)
        upper = upper + dot_nn(summed[0:portion], pick[b, :, 0:128])
        lower = lower + dot_nn(summed[2 * portion : 3 * portion], pick[b, :, last : last + 128])
        if b != 1:
            for a in range(3):
                beside = beside + dot_nn(summed[a * portion : (a + 1) * portion], side_pick[(b // 2) * 3 + a])
        if b == 2:
            row_send[0] = (upper * has_north).astype(BF16)
            row_send[1] = (lower * has_south).astype(BF16)
            side_out[...] = beside.astype(BF16)
            back_copies = [(row_send.at[0], row_in.at[0], (-1, 0)), (row_send.at[1], row_in.at[1], (1, 0))]
            back_sides = [(0, -1), (0, 1), (-1, -1), (-1, 1), (1, -1), (1, 1)]
            for n, where in enumerate(back_sides):
                back_copies.append((side_out, side_in.at[n], where))
            back_copies = [
                pltpu.make_async_remote_copy(
                    src_ref=src,
                    dst_ref=dst,
                    send_sem=back_send.at[n],
                    recv_sem=back_recv.at[n],
                    device_id=tile(*where),
                    device_id_type=MESH,
                )
                for n, (src, dst, where) in enumerate(back_copies)
            ]
            for copy in back_copies:
                copy.start()

        def scatter(i, b=b, summed=summed):
            here = pl.ds(pl.multiple_of(i * 512, 512), 512)
            after = pl.ds(pl.multiple_of(i * 512 + 128, 128), 512)
            part = dot_nn(summed, pick[b, :, here])
            if b == 0:
                up_part[:, here] = part[0:portion]
                mid_part[:, here] = part[portion : 2 * portion]
                down_part[:, after] = part[2 * portion :]
            else:
                up_part[:, here] += part[0:portion]
                mid_part[:, here] += part[portion : 2 * portion]
                down_part[:, after] += part[2 * portion :]

        loop(cells // 512, scatter)

    for copy in back_copies:
        copy.wait_recv()
    up_part[:, cells : cells + 128] = row_in[0].astype(F32)
    down_part[:, 0:128] = row_in[1].astype(F32)
    lane = iota((portion, 128), 1)
    block = side_in[0].astype(F32)
    for n, start in ((1, 32), (2, 64), (3, 80), (4, 96), (5, 112)):
        block = jnp.where(lane >= start, side_in[n].astype(F32), block)
    block = block.astype(BF16)

    def finish(r):
        here = pl.ds(pl.multiple_of(r * 128, 128), 128)
        below = pl.ds(pl.multiple_of((r + 1) * 128, 128), 128)
        total = up_part[:, below] + mid_part[:, here] + down_part[:, here] + dot_nn(block, edge[:, here])
        grad_ref[pl.ds(r, portion, stride=rows), :] = total

    loop(rows, finish, 2)
    for copy in halo + field_out + sum(relays, []) + sum(shares, []) + back_copies:
        copy.wait_send()


def per_device(
    latent,
    conv_weight,
    mid_weight,
    out_weight,
    vertical_inner_matrix,
    vertical_outer_matrix,
    obs_values,
    obs_weight,
    obs_index,
    obs_count,
):
    chans, rows, cols = latent.shape
    groups, hidden = conv_weight.shape[:2]
    slots, channels = obs_values.shape[2:]
    n_lev = lax.axis_size("lev")
    cells = rows * cols
    portion = chans // n_lev
    width = groups * hidden
    column = vertical_inner_matrix.shape[0]
    conv = conv_weight.transpose(0, 2, 1, 3)
    half = 3 * portion // 2
    vmem = pltpu.VMEM
    dma = pltpu.SemaphoreType.DMA
    grad = pl.pallas_call(
        kernel,
        out_shape=jax.ShapeDtypeStruct((portion * rows, cols), F32),
        in_specs=[pl.BlockSpec(memory_space=pl.ANY)] * 10,
        out_specs=pl.BlockSpec(memory_space=pltpu.VMEM),
        scratch_shapes=[
            vmem((chans * rows, cols), BF16),
            vmem(conv.shape, BF16),
            vmem(mid_weight.shape, BF16),
            vmem(out_weight.shape, BF16),
            vmem(vertical_inner_matrix.shape, BF16),
            vmem(vertical_outer_matrix.shape, BF16),
            vmem((slots, channels), F32),
            vmem((1, channels), F32),
            vmem((1, slots), jnp.int32),
            vmem((1, 1), jnp.int32),
            pltpu.SMEM((1, slots), jnp.int32),
            vmem((rows, chans, cols), BF16),
            vmem(((rows + 2) * 2 * (cols + 8), 128), F32),
            vmem((slots * 24, 128), F32),
            vmem((3, slots, cells), BF16),
            vmem((128, cells), BF16),
            vmem((6, slots, 128), BF16),
            vmem((2 * rows + 32, chans), F32),
            vmem((2 * rows + 32, chans), F32),
            vmem((2, cols, chans), BF16),
            vmem((cols, chans), BF16),
            vmem((cols, chans), BF16),
            vmem((slots, width), F32),
            vmem((slots, width), BF16),
            vmem((slots, width), F32),
            vmem((slots, width), F32),
            vmem((slots, column), BF16),
            vmem((slots, column), F32),
            vmem((channels, slots), BF16),
            vmem((slots, channels), BF16),
            vmem((slots, channels), BF16),
            vmem((slots, channels), F32),
            vmem((channels, width), BF16),
            vmem((slots, slots), BF16),
            vmem((3, n_lev, 3 * portion, slots), BF16),
            vmem((3, 2, half, slots), BF16),
            vmem((3, 2, half, slots), BF16),
            vmem((3, 4, half, slots), BF16),
            vmem((portion, cells + cols), F32),
            vmem((portion, cells), F32),
            vmem((portion, cells + cols), F32),
            vmem((2, portion, cols), BF16),
            vmem((2, portion, cols), BF16),
            vmem((portion, 128), BF16),
            vmem((6, portion, 128), BF16),
            dma((11,)),
            dma((8,)),
            dma((8,)),
            dma((n_lev - 1,)),
            dma((n_lev - 1,)),
            dma((3, 2)),
            dma((3, 2)),
            dma((3, 4)),
            dma((3, 4)),
            dma((8,)),
            dma((8,)),
        ],
        compiler_params=pltpu.CompilerParams(
            collective_id=0, has_side_effects=True, vmem_limit_bytes=60 * 1024 * 1024
        ),
        name="slots_step",
    )(
        latent.reshape(chans * rows, cols),
        conv,
        mid_weight,
        out_weight,
        vertical_inner_matrix,
        vertical_outer_matrix,
        obs_values.reshape(slots, channels),
        obs_weight,
        obs_index.reshape(1, slots),
        obs_count,
    )
    mine = lax.dynamic_slice_in_dim(latent, lax.axis_index("lev") * portion, portion, 0)
    return mine.astype(F32) + grad.reshape(portion, rows, cols)


def solution(mesh):
    return jax.shard_map(
        per_device,
        mesh=mesh,
        in_specs=(
            P(None, "lat", "lon"),
            P("lev", None, None, None),
            P("lev", None, None),
            P("lev", None, None),
            P(),
            P(),
            P("lat", "lon", None, None),
            P(),
            P("lat", "lon", None),
            P("lat", "lon"),
        ),
        out_specs=P("lev", "lat", "lon"),
        check_vma=False,
    )
```

```python
import functools

import jax
import jax.numpy as jnp
from jax import lax
from jax.experimental import pallas as pl
from jax.experimental.pallas import tpu as pltpu
from jax.sharding import PartitionSpec as P

KAPPA = 0.7978845608028654
CUBIC = 0.044715
F32 = jnp.float32
BF16 = jnp.bfloat16
MESH = pl.DeviceIdType.MESH


def gelu_slope(pre):
    tanh_v = jnp.tanh(KAPPA * (pre + CUBIC * pre * pre * pre))
    half = 0.5 * (1.0 + tanh_v)
    value = pre * half
    slope = half + 0.5 * pre * (1.0 - tanh_v * tanh_v) * (KAPPA + 3.0 * KAPPA * CUBIC * pre * pre)
    return (value, slope)


def dot_nn(x, y):
    return lax.dot_general(x, y, (((1,), (0,)), ((), ())), preferred_element_type=F32)


def dot_nt(x, y):
    return lax.dot_general(x, y, (((1,), (1,)), ((), ())), preferred_element_type=F32)


def iota(shape, dim):
    return lax.broadcasted_iota(jnp.int32, shape, dim)


def loop(count, body, unroll=1):
    def step(i, carry):
        body(i)
        return carry

    lax.fori_loop(0, count, step, 0, unroll=unroll)


def kernel(
    latent_hbm,
    conv_hbm,
    mid_hbm,
    out_hbm,
    inner_hbm,
    outer_hbm,
    obs_hbm,
    weight_hbm,
    index_hbm,
    count_hbm,
    grad_ref,
    raw,
    conv,
    mid_ref,
    out_ref,
    inner,
    outer,
    obs,
    weight_ref,
    index_ref,
    count_ref,
    index_smem,
    slab,
    table,
    patch,
    pick,
    edge,
    side_pick,
    side_send,
    side,
    row_out,
    north,
    south,
    pre,
    act,
    slope_one,
    slope_two,
    act_col,
    slope_col,
    fields,
    fields_t,
    cast,
    misfit,
    out_pad,
    eye,
    taps,
    relay_in,
    relay_out,
    taps_in,
    up_part,
    mid_part,
    down_part,
    row_send,
    row_in,
    side_out,
    side_in,
    load_sem,
    halo_send,
    halo_recv,
    field_send,
    field_recv,
    relay_send,
    relay_recv,
    taps_send,
    taps_recv,
    back_send,
    back_recv,
):
    lev, lat, lon = lax.axis_index("lev"), lax.axis_index("lat"), lax.axis_index("lon")
    n_lev, n_lat, n_lon = lax.axis_size("lev"), lax.axis_size("lat"), lax.axis_size("lon")
    slots = pick.shape[1]
    cells = pick.shape[2]
    chans = slab.shape[1]
    rows = cells // 128
    groups, hidden = mid_ref.shape[:2]
    levels = out_ref.shape[1]
    own = groups * levels
    portion = chans // n_lev
    pitch = table.shape[0] // (rows + 2)

    pairs = (
        (latent_hbm, raw),
        (index_hbm, index_smem),
        (index_hbm, index_ref),
        (count_hbm, count_ref),
        (conv_hbm, conv),
        (mid_hbm, mid_ref),
        (out_hbm, out_ref),
        (inner_hbm, inner),
        (outer_hbm, outer),
        (obs_hbm, obs),
        (weight_hbm, weight_ref.at[0]),
    )
    loads = [pltpu.make_async_copy(src, dst, load_sem.at[n]) for n, (src, dst) in enumerate(pairs)]
    for load in loads[:4]:
        load.start()

    def tile(dlat, dlon):
        return (lev, lax.rem(lat + dlat + n_lat, n_lat), lax.rem(lon + dlon + n_lon, n_lon))

    def peer(d):
        return (lax.rem(lev + d, n_lev), lat, lon)

    around = [(x, y) for x in (-1, 0, 1) for y in (-1, 0, 1) if (x, y) != (0, 0)]
    barrier = pltpu.get_barrier_semaphore()
    for x, y in around:
        pl.semaphore_signal(barrier, inc=1, device_id=tile(x, y), device_id_type=MESH)
    for d in range(1, n_lev):
        pl.semaphore_signal(barrier, inc=1, device_id=peer(d), device_id_type=MESH)

    square = iota((slots, slots), 0) == iota((slots, slots), 1)
    eye[...] = jnp.where(square, 1.0, 0.0).astype(BF16)
    order = iota((slots, 1), 0)
    order = lax.bitwise_and(order, 7) * rows + lax.shift_right_logical(order, 3)
    order = jnp.where(iota((slots, slots), 1) == order, 1.0, 0.0).astype(BF16)
    loads[0].wait()
    for load in loads[4:]:
        load.start()

    def relayout(i):
        start = pl.multiple_of(i * 16 * rows, 16 * rows)
        parts = [
            dot_nn(order, raw[pl.ds(start + h * 8 * rows, 8 * rows), :]).reshape(rows, 8, 128) for h in range(2)
        ]
        slab[:, pl.ds(pl.multiple_of(i * 16, 16), 16), :] = jnp.concatenate(parts, axis=1).astype(BF16)

    loop(chans // 16, relayout, 2)

    def put_row(line, value):
        start = line * pitch + 2
        table[pl.ds(start, 128, stride=2), :] = value[:, 0:128]
        table[pl.ds(start + 1, 128, stride=2), :] = value[:, 128:256]

    def table_row(r):
        put_row(r + 1, dot_nt(eye[0:128, 0:128], slab[r]))

    loop(rows, table_row, 2)

    for n, line in ((0, 0), (1, rows - 1)):
        row_out[n] = dot_nt(eye[0:128, 0:128], slab[line]).astype(BF16)
    for h in range(2):
        part = slice(h * 128, (h + 1) * 128)
        side_send[0:rows, part] = table[pl.ds(pitch + 256 + h, rows, stride=pitch), :]
        side_send[rows : 2 * rows, part] = table[pl.ds(pitch + 2 + h, rows, stride=pitch), :]
        for n, at in enumerate(
            (rows * pitch + 256, rows * pitch + 2, pitch + 256, pitch + 2)
        ):
            first = 2 * rows + 8 * n
            side_send[first : first + 8, part] = jnp.broadcast_to(table[at + h : at + h + 1, :], (8, 128))

    pl.semaphore_wait(barrier, len(around) + n_lev - 1)
    halo = [(row_out.at[0], south, (-1, 0)), (row_out.at[1], north, (1, 0))]
    sides = [(0, 32, (0, 1)), (32, 32, (0, -1)), (64, 8, (1, 1)), (72, 8, (1, -1)), (80, 8, (-1, 1)), (88, 8, (-1, -1))]
    for first, length, where in sides:
        halo.append((side_send.at[pl.ds(first, length)], side.at[pl.ds(first, length)], where))
    halo = [
        pltpu.make_async_remote_copy(
            src_ref=src,
            dst_ref=dst,
            send_sem=halo_send.at[n],
            recv_sem=halo_recv.at[n],
            device_id=tile(*where),
            device_id_type=MESH,
        )
        for n, (src, dst, where) in enumerate(halo)
    ]
    for copy in halo:
        copy.start()

    out_pad[...] = jnp.zeros(out_pad.shape, BF16)
    pre[...] = jnp.zeros(pre.shape, F32)
    for load in loads[1:7]:
        load.wait()
    for g in range(groups):
        part = pl.ds(pl.multiple_of(lev * own + g * levels, 16), levels)
        out_pad[part, g * hidden : (g + 1) * hidden] = out_ref[g]

    for copy in halo:
        copy.wait_recv()
    has_north = jnp.where(lat > 0, 1.0, 0.0)
    has_south = jnp.where(lat < n_lat - 1, 1.0, 0.0)
    put_row(0, north[...].astype(F32) * has_north)
    put_row(rows + 1, south[...].astype(F32) * has_south)
    for h in range(2):
        part = slice(h * 128, (h + 1) * 128)
        table[pl.ds(pitch + h, rows, stride=pitch), :] = side[0:rows, part]
        table[pl.ds(pitch + 258 + h, rows, stride=pitch), :] = side[rows : 2 * rows, part]
        low = (rows + 1) * pitch
        for n, (at, scale) in enumerate(((0, has_north), (258, has_north), (low, has_south), (low + 258, has_south))):
            first = 2 * rows + 8 * n
            table[at + h : at + h + 1, :] = side[first : first + 1, part] * scale

    def slot_patch(k):
        where = index_smem[0, k]
        start = lax.shift_right_logical(where, 7) * pitch + lax.bitwise_and(where, 127) * 2
        for a in range(3):
            patch[pl.ds(pl.multiple_of(k * 24 + a * 8, 8), 8), :] = table[pl.ds(start + a * pitch, 8), :]

    loop(slots, slot_patch, 8)

    def tap(a):
        for b in range(3):
            parts = [patch[pl.ds(a * 8 + b * 2 + h, slots, stride=24), :] for h in range(2)]
            cells_t = jnp.concatenate(parts, axis=1).astype(BF16)
            pre[...] += dot_nt(cells_t, conv[:, a * 3 + b].reshape(groups * hidden, chans))

    loop(3, tap, 3)

    step = 32

    def gelu_one(i):
        part = pl.ds(pl.multiple_of(i * step, step), step)
        value, slope = gelu_slope(pre[part, :])
        act[part, :] = value.astype(BF16)
        slope_one[part, :] = slope

    def gelu_two(i):
        part = pl.ds(pl.multiple_of(i * step, step), step)
        value, slope = gelu_slope(pre[part, :])
        act[part, :] = value.astype(BF16)
        slope_two[part, :] = slope

    loop(slots // step, gelu_one)
    for g in range(groups):
        part = slice(g * hidden, (g + 1) * hidden)
        pre[:, part] = dot_nt(act[:, part], mid_ref[g])
    loop(slots // step, gelu_two)
    for g in range(groups):
        part = slice(g * hidden, (g + 1) * hidden)
        fields[pl.ds(pl.multiple_of(lev * own + g * levels, 16), levels), :] = dot_nt(
            out_ref[g], act[:, part]
        ).astype(BF16)

    def field_copy(d, source):
        part = pl.ds(pl.multiple_of(source * own, 16), own)
        return pltpu.make_async_remote_copy(
            src_ref=fields.at[part],
            dst_ref=fields.at[part],
            send_sem=field_send.at[d - 1],
            recv_sem=field_recv.at[d - 1],
            device_id=peer(d),
            device_id_type=MESH,
        )

    field_out = [field_copy(d, lev) for d in range(1, n_lev)]
    for copy in field_out:
        copy.start()

    spread = jnp.broadcast_to(index_ref[...].astype(F32), (slots, slots))
    index = jnp.sum(jnp.where(square, spread, 0.0), axis=1, keepdims=True).astype(jnp.int32)
    row = lax.shift_right_logical(index, 7)
    col = lax.bitwise_and(index, 127)
    live = jnp.where(iota((slots, 1), 0) < count_ref[...], 1.0, 0.0)
    row_wide = jnp.broadcast_to(row, (slots, 128))
    lane_wide = iota((slots, 128), 1)
    last = (rows - 1) * 128
    for b in range(3):
        cast[:, b * 128 : (b + 1) * 128] = jnp.where(lane_wide == col + (b - 1), 1.0, 0.0).astype(BF16)

    def pick_row(r):
        hit = row_wide == r
        for b in range(3):
            column_b = cast[:, b * 128 : (b + 1) * 128].astype(F32)
            pick[b, :, pl.ds(pl.multiple_of(r * 128, 128), 128)] = jnp.where(hit, column_b, 0.0).astype(BF16)

    loop(rows, pick_row)

    for a in range(3):
        line = row + (a - 1)
        above = (line < 0) & (lat > 0)
        below = (line >= rows) & (lat < n_lat - 1)
        inside = (line >= 0) & (line < rows)
        for n, b in enumerate((0, 2)):
            first, upper, lower = (0, 64, 96) if b == 0 else (32, 80, 112)
            out = (col == 0) if b == 0 else (col == 127)
            target = jnp.where(inside, first + line, jnp.where(above, upper, jnp.where(below, lower, -1)))
            target = jnp.where(out, target, -1)
            side_pick[n * 3 + a] = jnp.where(lane_wide == target, 1.0, 0.0).astype(BF16)

    j = iota((128, 1), 0)
    spot = jnp.where(j < 32, j * 128 + 127, (j - 32) * 128)
    for at, cell in ((64, last + 127), (80, last), (96, 127), (112, 0)):
        spot = jnp.where(j == at, cell, jnp.where(j > at, -1, spot))

    def edge_block(i):
        start = pl.multiple_of(i * 512, 512)
        edge[:, pl.ds(start, 512)] = jnp.where(iota((128, 512), 1) + start == spot, 1.0, 0.0).astype(BF16)

    loop(cells // 512, edge_block)
    up_part[:, cells : cells + 128] = jnp.zeros((portion, 128), F32)
    down_part[:, 0:128] = jnp.zeros((portion, 128), F32)

    for load in loads[7:]:
        load.wait()
    for d in range(1, n_lev):
        field_copy(d, lax.rem(lev + n_lev - d, n_lev)).wait_recv()

    blocks = fields.shape[0] // 256
    for i in range(blocks):
        part = slice(i * 256, (i + 1) * 256)
        fields_t[:, part] = dot_nt(eye[...], fields[part, :]).astype(BF16)

    def column(i):
        part = pl.ds(pl.multiple_of(i * 256, 256), 256)
        value, slope = gelu_slope(dot_nt(fields_t[...], inner[part, :]))
        slope_col[:, part] = slope
        act_col[:, part] = value.astype(BF16)

    loop(inner.shape[0] // 256, column, 4)

    def compare(i):
        part = pl.ds(pl.multiple_of(i * 256, 256), 256)
        forecast = fields_t[:, part].astype(F32) + dot_nt(act_col[...], outer[part, :])
        value = (forecast - obs[:, part]) * live * weight_ref[:, part]
        misfit[:, part] = value
        cast[:, part] = value.astype(BF16)

    loop(blocks, compare, 3)

    def column_back(i):
        part = pl.ds(pl.multiple_of(i * 256, 256), 256)
        act_col[:, part] = (dot_nn(cast[...], outer[:, part]) * slope_col[:, part]).astype(BF16)

    loop(inner.shape[0] // 256, column_back, 4)

    def fields_back(i):
        part = pl.ds(pl.multiple_of(i * 256, 256), 256)
        fields_t[:, part] = (misfit[:, part] + dot_nn(act_col[...], inner[:, part])).astype(BF16)

    loop(blocks, fields_back, 3)
    act[...] = (dot_nn(fields_t[...], out_pad[...]) * slope_two[...]).astype(BF16)
    for g in range(groups):
        part = slice(g * hidden, (g + 1) * hidden)
        slope_one[:, part] = slope_one[:, part] * dot_nn(act[:, part], mid_ref[g])
    act[...] = slope_one[...].astype(BF16)

    above_lev, below_lev, across = lax.rem(lev + 1, n_lev), lax.rem(lev + 3, n_lev), lax.rem(lev + 2, n_lev)
    half = 3 * portion // 2
    low_half, high_half = pl.ds(0, half), pl.ds(half, half)

    def send(src, dst, sems, device):
        return pltpu.make_async_remote_copy(
            src_ref=src,
            dst_ref=dst,
            send_sem=sems[0],
            recv_sem=sems[1],
            device_id=(device, lat, lon),
            device_id_type=MESH,
        )

    def relay_copies(b):
        return [
            send(taps.at[b, across, low_half], relay_in.at[b, 0], (relay_send.at[b, 0], relay_recv.at[b, 0]), above_lev),
            send(taps.at[b, across, high_half], relay_in.at[b, 1], (relay_send.at[b, 1], relay_recv.at[b, 1]), below_lev),
        ]

    def taps_copies(b):
        sources = (
            (relay_out.at[b, 0], above_lev),
            (taps.at[b, above_lev, high_half], above_lev),
            (taps.at[b, below_lev, low_half], below_lev),
            (relay_out.at[b, 1], below_lev),
        )
        return [
            send(src, taps_in.at[b, n], (taps_send.at[b, n], taps_recv.at[b, n]), device)
            for n, (src, device) in enumerate(sources)
        ]

    relays = [relay_copies(b) for b in range(3)]
    shares = [taps_copies(b) for b in range(3)]
    for b in range(3):

        def back(a, b=b):
            kernel_t = conv[:, a * 3 + b].reshape(groups * hidden, chans)
            part = dot_nn(act[...], kernel_t).astype(BF16)
            part = dot_nt(eye[...], part).astype(BF16)
            for d in range(n_lev):
                taps[b, d, pl.ds(pl.multiple_of(a * portion, 16), portion), :] = part[
                    d * portion : (d + 1) * portion
                ]

        loop(3, back, 3)
        for copy in relays[b]:
            copy.start()
    for b in range(3):
        shares[b][1].start()
        shares[b][2].start()
    for b in range(3):
        for copy in relays[b]:
            copy.wait_recv()
        for n, (device, part) in enumerate(((above_lev, low_half), (below_lev, high_half))):
            mine = taps[b, device, part, :].astype(F32)
            relay_out[b, n] = (mine + relay_in[b, n].astype(F32)).astype(BF16)
        shares[b][0].start()
        shares[b][3].start()

    upper = jnp.zeros((portion, 128), F32)
    lower = jnp.zeros((portion, 128), F32)
    beside = jnp.zeros((portion, 128), F32)
    for b in range(3):
        for copy in shares[b]:
            copy.wait_recv()
        halves = []
        for part, first, second in ((low_half, 0, 2), (high_half, 1, 3)):
            total = taps[b, lev, part, :].astype(F32)
            halves.append(total + taps_in[b, first].astype(F32) + taps_in[b, second].astype(F32))
        summed = jnp.concatenate(halves, axis=0).astype(BF16)
        upper = upper + dot_nn(summed[0:portion], pick[b, :, 0:128])
        lower = lower + dot_nn(summed[2 * portion : 3 * portion], pick[b, :, last : last + 128])
        if b != 1:
            for a in range(3):
                beside = beside + dot_nn(summed[a * portion : (a + 1) * portion], side_pick[(b // 2) * 3 + a])
        if b == 2:
            row_send[0] = (upper * has_north).astype(BF16)
            row_send[1] = (lower * has_south).astype(BF16)
            side_out[...] = beside.astype(BF16)
            back_copies = [(row_send.at[0], row_in.at[0], (-1, 0)), (row_send.at[1], row_in.at[1], (1, 0))]
            back_sides = [(0, -1), (0, 1), (-1, -1), (-1, 1), (1, -1), (1, 1)]
            for n, where in enumerate(back_sides):
                back_copies.append((side_out, side_in.at[n], where))
            back_copies = [
                pltpu.make_async_remote_copy(
                    src_ref=src,
                    dst_ref=dst,
                    send_sem=back_send.at[n],
                    recv_sem=back_recv.at[n],
                    device_id=tile(*where),
                    device_id_type=MESH,
                )
                for n, (src, dst, where) in enumerate(back_copies)
            ]
            for copy in back_copies:
                copy.start()

        def scatter(i, b=b, summed=summed):
            here = pl.ds(pl.multiple_of(i * 512, 512), 512)
            after = pl.ds(pl.multiple_of(i * 512 + 128, 128), 512)
            part = dot_nn(summed, pick[b, :, here])
            if b == 0:
                up_part[:, here] = part[0:portion]
                mid_part[:, here] = part[portion : 2 * portion]
                down_part[:, after] = part[2 * portion :]
            else:
                up_part[:, here] += part[0:portion]
                mid_part[:, here] += part[portion : 2 * portion]
                down_part[:, after] += part[2 * portion :]

        loop(cells // 512, scatter, 2)

    def finish(r):
        here = pl.ds(pl.multiple_of(r * 128, 128), 128)
        below = pl.ds(pl.multiple_of((r + 1) * 128, 128), 128)
        grad_ref[pl.ds(r, portion, stride=rows), :] = up_part[:, below] + mid_part[:, here] + down_part[:, here]

    loop(rows, finish, 4)
    for copy in back_copies:
        copy.wait_recv()
    lane = iota((portion, 128), 1)
    block = side_in[0].astype(F32)
    for n, start in ((1, 32), (2, 64), (3, 80), (4, 96), (5, 112)):
        block = jnp.where(lane >= start, side_in[n].astype(F32), block)
    block = block.astype(BF16)

    for n, line in ((0, rows - 1), (1, 0)):
        grad_ref[pl.ds(line, portion, stride=rows), :] += row_in[n].astype(F32)

    def patch_edges(i):
        part = dot_nn(block, edge[:, pl.ds(pl.multiple_of(i * 1024, 1024), 1024)])
        for n in range(8):
            grad_ref[pl.ds(i * 8 + n, portion, stride=rows), :] += part[:, n * 128 : (n + 1) * 128]

    loop(rows // 8, patch_edges, 4)
    for copy in halo + field_out + sum(relays, []) + sum(shares, []) + back_copies:
        copy.wait_send()


def per_device(
    latent,
    conv_weight,
    mid_weight,
    out_weight,
    vertical_inner_matrix,
    vertical_outer_matrix,
    obs_values,
    obs_weight,
    obs_index,
    obs_count,
):
    chans, rows, cols = latent.shape
    groups, hidden = conv_weight.shape[:2]
    slots, channels = obs_values.shape[2:]
    n_lev = lax.axis_size("lev")
    cells = rows * cols
    portion = chans // n_lev
    width = groups * hidden
    column = vertical_inner_matrix.shape[0]
    conv = conv_weight.transpose(0, 2, 1, 3)
    half = 3 * portion // 2
    vmem = pltpu.VMEM
    dma = pltpu.SemaphoreType.DMA
    grad = pl.pallas_call(
        kernel,
        out_shape=jax.ShapeDtypeStruct((portion * rows, cols), F32),
        in_specs=[pl.BlockSpec(memory_space=pl.ANY)] * 10,
        out_specs=pl.BlockSpec(memory_space=pltpu.VMEM),
        scratch_shapes=[
            vmem((chans * rows, cols), BF16),
            vmem(conv.shape, BF16),
            vmem(mid_weight.shape, BF16),
            vmem(out_weight.shape, BF16),
            vmem(vertical_inner_matrix.shape, BF16),
            vmem(vertical_outer_matrix.shape, BF16),
            vmem((slots, channels), F32),
            vmem((1, channels), F32),
            vmem((1, slots), jnp.int32),
            vmem((1, 1), jnp.int32),
            pltpu.SMEM((1, slots), jnp.int32),
            vmem((rows, chans, cols), BF16),
            vmem(((rows + 2) * 2 * (cols + 8), 128), F32),
            vmem((slots * 24, 128), F32),
            vmem((3, slots, cells), BF16),
            vmem((128, cells), BF16),
            vmem((6, slots, 128), BF16),
            vmem((2 * rows + 32, chans), F32),
            vmem((2 * rows + 32, chans), F32),
            vmem((2, cols, chans), BF16),
            vmem((cols, chans), BF16),
            vmem((cols, chans), BF16),
            vmem((slots, width), F32),
            vmem((slots, width), BF16),
            vmem((slots, width), F32),
            vmem((slots, width), F32),
            vmem((slots, column), BF16),
            vmem((slots, column), F32),
            vmem((channels, slots), BF16),
            vmem((slots, channels), BF16),
            vmem((slots, channels), BF16),
            vmem((slots, channels), F32),
            vmem((channels, width), BF16),
            vmem((slots, slots), BF16),
            vmem((3, n_lev, 3 * portion, slots), BF16),
            vmem((3, 2, half, slots), BF16),
            vmem((3, 2, half, slots), BF16),
            vmem((3, 4, half, slots), BF16),
            vmem((portion, cells + cols), F32),
            vmem((portion, cells), F32),
            vmem((portion, cells + cols), F32),
            vmem((2, portion, cols), BF16),
            vmem((2, portion, cols), BF16),
            vmem((portion, 128), BF16),
            vmem((6, portion, 128), BF16),
            dma((11,)),
            dma((8,)),
            dma((8,)),
            dma((n_lev - 1,)),
            dma((n_lev - 1,)),
            dma((3, 2)),
            dma((3, 2)),
            dma((3, 4)),
            dma((3, 4)),
            dma((8,)),
            dma((8,)),
        ],
        compiler_params=pltpu.CompilerParams(
            collective_id=0, has_side_effects=True, vmem_limit_bytes=60 * 1024 * 1024
        ),
        name="slots_step",
    )(
        latent.reshape(chans * rows, cols),
        conv,
        mid_weight,
        out_weight,
        vertical_inner_matrix,
        vertical_outer_matrix,
        obs_values.reshape(slots, channels),
        obs_weight,
        obs_index.reshape(1, slots),
        obs_count,
    )
    mine = lax.dynamic_slice_in_dim(latent, lax.axis_index("lev") * portion, portion, 0)
    return mine.astype(F32) + grad.reshape(portion, rows, cols)


def solution(mesh):
    return jax.shard_map(
        per_device,
        mesh=mesh,
        in_specs=(
            P(None, "lat", "lon"),
            P("lev", None, None, None),
            P("lev", None, None),
            P("lev", None, None),
            P(),
            P(),
            P("lat", "lon", None, None),
            P(),
            P("lat", "lon", None),
            P("lat", "lon"),
        ),
        out_specs=P("lev", "lat", "lon"),
        check_vma=False,
    )
```

```python
import functools

import jax
import jax.numpy as jnp
from jax import lax
from jax.experimental import pallas as pl
from jax.experimental.pallas import tpu as pltpu
from jax.sharding import PartitionSpec as P

KAPPA = 0.7978845608028654
CUBIC = 0.044715
F32 = jnp.float32
BF16 = jnp.bfloat16
MESH = pl.DeviceIdType.MESH


def gelu_slope(pre):
    tanh_v = jnp.tanh(KAPPA * (pre + CUBIC * pre * pre * pre))
    half = 0.5 * (1.0 + tanh_v)
    value = pre * half
    slope = half + 0.5 * pre * (1.0 - tanh_v * tanh_v) * (KAPPA + 3.0 * KAPPA * CUBIC * pre * pre)
    return (value, slope)


def dot_nn(x, y):
    return lax.dot_general(x, y, (((1,), (0,)), ((), ())), preferred_element_type=F32)


def dot_nt(x, y):
    return lax.dot_general(x, y, (((1,), (1,)), ((), ())), preferred_element_type=F32)


def iota(shape, dim):
    return lax.broadcasted_iota(jnp.int32, shape, dim)


def loop(count, body, unroll=1):
    def step(i, carry):
        body(i)
        return carry

    lax.fori_loop(0, count, step, 0, unroll=unroll)


def kernel(
    latent_hbm,
    conv_hbm,
    mid_hbm,
    out_hbm,
    inner_hbm,
    outer_hbm,
    obs_hbm,
    weight_hbm,
    index_hbm,
    count_hbm,
    grad_ref,
    raw,
    conv,
    mid_ref,
    out_ref,
    inner,
    outer,
    obs,
    weight_ref,
    index_ref,
    count_ref,
    index_smem,
    slab,
    table,
    patch,
    patches,
    pick,
    edge,
    side_pick,
    side_send,
    side,
    row_out,
    north,
    south,
    pre,
    act,
    slope_one,
    slope_two,
    act_col,
    slope_col,
    fields,
    fields_t,
    cast,
    misfit,
    out_pad,
    eye,
    taps,
    relay_in,
    relay_out,
    taps_in,
    summed,
    up_part,
    mid_part,
    down_part,
    row_send,
    row_in,
    side_out,
    side_in,
    first_sem,
    load_sem,
    halo_send,
    halo_recv,
    field_send,
    field_recv,
    relay_send,
    relay_recv,
    taps_send,
    taps_recv,
    back_send,
    back_recv,
):
    lev, lat, lon = lax.axis_index("lev"), lax.axis_index("lat"), lax.axis_index("lon")
    n_lev, n_lat, n_lon = lax.axis_size("lev"), lax.axis_size("lat"), lax.axis_size("lon")
    slots = pick.shape[1]
    cells = pick.shape[2]
    chans = slab.shape[1]
    rows = cells // 128
    groups, hidden = mid_ref.shape[:2]
    levels = out_ref.shape[1]
    own = groups * levels
    portion = chans // n_lev
    pitch = table.shape[0] // (rows + 2)

    pairs = (
        (index_hbm, index_smem),
        (index_hbm, index_ref),
        (count_hbm, count_ref),
        (conv_hbm, conv),
        (mid_hbm, mid_ref),
        (out_hbm, out_ref),
        (inner_hbm, inner),
        (outer_hbm, outer),
        (obs_hbm, obs),
        (weight_hbm, weight_ref.at[0]),
    )
    loads = [pltpu.make_async_copy(src, dst, load_sem.at[n]) for n, (src, dst) in enumerate(pairs)]
    pieces = 4
    first_loads = []
    for n in range(pieces):
        part = pl.ds(n * (raw.shape[0] // pieces), raw.shape[0] // pieces)
        first_loads.append(pltpu.make_async_copy(latent_hbm.at[part], raw.at[part], first_sem.at[n]))
    for load in first_loads + loads[:3]:
        load.start()

    def tile(dlat, dlon):
        return (lev, lax.rem(lat + dlat + n_lat, n_lat), lax.rem(lon + dlon + n_lon, n_lon))

    def peer(d):
        return (lax.rem(lev + d, n_lev), lat, lon)

    around = [(x, y) for x in (-1, 0, 1) for y in (-1, 0, 1) if (x, y) != (0, 0)]
    barrier = pltpu.get_barrier_semaphore()
    for x, y in around:
        pl.semaphore_signal(barrier, inc=1, device_id=tile(x, y), device_id_type=MESH)
    for d in range(1, n_lev):
        pl.semaphore_signal(barrier, inc=1, device_id=peer(d), device_id_type=MESH)

    square = iota((slots, slots), 0) == iota((slots, slots), 1)
    eye[...] = jnp.where(square, 1.0, 0.0).astype(BF16)
    order = iota((slots, 1), 0)
    order = lax.bitwise_and(order, 7) * rows + lax.shift_right_logical(order, 3)
    order = jnp.where(iota((slots, slots), 1) == order, 1.0, 0.0).astype(BF16)

    def relayout(i):
        start = i * 16 * rows
        parts = [
            dot_nn(order, raw[pl.ds(start + h * 8 * rows, 8 * rows), :]).reshape(rows, 8, 128) for h in range(2)
        ]
        slab[:, pl.ds(i * 16, 16), :] = jnp.concatenate(parts, axis=1).astype(BF16)

    for n, load in enumerate(first_loads):
        load.wait()
        if n == pieces - 1:
            for later in loads[3:]:
                later.start()
        for i in range(chans // 16 // pieces):
            relayout(n * (chans // 16 // pieces) + i)

    def put_row(line, value):
        start = line * pitch + 2
        table[pl.ds(start, 128, stride=2), :] = value[:, 0:128]
        table[pl.ds(start + 1, 128, stride=2), :] = value[:, 128:256]

    def table_row(r):
        put_row(r + 1, dot_nt(eye[0:128, 0:128], slab[r]))

    loop(rows, table_row, rows)

    for n, line in ((0, 0), (1, rows - 1)):
        row_out[n] = dot_nt(eye[0:128, 0:128], slab[line]).astype(BF16)
    for h in range(2):
        part = slice(h * 128, (h + 1) * 128)
        side_send[0:rows, part] = table[pl.ds(pitch + 256 + h, rows, stride=pitch), :]
        side_send[rows : 2 * rows, part] = table[pl.ds(pitch + 2 + h, rows, stride=pitch), :]
        for n, at in enumerate(
            (rows * pitch + 256, rows * pitch + 2, pitch + 256, pitch + 2)
        ):
            first = 2 * rows + 8 * n
            side_send[first : first + 8, part] = jnp.broadcast_to(table[at + h : at + h + 1, :], (8, 128))

    pl.semaphore_wait(barrier, len(around) + n_lev - 1)
    halo = [(row_out.at[0], south, (-1, 0)), (row_out.at[1], north, (1, 0))]
    sides = [(0, 32, (0, 1)), (32, 32, (0, -1)), (64, 8, (1, 1)), (72, 8, (1, -1)), (80, 8, (-1, 1)), (88, 8, (-1, -1))]
    for first, length, where in sides:
        halo.append((side_send.at[pl.ds(first, length)], side.at[pl.ds(first, length)], where))
    halo = [
        pltpu.make_async_remote_copy(
            src_ref=src,
            dst_ref=dst,
            send_sem=halo_send.at[n],
            recv_sem=halo_recv.at[n],
            device_id=tile(*where),
            device_id_type=MESH,
        )
        for n, (src, dst, where) in enumerate(halo)
    ]
    for copy in halo:
        copy.start()

    out_pad[...] = jnp.zeros(out_pad.shape, BF16)
    for load in loads[:6]:
        load.wait()
    for g in range(groups):
        part = pl.ds(pl.multiple_of(lev * own + g * levels, 16), levels)
        out_pad[part, g * hidden : (g + 1) * hidden] = out_ref[g]

    for copy in halo:
        copy.wait_recv()
    has_north = jnp.where(lat > 0, 1.0, 0.0)
    has_south = jnp.where(lat < n_lat - 1, 1.0, 0.0)
    put_row(0, north[...].astype(F32) * has_north)
    put_row(rows + 1, south[...].astype(F32) * has_south)
    for h in range(2):
        part = slice(h * 128, (h + 1) * 128)
        table[pl.ds(pitch + h, rows, stride=pitch), :] = side[0:rows, part]
        table[pl.ds(pitch + 258 + h, rows, stride=pitch), :] = side[rows : 2 * rows, part]
        low = (rows + 1) * pitch
        for n, (at, scale) in enumerate(((0, has_north), (258, has_north), (low, has_south), (low + 258, has_south))):
            first = 2 * rows + 8 * n
            table[at + h : at + h + 1, :] = side[first : first + 1, part] * scale

    def slot_patch(k):
        where = index_smem[0, k]
        start = lax.shift_right_logical(where, 7) * pitch + lax.bitwise_and(where, 127) * 2
        for a in range(3):
            patch[pl.ds(pl.multiple_of(k * 24 + a * 8, 8), 8), :] = table[pl.ds(start + a * pitch, 8), :]

    loop(slots, slot_patch, 8)

    step = 32
    sets = 2
    per_set = groups // sets

    def field_copy(p, d, source):
        part = pl.ds(pl.multiple_of(source * own + p * (own // sets), 16), own // sets)
        return pltpu.make_async_remote_copy(
            src_ref=fields.at[part],
            dst_ref=fields.at[part],
            send_sem=field_send.at[p, d - 1],
            recv_sem=field_recv.at[p, d - 1],
            device_id=peer(d),
            device_id_type=MESH,
        )

    field_out = []
    for p in range(sets):
        span = slice(p * per_set * hidden, (p + 1) * per_set * hidden)
        first = p * per_set
        total = None
        for t in range(9):
            if p == 0:
                parts = [patch[pl.ds((t // 3) * 8 + (t % 3) * 2 + h, slots, stride=24), :] for h in range(2)]
                patches[t] = jnp.concatenate(parts, axis=1).astype(BF16)
            kernel_t = conv[first : first + per_set, t].reshape(per_set * hidden, chans)
            part = dot_nt(patches[t], kernel_t)
            total = part if total is None else total + part
        pre[:, span] = total

        def gelu_one(i, span=span):
            part = pl.ds(pl.multiple_of(i * step, step), step)
            value, slope = gelu_slope(pre[part, span])
            act[part, span] = value.astype(BF16)
            slope_one[part, span] = slope

        def gelu_two(i, span=span):
            part = pl.ds(pl.multiple_of(i * step, step), step)
            value, slope = gelu_slope(pre[part, span])
            act[part, span] = value.astype(BF16)
            slope_two[part, span] = slope

        loop(slots // step, gelu_one, 4)
        for g in range(first, first + per_set):
            part = slice(g * hidden, (g + 1) * hidden)
            pre[:, part] = dot_nt(act[:, part], mid_ref[g])
        loop(slots // step, gelu_two, 4)
        for g in range(first, first + per_set):
            part = slice(g * hidden, (g + 1) * hidden)
            fields[pl.ds(pl.multiple_of(lev * own + g * levels, 16), levels), :] = dot_nt(
                out_ref[g], act[:, part]
            ).astype(BF16)
        for d in range(1, n_lev):
            copy = field_copy(p, d, lev)
            copy.start()
            field_out.append(copy)

    spread = jnp.broadcast_to(index_ref[...].astype(F32), (slots, slots))
    index = jnp.sum(jnp.where(square, spread, 0.0), axis=1, keepdims=True).astype(jnp.int32)
    row = lax.shift_right_logical(index, 7)
    col = lax.bitwise_and(index, 127)
    live = jnp.where(iota((slots, 1), 0) < count_ref[...], 1.0, 0.0)
    row_wide = jnp.broadcast_to(row, (slots, 128))
    lane_wide = iota((slots, 128), 1)
    last = (rows - 1) * 128
    for b in range(3):
        cast[:, b * 128 : (b + 1) * 128] = jnp.where(lane_wide == col + (b - 1), 1.0, 0.0).astype(BF16)

    def pick_row(r):
        hit = row_wide == r
        for b in range(3):
            column_b = cast[:, b * 128 : (b + 1) * 128].astype(F32)
            pick[b, :, pl.ds(pl.multiple_of(r * 128, 128), 128)] = jnp.where(hit, column_b, 0.0).astype(BF16)

    loop(rows, pick_row)

    for a in range(3):
        line = row + (a - 1)
        above = (line < 0) & (lat > 0)
        below = (line >= rows) & (lat < n_lat - 1)
        inside = (line >= 0) & (line < rows)
        for n, b in enumerate((0, 2)):
            first, upper, lower = (0, 64, 96) if b == 0 else (32, 80, 112)
            out = (col == 0) if b == 0 else (col == 127)
            target = jnp.where(inside, first + line, jnp.where(above, upper, jnp.where(below, lower, -1)))
            target = jnp.where(out, target, -1)
            side_pick[n * 3 + a] = jnp.where(lane_wide == target, 1.0, 0.0).astype(BF16)

    j = iota((128, 1), 0)
    spot = jnp.where(j < 32, j * 128 + 127, (j - 32) * 128)
    for at, cell in ((64, last + 127), (80, last), (96, 127), (112, 0)):
        spot = jnp.where(j == at, cell, jnp.where(j > at, -1, spot))

    def edge_block(i):
        start = pl.multiple_of(i * 512, 512)
        edge[:, pl.ds(start, 512)] = jnp.where(iota((128, 512), 1) + start == spot, 1.0, 0.0).astype(BF16)

    loop(cells // 512, edge_block)
    up_part[:, cells : cells + 128] = jnp.zeros((portion, 128), F32)
    down_part[:, 0:128] = jnp.zeros((portion, 128), F32)

    for load in loads[6:]:
        load.wait()
    for p in range(sets):
        for d in range(1, n_lev):
            field_copy(p, d, lax.rem(lev + n_lev - d, n_lev)).wait_recv()

    blocks = fields.shape[0] // 256
    for i in range(blocks):
        part = slice(i * 256, (i + 1) * 256)
        fields_t[:, part] = dot_nt(eye[...], fields[part, :]).astype(BF16)

    def column(i):
        part = pl.ds(pl.multiple_of(i * 256, 256), 256)
        value, slope = gelu_slope(dot_nt(fields_t[...], inner[part, :]))
        slope_col[:, part] = slope
        act_col[:, part] = value.astype(BF16)

    loop(inner.shape[0] // 256, column, 4)

    def compare(i):
        part = pl.ds(pl.multiple_of(i * 256, 256), 256)
        forecast = fields_t[:, part].astype(F32) + dot_nt(act_col[...], outer[part, :])
        value = (forecast - obs[:, part]) * live * weight_ref[:, part]
        misfit[:, part] = value
        cast[:, part] = value.astype(BF16)

    loop(blocks, compare, 3)

    def column_back(i):
        part = pl.ds(pl.multiple_of(i * 256, 256), 256)
        act_col[:, part] = (dot_nn(cast[...], outer[:, part]) * slope_col[:, part]).astype(BF16)

    loop(inner.shape[0] // 256, column_back, 4)

    def fields_back(i):
        part = pl.ds(pl.multiple_of(i * 256, 256), 256)
        fields_t[:, part] = (misfit[:, part] + dot_nn(act_col[...], inner[:, part])).astype(BF16)

    loop(blocks, fields_back, 3)
    act[...] = (dot_nn(fields_t[...], out_pad[...]) * slope_two[...]).astype(BF16)
    for g in range(groups):
        part = slice(g * hidden, (g + 1) * hidden)
        slope_one[:, part] = slope_one[:, part] * dot_nn(act[:, part], mid_ref[g])
    act[...] = slope_one[...].astype(BF16)

    above_lev, below_lev, across = lax.rem(lev + 1, n_lev), lax.rem(lev + 3, n_lev), lax.rem(lev + 2, n_lev)
    half = 3 * portion // 2
    low_half, high_half = pl.ds(0, half), pl.ds(half, half)

    def send(src, dst, sems, device):
        return pltpu.make_async_remote_copy(
            src_ref=src,
            dst_ref=dst,
            send_sem=sems[0],
            recv_sem=sems[1],
            device_id=(device, lat, lon),
            device_id_type=MESH,
        )

    def relay_copies(b):
        return [
            send(taps.at[b, across, low_half], relay_in.at[b, 0], (relay_send.at[b, 0], relay_recv.at[b, 0]), above_lev),
            send(taps.at[b, across, high_half], relay_in.at[b, 1], (relay_send.at[b, 1], relay_recv.at[b, 1]), below_lev),
        ]

    def taps_copies(b):
        sources = (
            (relay_out.at[b, 0], above_lev),
            (taps.at[b, above_lev, high_half], above_lev),
            (taps.at[b, below_lev, low_half], below_lev),
            (relay_out.at[b, 1], below_lev),
        )
        return [
            send(src, taps_in.at[b, n], (taps_send.at[b, n], taps_recv.at[b, n]), device)
            for n, (src, device) in enumerate(sources)
        ]

    relays = [relay_copies(b) for b in range(3)]
    shares = [taps_copies(b) for b in range(3)]
    for b in range(3):

        def back(a, b=b):
            kernel_t = conv[:, a * 3 + b].reshape(groups * hidden, chans)
            part = dot_nn(act[...], kernel_t).astype(BF16)
            part = dot_nt(eye[...], part).astype(BF16)
            for d in range(n_lev):
                taps[b, d, pl.ds(pl.multiple_of(a * portion, 16), portion), :] = part[
                    d * portion : (d + 1) * portion
                ]

        loop(3, back, 3)
        for copy in relays[b]:
            copy.start()
    for b in range(3):
        shares[b][1].start()
        shares[b][2].start()
    for b in range(3):
        for copy in relays[b]:
            copy.wait_recv()
        for n, (device, part) in enumerate(((above_lev, low_half), (below_lev, high_half))):
            mine = taps[b, device, part, :].astype(F32)
            relay_out[b, n] = (mine + relay_in[b, n].astype(F32)).astype(BF16)
        shares[b][0].start()
        shares[b][3].start()

    upper = jnp.zeros((portion, 128), F32)
    lower = jnp.zeros((portion, 128), F32)
    beside = jnp.zeros((portion, 128), F32)
    for b in range(3):
        for copy in shares[b]:
            copy.wait_recv()
        halves = []
        for part, first, second in ((low_half, 0, 2), (high_half, 1, 3)):
            total = taps[b, lev, part, :].astype(F32)
            halves.append(total + taps_in[b, first].astype(F32) + taps_in[b, second].astype(F32))
        summed_b = jnp.concatenate(halves, axis=0).astype(BF16)
        summed[b] = summed_b
        upper = upper + dot_nn(summed_b[0:portion], pick[b, :, 0:128])
        lower = lower + dot_nn(summed_b[2 * portion : 3 * portion], pick[b, :, last : last + 128])
        if b != 1:
            for a in range(3):
                beside = beside + dot_nn(summed_b[a * portion : (a + 1) * portion], side_pick[(b // 2) * 3 + a])
        if b == 2:
            row_send[0] = (upper * has_north).astype(BF16)
            row_send[1] = (lower * has_south).astype(BF16)
            side_out[...] = beside.astype(BF16)
            back_copies = [(row_send.at[0], row_in.at[0], (-1, 0)), (row_send.at[1], row_in.at[1], (1, 0))]
            back_sides = [(0, -1), (0, 1), (-1, -1), (-1, 1), (1, -1), (1, 1)]
            for n, where in enumerate(back_sides):
                back_copies.append((side_out, side_in.at[n], where))
            back_copies = [
                pltpu.make_async_remote_copy(
                    src_ref=src,
                    dst_ref=dst,
                    send_sem=back_send.at[n],
                    recv_sem=back_recv.at[n],
                    device_id=tile(*where),
                    device_id_type=MESH,
                )
                for n, (src, dst, where) in enumerate(back_copies)
            ]
            for copy in back_copies:
                copy.start()

    def scatter(i):
        here = pl.ds(pl.multiple_of(i * 512, 512), 512)
        after = pl.ds(pl.multiple_of(i * 512 + 128, 128), 512)
        part = dot_nn(summed[0], pick[0, :, here])
        part = part + dot_nn(summed[1], pick[1, :, here])
        part = part + dot_nn(summed[2], pick[2, :, here])
        up_part[:, here] = part[0:portion]
        mid_part[:, here] = part[portion : 2 * portion]
        down_part[:, after] = part[2 * portion :]

    loop(cells // 512, scatter, 2)

    def finish(r):
        here = pl.ds(pl.multiple_of(r * 128, 128), 128)
        below = pl.ds(pl.multiple_of((r + 1) * 128, 128), 128)
        grad_ref[pl.ds(r, portion, stride=rows), :] = up_part[:, below] + mid_part[:, here] + down_part[:, here]

    loop(rows, finish, 4)
    for copy in back_copies:
        copy.wait_recv()
    lane = iota((portion, 128), 1)
    block = side_in[0].astype(F32)
    for n, start in ((1, 32), (2, 64), (3, 80), (4, 96), (5, 112)):
        block = jnp.where(lane >= start, side_in[n].astype(F32), block)
    block = block.astype(BF16)

    for n, line in ((0, rows - 1), (1, 0)):
        grad_ref[pl.ds(line, portion, stride=rows), :] += row_in[n].astype(F32)

    def patch_edges(i):
        part = dot_nn(block, edge[:, pl.ds(pl.multiple_of(i * 1024, 1024), 1024)])
        for n in range(8):
            grad_ref[pl.ds(i * 8 + n, portion, stride=rows), :] += part[:, n * 128 : (n + 1) * 128]

    loop(rows // 8, patch_edges, 4)
    for copy in halo + field_out + sum(relays, []) + sum(shares, []) + back_copies:
        copy.wait_send()


def per_device(
    latent,
    conv_weight,
    mid_weight,
    out_weight,
    vertical_inner_matrix,
    vertical_outer_matrix,
    obs_values,
    obs_weight,
    obs_index,
    obs_count,
):
    chans, rows, cols = latent.shape
    groups, hidden = conv_weight.shape[:2]
    slots, channels = obs_values.shape[2:]
    n_lev = lax.axis_size("lev")
    cells = rows * cols
    portion = chans // n_lev
    width = groups * hidden
    column = vertical_inner_matrix.shape[0]
    conv = conv_weight.transpose(0, 2, 1, 3)
    half = 3 * portion // 2
    vmem = pltpu.VMEM
    dma = pltpu.SemaphoreType.DMA
    operands = [
        latent.reshape(chans * rows, cols),
        conv,
        mid_weight,
        out_weight,
        vertical_inner_matrix,
        vertical_outer_matrix,
        obs_values.reshape(slots, channels),
        obs_weight,
        obs_index.reshape(1, slots),
    ]
    operands = [pltpu.with_memory_space_constraint(x, pltpu.HBM) for x in operands]
    grad = pl.pallas_call(
        kernel,
        out_shape=jax.ShapeDtypeStruct((portion * rows, cols), F32),
        in_specs=[pl.BlockSpec(memory_space=pl.ANY)] * 10,
        out_specs=pl.BlockSpec(memory_space=pltpu.VMEM),
        scratch_shapes=[
            vmem((chans * rows, cols), BF16),
            vmem(conv.shape, BF16),
            vmem(mid_weight.shape, BF16),
            vmem(out_weight.shape, BF16),
            vmem(vertical_inner_matrix.shape, BF16),
            vmem(vertical_outer_matrix.shape, BF16),
            vmem((slots, channels), F32),
            vmem((1, channels), F32),
            vmem((1, slots), jnp.int32),
            vmem((1, 1), jnp.int32),
            pltpu.SMEM((1, slots), jnp.int32),
            vmem((rows, chans, cols), BF16),
            vmem(((rows + 2) * 2 * (cols + 8), 128), F32),
            vmem((slots * 24, 128), F32),
            vmem((9, slots, chans), BF16),
            vmem((3, slots, cells), BF16),
            vmem((128, cells), BF16),
            vmem((6, slots, 128), BF16),
            vmem((2 * rows + 32, chans), F32),
            vmem((2 * rows + 32, chans), F32),
            vmem((2, cols, chans), BF16),
            vmem((cols, chans), BF16),
            vmem((cols, chans), BF16),
            vmem((slots, width), F32),
            vmem((slots, width), BF16),
            vmem((slots, width), F32),
            vmem((slots, width), F32),
            vmem((slots, column), BF16),
            vmem((slots, column), F32),
            vmem((channels, slots), BF16),
            vmem((slots, channels), BF16),
            vmem((slots, channels), BF16),
            vmem((slots, channels), F32),
            vmem((channels, width), BF16),
            vmem((slots, slots), BF16),
            vmem((3, n_lev, 3 * portion, slots), BF16),
            vmem((3, 2, half, slots), BF16),
            vmem((3, 2, half, slots), BF16),
            vmem((3, 4, half, slots), BF16),
            vmem((3, 3 * portion, slots), BF16),
            vmem((portion, cells + cols), F32),
            vmem((portion, cells), F32),
            vmem((portion, cells + cols), F32),
            vmem((2, portion, cols), BF16),
            vmem((2, portion, cols), BF16),
            vmem((portion, 128), BF16),
            vmem((6, portion, 128), BF16),
            dma((4,)),
            dma((10,)),
            dma((8,)),
            dma((8,)),
            dma((2, n_lev - 1)),
            dma((2, n_lev - 1)),
            dma((3, 2)),
            dma((3, 2)),
            dma((3, 4)),
            dma((3, 4)),
            dma((8,)),
            dma((8,)),
        ],
        compiler_params=pltpu.CompilerParams(
            collective_id=0, has_side_effects=True, vmem_limit_bytes=50 * 1024 * 1024
        ),
        name="slots_step",
    )(*operands, obs_count)
    mine = lax.dynamic_slice_in_dim(latent, lax.axis_index("lev") * portion, portion, 0)
    return mine.astype(F32) + grad.reshape(portion, rows, cols)


def solution(mesh):
    return jax.shard_map(
        per_device,
        mesh=mesh,
        in_specs=(
            P(None, "lat", "lon"),
            P("lev", None, None, None),
            P("lev", None, None),
            P("lev", None, None),
            P(),
            P(),
            P("lat", "lon", None, None),
            P(),
            P("lat", "lon", None),
            P("lat", "lon"),
        ),
        out_specs=P("lev", "lat", "lon"),
        check_vma=False,
    )
```

```python
import functools

import jax
import jax.numpy as jnp
from jax import lax
from jax.experimental import pallas as pl
from jax.experimental.pallas import tpu as pltpu
from jax.sharding import PartitionSpec as P

KAPPA = 0.7978845608028654
CUBIC = 0.044715
F32 = jnp.float32
BF16 = jnp.bfloat16
MESH = pl.DeviceIdType.MESH


def gelu_slope(pre):
    tanh_v = jnp.tanh(KAPPA * (pre + CUBIC * pre * pre * pre))
    half = 0.5 * (1.0 + tanh_v)
    value = pre * half
    slope = half + 0.5 * pre * (1.0 - tanh_v * tanh_v) * (KAPPA + 3.0 * KAPPA * CUBIC * pre * pre)
    return (value, slope)


def dot_nn(x, y):
    return lax.dot_general(x, y, (((1,), (0,)), ((), ())), preferred_element_type=F32)


def dot_nt(x, y):
    return lax.dot_general(x, y, (((1,), (1,)), ((), ())), preferred_element_type=F32)


def iota(shape, dim):
    return lax.broadcasted_iota(jnp.int32, shape, dim)


def loop(count, body, unroll=1):
    def step(i, carry):
        body(i)
        return carry

    lax.fori_loop(0, count, step, 0, unroll=unroll)


def kernel(
    latent_hbm,
    conv_hbm,
    mid_hbm,
    out_hbm,
    inner_hbm,
    outer_hbm,
    obs_hbm,
    weight_hbm,
    index_hbm,
    count_hbm,
    grad_ref,
    raw,
    conv,
    mid_ref,
    out_ref,
    inner,
    outer,
    obs,
    weight_ref,
    index_ref,
    count_ref,
    index_smem,
    slab,
    table,
    patch,
    patches,
    pick,
    edge,
    side_pick,
    side_send,
    side,
    row_out,
    north,
    south,
    pre,
    act,
    slope_one,
    slope_two,
    act_col,
    slope_col,
    fields,
    fields_t,
    cast,
    misfit,
    out_pad,
    eye,
    taps,
    relay_in,
    relay_out,
    taps_in,
    summed,
    up_part,
    mid_part,
    down_part,
    row_send,
    row_in,
    side_out,
    side_in,
    strips,
    strips_in,
    first_sem,
    load_sem,
    halo_send,
    halo_recv,
    field_send,
    field_recv,
    relay_send,
    relay_recv,
    taps_send,
    taps_recv,
    back_send,
    back_recv,
    strip_send,
    strip_recv,
):
    lev, lat, lon = lax.axis_index("lev"), lax.axis_index("lat"), lax.axis_index("lon")
    n_lev, n_lat, n_lon = lax.axis_size("lev"), lax.axis_size("lat"), lax.axis_size("lon")
    slots = pick.shape[1]
    cells = pick.shape[2]
    chans = slab.shape[1]
    rows = cells // 128
    groups, hidden = mid_ref.shape[:2]
    levels = out_ref.shape[1]
    own = groups * levels
    portion = chans // n_lev
    pitch = table.shape[0] // (rows + 2)

    pairs = (
        (index_hbm, index_smem),
        (index_hbm, index_ref),
        (count_hbm, count_ref),
        (conv_hbm, conv),
        (mid_hbm, mid_ref),
        (out_hbm, out_ref),
        (inner_hbm, inner),
        (outer_hbm, outer),
        (obs_hbm, obs),
        (weight_hbm, weight_ref.at[0]),
    )
    loads = [pltpu.make_async_copy(src, dst, load_sem.at[n]) for n, (src, dst) in enumerate(pairs)]
    pieces = 4
    first_loads = []
    for n in range(pieces):
        part = pl.ds(n * (raw.shape[0] // pieces), raw.shape[0] // pieces)
        first_loads.append(pltpu.make_async_copy(latent_hbm.at[part], raw.at[part], first_sem.at[n]))
    for load in first_loads + loads[:3]:
        load.start()

    def tile(dlat, dlon):
        return (lev, lax.rem(lat + dlat + n_lat, n_lat), lax.rem(lon + dlon + n_lon, n_lon))

    def peer(d):
        return (lax.rem(lev + d, n_lev), lat, lon)

    around = [(x, y) for x in (-1, 0, 1) for y in (-1, 0, 1) if (x, y) != (0, 0)]
    barrier = pltpu.get_barrier_semaphore()
    for x, y in around:
        pl.semaphore_signal(barrier, inc=1, device_id=tile(x, y), device_id_type=MESH)
    for d in range(1, n_lev):
        pl.semaphore_signal(barrier, inc=1, device_id=peer(d), device_id_type=MESH)

    square = iota((slots, slots), 0) == iota((slots, slots), 1)
    eye[...] = jnp.where(square, 1.0, 0.0).astype(BF16)
    order = iota((slots, 1), 0)
    order = lax.bitwise_and(order, 7) * rows + lax.shift_right_logical(order, 3)
    order = jnp.where(iota((slots, slots), 1) == order, 1.0, 0.0).astype(BF16)

    def relayout(i):
        start = i * 16 * rows
        parts = [
            dot_nn(order, raw[pl.ds(start + h * 8 * rows, 8 * rows), :]).reshape(rows, 8, 128) for h in range(2)
        ]
        slab[:, pl.ds(i * 16, 16), :] = jnp.concatenate(parts, axis=1).astype(BF16)

    for n, load in enumerate(first_loads):
        load.wait()
        if n == pieces - 1:
            for later in loads[3:]:
                later.start()
        for i in range(chans // 16 // pieces):
            relayout(n * (chans // 16 // pieces) + i)

    def put_row(line, value):
        start = line * pitch + 2
        table[pl.ds(start, 128, stride=2), :] = value[:, 0:128]
        table[pl.ds(start + 1, 128, stride=2), :] = value[:, 128:256]

    def table_row(r):
        put_row(r + 1, dot_nt(eye[0:128, 0:128], slab[r]))

    loop(rows, table_row, rows)

    for n, line in ((0, 0), (1, rows - 1)):
        row_out[n] = dot_nt(eye[0:128, 0:128], slab[line]).astype(BF16)
    for h in range(2):
        part = slice(h * 128, (h + 1) * 128)
        side_send[0:rows, part] = table[pl.ds(pitch + 256 + h, rows, stride=pitch), :]
        side_send[rows : 2 * rows, part] = table[pl.ds(pitch + 2 + h, rows, stride=pitch), :]
        for n, at in enumerate(
            (rows * pitch + 256, rows * pitch + 2, pitch + 256, pitch + 2)
        ):
            first = 2 * rows + 8 * n
            side_send[first : first + 8, part] = jnp.broadcast_to(table[at + h : at + h + 1, :], (8, 128))

    pl.semaphore_wait(barrier, len(around) + n_lev - 1)
    halo = [(row_out.at[0], south, (-1, 0)), (row_out.at[1], north, (1, 0))]
    sides = [(0, 32, (0, 1)), (32, 32, (0, -1)), (64, 8, (1, 1)), (72, 8, (1, -1)), (80, 8, (-1, 1)), (88, 8, (-1, -1))]
    for first, length, where in sides:
        halo.append((side_send.at[pl.ds(first, length)], side.at[pl.ds(first, length)], where))
    halo = [
        pltpu.make_async_remote_copy(
            src_ref=src,
            dst_ref=dst,
            send_sem=halo_send.at[n],
            recv_sem=halo_recv.at[n],
            device_id=tile(*where),
            device_id_type=MESH,
        )
        for n, (src, dst, where) in enumerate(halo)
    ]
    for copy in halo:
        copy.start()

    out_pad[...] = jnp.zeros(out_pad.shape, BF16)
    for load in loads[:6]:
        load.wait()
    for g in range(groups):
        part = pl.ds(pl.multiple_of(lev * own + g * levels, 16), levels)
        out_pad[part, g * hidden : (g + 1) * hidden] = out_ref[g]

    for copy in halo:
        copy.wait_recv()
    has_north = jnp.where(lat > 0, 1.0, 0.0)
    has_south = jnp.where(lat < n_lat - 1, 1.0, 0.0)
    put_row(0, north[...].astype(F32) * has_north)
    put_row(rows + 1, south[...].astype(F32) * has_south)
    for h in range(2):
        part = slice(h * 128, (h + 1) * 128)
        table[pl.ds(pitch + h, rows, stride=pitch), :] = side[0:rows, part]
        table[pl.ds(pitch + 258 + h, rows, stride=pitch), :] = side[rows : 2 * rows, part]
        low = (rows + 1) * pitch
        for n, (at, scale) in enumerate(((0, has_north), (258, has_north), (low, has_south), (low + 258, has_south))):
            first = 2 * rows + 8 * n
            table[at + h : at + h + 1, :] = side[first : first + 1, part] * scale

    def slot_patch(k):
        where = index_smem[0, k]
        start = lax.shift_right_logical(where, 7) * pitch + lax.bitwise_and(where, 127) * 2
        for a in range(3):
            patch[pl.ds(pl.multiple_of(k * 24 + a * 8, 8), 8), :] = table[pl.ds(start + a * pitch, 8), :]

    loop(slots, slot_patch, 8)

    step = 32
    sets = 2
    per_set = groups // sets

    def field_copy(p, d, source):
        part = pl.ds(pl.multiple_of(source * own + p * (own // sets), 16), own // sets)
        return pltpu.make_async_remote_copy(
            src_ref=fields.at[part],
            dst_ref=fields.at[part],
            send_sem=field_send.at[p, d - 1],
            recv_sem=field_recv.at[p, d - 1],
            device_id=peer(d),
            device_id_type=MESH,
        )

    field_out = []
    for p in range(sets):
        span = slice(p * per_set * hidden, (p + 1) * per_set * hidden)
        first = p * per_set
        total = None
        for t in range(9):
            if p == 0:
                parts = [patch[pl.ds((t // 3) * 8 + (t % 3) * 2 + h, slots, stride=24), :] for h in range(2)]
                patches[t] = jnp.concatenate(parts, axis=1).astype(BF16)
            kernel_t = conv[first : first + per_set, t].reshape(per_set * hidden, chans)
            part = dot_nt(patches[t], kernel_t)
            total = part if total is None else total + part
        pre[:, span] = total

        def gelu_one(i, span=span):
            part = pl.ds(pl.multiple_of(i * step, step), step)
            value, slope = gelu_slope(pre[part, span])
            act[part, span] = value.astype(BF16)
            slope_one[part, span] = slope

        def gelu_two(i, span=span):
            part = pl.ds(pl.multiple_of(i * step, step), step)
            value, slope = gelu_slope(pre[part, span])
            act[part, span] = value.astype(BF16)
            slope_two[part, span] = slope

        loop(slots // step, gelu_one, 4)
        for g in range(first, first + per_set):
            part = slice(g * hidden, (g + 1) * hidden)
            pre[:, part] = dot_nt(act[:, part], mid_ref[g])
        loop(slots // step, gelu_two, 4)
        for g in range(first, first + per_set):
            part = slice(g * hidden, (g + 1) * hidden)
            fields[pl.ds(pl.multiple_of(lev * own + g * levels, 16), levels), :] = dot_nt(
                out_ref[g], act[:, part]
            ).astype(BF16)
        for d in (1, 3) if p == 0 else (2, 1, 3):
            copy = field_copy(p, d, lev)
            copy.start()
            field_out.append(copy)

    spread = jnp.broadcast_to(index_ref[...].astype(F32), (slots, slots))
    index = jnp.sum(jnp.where(square, spread, 0.0), axis=1, keepdims=True).astype(jnp.int32)
    row = lax.shift_right_logical(index, 7)
    col = lax.bitwise_and(index, 127)
    live = jnp.where(iota((slots, 1), 0) < count_ref[...], 1.0, 0.0)
    row_wide = jnp.broadcast_to(row, (slots, 128))
    lane_wide = iota((slots, 128), 1)
    last = (rows - 1) * 128
    for b in range(3):
        cast[:, b * 128 : (b + 1) * 128] = jnp.where(lane_wide == col + (b - 1), 1.0, 0.0).astype(BF16)

    def pick_row(r):
        hit = row_wide == r
        for b in range(3):
            column_b = cast[:, b * 128 : (b + 1) * 128].astype(F32)
            pick[b, :, pl.ds(pl.multiple_of(r * 128, 128), 128)] = jnp.where(hit, column_b, 0.0).astype(BF16)

    loop(rows, pick_row)

    for a in range(3):
        line = row + (a - 1)
        above = (line < 0) & (lat > 0)
        below = (line >= rows) & (lat < n_lat - 1)
        inside = (line >= 0) & (line < rows)
        for n, b in enumerate((0, 2)):
            first, upper, lower = (0, 64, 96) if b == 0 else (32, 80, 112)
            out = (col == 0) if b == 0 else (col == 127)
            target = jnp.where(inside, first + line, jnp.where(above, upper, jnp.where(below, lower, -1)))
            target = jnp.where(out, target, -1)
            side_pick[n * 3 + a] = jnp.where(lane_wide == target, 1.0, 0.0).astype(BF16)

    j = iota((128, 1), 0)
    spot = jnp.where(j < 32, j * 128 + 127, (j - 32) * 128)
    for at, cell in ((64, last + 127), (80, last), (96, 127), (112, 0)):
        spot = jnp.where(j == at, cell, jnp.where(j > at, -1, spot))

    def edge_block(i):
        start = pl.multiple_of(i * 512, 512)
        edge[:, pl.ds(start, 512)] = jnp.where(iota((128, 512), 1) + start == spot, 1.0, 0.0).astype(BF16)

    loop(cells // 512, edge_block)

    field_copy(0, 3, lax.rem(lev + 1, n_lev)).wait_recv()
    part = pl.ds(pl.multiple_of(lax.rem(lev + 1, n_lev) * own, 16), own // sets)
    onward = pltpu.make_async_remote_copy(
        src_ref=fields.at[part],
        dst_ref=fields.at[part],
        send_sem=field_send.at[0, 1],
        recv_sem=field_recv.at[0, 1],
        device_id=peer(3),
        device_id_type=MESH,
    )
    onward.start()
    field_out.append(onward)
    for load in loads[6:]:
        load.wait()
    for p in range(sets):
        for d in range(1, n_lev):
            if (p, d) != (0, 3):
                field_copy(p, d, lax.rem(lev + n_lev - d, n_lev)).wait_recv()

    blocks = fields.shape[0] // 256
    for i in range(blocks):
        part = slice(i * 256, (i + 1) * 256)
        fields_t[:, part] = dot_nt(eye[...], fields[part, :]).astype(BF16)

    def column(i):
        part = pl.ds(pl.multiple_of(i * 256, 256), 256)
        value, slope = gelu_slope(dot_nt(fields_t[...], inner[part, :]))
        slope_col[:, part] = slope
        act_col[:, part] = value.astype(BF16)

    loop(inner.shape[0] // 256, column, 4)

    def compare(i):
        part = pl.ds(pl.multiple_of(i * 256, 256), 256)
        forecast = fields_t[:, part].astype(F32) + dot_nt(act_col[...], outer[part, :])
        value = (forecast - obs[:, part]) * live * weight_ref[:, part]
        misfit[:, part] = value
        cast[:, part] = value.astype(BF16)

    loop(blocks, compare, 3)

    def column_back(i):
        part = pl.ds(pl.multiple_of(i * 256, 256), 256)
        act_col[:, part] = (dot_nn(cast[...], outer[:, part]) * slope_col[:, part]).astype(BF16)

    loop(inner.shape[0] // 256, column_back, 4)

    def fields_back(i):
        part = pl.ds(pl.multiple_of(i * 256, 256), 256)
        fields_t[:, part] = (misfit[:, part] + dot_nn(act_col[...], inner[:, part])).astype(BF16)

    loop(blocks, fields_back, 3)
    act[...] = (dot_nn(fields_t[...], out_pad[...]) * slope_two[...]).astype(BF16)
    for g in range(groups):
        part = slice(g * hidden, (g + 1) * hidden)
        slope_one[:, part] = slope_one[:, part] * dot_nn(act[:, part], mid_ref[g])
    act[...] = slope_one[...].astype(BF16)

    above_lev, below_lev, across = lax.rem(lev + 1, n_lev), lax.rem(lev + 3, n_lev), lax.rem(lev + 2, n_lev)
    half = 3 * portion // 2
    low_half, high_half = pl.ds(0, half), pl.ds(half, half)

    def send(src, dst, sems, device):
        return pltpu.make_async_remote_copy(
            src_ref=src,
            dst_ref=dst,
            send_sem=sems[0],
            recv_sem=sems[1],
            device_id=(device, lat, lon),
            device_id_type=MESH,
        )

    def relay_copies(b):
        return [
            send(taps.at[b, across, low_half], relay_in.at[b, 0], (relay_send.at[b, 0], relay_recv.at[b, 0]), above_lev),
            send(taps.at[b, across, high_half], relay_in.at[b, 1], (relay_send.at[b, 1], relay_recv.at[b, 1]), below_lev),
        ]

    def taps_copies(b):
        sources = (
            (relay_out.at[b, 0], above_lev),
            (taps.at[b, above_lev, high_half], above_lev),
            (taps.at[b, below_lev, low_half], below_lev),
            (relay_out.at[b, 1], below_lev),
        )
        return [
            send(src, taps_in.at[b, n], (taps_send.at[b, n], taps_recv.at[b, n]), device)
            for n, (src, device) in enumerate(sources)
        ]

    relays = [relay_copies(b) for b in range(3)]
    shares = [taps_copies(b) for b in range(3)]
    for b in range(3):

        def back(a, b=b):
            kernel_t = conv[:, a * 3 + b].reshape(groups * hidden, chans)
            part = dot_nn(act[...], kernel_t).astype(BF16)
            part = dot_nt(eye[...], part).astype(BF16)
            for d in range(n_lev):
                taps[b, d, pl.ds(pl.multiple_of(a * portion, 16), portion), :] = part[
                    d * portion : (d + 1) * portion
                ]

        loop(3, back, 3)
        for copy in relays[b]:
            copy.start()
    for b in range(3):
        shares[b][1].start()
        shares[b][2].start()

    upper = jnp.zeros((chans, 128), F32)
    lower = jnp.zeros((chans, 128), F32)
    beside = jnp.zeros((chans, 128), F32)
    for b in range(3):
        tap_b = [taps[b, :, a * portion : (a + 1) * portion, :].reshape(chans, slots) for a in range(3)]
        upper = upper + dot_nn(tap_b[0], pick[b, :, 0:128])
        lower = lower + dot_nn(tap_b[2], pick[b, :, last : last + 128])
        if b != 1:
            for a in range(3):
                beside = beside + dot_nn(tap_b[a], side_pick[(b // 2) * 3 + a])
    row_send[0] = (upper * has_north).astype(BF16)
    row_send[1] = (lower * has_south).astype(BF16)
    side_out[...] = dot_nt(eye[0:128, 0:128], beside.astype(BF16)).astype(BF16)
    back_copies = [(row_send.at[0], row_in.at[0], (-1, 0)), (row_send.at[1], row_in.at[1], (1, 0))]
    back_sides = [(0, 32, (0, -1)), (32, 32, (0, 1)), (64, 16, (-1, -1)), (80, 16, (-1, 1)), (96, 16, (1, -1)), (112, 16, (1, 1))]
    for first, length, where in back_sides:
        back_copies.append((side_out.at[pl.ds(first, length)], side_in.at[pl.ds(first, length)], where))
    back_copies = [
        pltpu.make_async_remote_copy(
            src_ref=src,
            dst_ref=dst,
            send_sem=back_send.at[n],
            recv_sem=back_recv.at[n],
            device_id=tile(*where),
            device_id_type=MESH,
        )
        for n, (src, dst, where) in enumerate(back_copies)
    ]
    for copy in back_copies:
        copy.start()

    for b in range(3):
        for copy in relays[b]:
            copy.wait_recv()
        for n, (device, part) in enumerate(((above_lev, low_half), (below_lev, high_half))):
            mine = taps[b, device, part, :].astype(F32)
            relay_out[b, n] = (mine + relay_in[b, n].astype(F32)).astype(BF16)
        shares[b][0].start()
        shares[b][3].start()

    for copy in back_copies:
        copy.wait_recv()
    for n in range(2):
        strips[:, :, n * 128 : (n + 1) * 128] = row_in[n].reshape(n_lev, portion, 128)
    strips[:, :, 256:384] = dot_nt(eye[...], side_in[...]).astype(BF16).reshape(n_lev, portion, 128)
    strip_copies = [
        send(strips.at[lax.rem(lev + d, n_lev)], strips_in.at[d - 1], (strip_send.at[d - 1], strip_recv.at[d - 1]), lax.rem(lev + d, n_lev))
        for d in (2, 1, 3)
    ]
    for copy in strip_copies:
        copy.start()

    for b in range(3):
        for copy in shares[b]:
            copy.wait_recv()
        halves = []
        for part, first, second in ((low_half, 0, 2), (high_half, 1, 3)):
            total = taps[b, lev, part, :].astype(F32)
            halves.append(total + taps_in[b, first].astype(F32) + taps_in[b, second].astype(F32))
        summed[b] = jnp.concatenate(halves, axis=0).astype(BF16)

        def scatter(i, b=b):
            here = pl.ds(pl.multiple_of(i * 512, 512), 512)
            after = pl.ds(pl.multiple_of(i * 512 + 128, 128), 512)
            part = dot_nn(summed[b], pick[b, :, here])
            if b == 0:
                up_part[:, here] = part[0:portion]
                mid_part[:, here] = part[portion : 2 * portion]
                down_part[:, after] = part[2 * portion :]
            else:
                up_part[:, here] += part[0:portion]
                mid_part[:, here] += part[portion : 2 * portion]
                down_part[:, after] += part[2 * portion :]

        loop(cells // 512, scatter, 4)

    for copy in strip_copies:
        copy.wait_recv()
    strip = strips[lev].astype(F32)
    for d in range(1, n_lev):
        strip = strip + strips_in[d - 1].astype(F32)
    up_part[:, cells : cells + 128] = strip[:, 0:128]
    down_part[:, 0:128] = strip[:, 128:256]
    block = strip[:, 256:384].astype(BF16)

    def finish(i):
        start = i * 1024
        here = pl.ds(pl.multiple_of(start, 1024), 1024)
        below = pl.ds(pl.multiple_of(start + 128, 128), 1024)
        total = up_part[:, below] + mid_part[:, here] + down_part[:, here] + dot_nn(block, edge[:, here])
        for n in range(8):
            grad_ref[pl.ds(i * 8 + n, portion, stride=rows), :] = total[:, n * 128 : (n + 1) * 128]

    loop(rows // 8, finish, 4)
    for copy in halo + field_out + sum(relays, []) + sum(shares, []) + back_copies + strip_copies:
        copy.wait_send()


def per_device(
    latent,
    conv_weight,
    mid_weight,
    out_weight,
    vertical_inner_matrix,
    vertical_outer_matrix,
    obs_values,
    obs_weight,
    obs_index,
    obs_count,
):
    chans, rows, cols = latent.shape
    groups, hidden = conv_weight.shape[:2]
    slots, channels = obs_values.shape[2:]
    n_lev = lax.axis_size("lev")
    cells = rows * cols
    portion = chans // n_lev
    width = groups * hidden
    column = vertical_inner_matrix.shape[0]
    conv = conv_weight.transpose(0, 2, 1, 3)
    half = 3 * portion // 2
    vmem = pltpu.VMEM
    dma = pltpu.SemaphoreType.DMA
    operands = [
        latent.reshape(chans * rows, cols),
        conv,
        mid_weight,
        out_weight,
        vertical_inner_matrix,
        vertical_outer_matrix,
        obs_values.reshape(slots, channels),
        obs_weight,
        obs_index.reshape(1, slots),
    ]
    operands = [pltpu.with_memory_space_constraint(x, pltpu.HBM) for x in operands]
    grad = pl.pallas_call(
        kernel,
        out_shape=jax.ShapeDtypeStruct((portion * rows, cols), F32),
        in_specs=[pl.BlockSpec(memory_space=pl.ANY)] * 10,
        out_specs=pl.BlockSpec(memory_space=pltpu.VMEM),
        scratch_shapes=[
            vmem((chans * rows, cols), BF16),
            vmem(conv.shape, BF16),
            vmem(mid_weight.shape, BF16),
            vmem(out_weight.shape, BF16),
            vmem(vertical_inner_matrix.shape, BF16),
            vmem(vertical_outer_matrix.shape, BF16),
            vmem((slots, channels), F32),
            vmem((1, channels), F32),
            vmem((1, slots), jnp.int32),
            vmem((1, 1), jnp.int32),
            pltpu.SMEM((1, slots), jnp.int32),
            vmem((rows, chans, cols), BF16),
            vmem(((rows + 2) * 2 * (cols + 8), 128), F32),
            vmem((slots * 24, 128), F32),
            vmem((9, slots, chans), BF16),
            vmem((3, slots, cells), BF16),
            vmem((128, cells), BF16),
            vmem((6, slots, 128), BF16),
            vmem((2 * rows + 32, chans), F32),
            vmem((2 * rows + 32, chans), F32),
            vmem((2, cols, chans), BF16),
            vmem((cols, chans), BF16),
            vmem((cols, chans), BF16),
            vmem((slots, width), F32),
            vmem((slots, width), BF16),
            vmem((slots, width), F32),
            vmem((slots, width), F32),
            vmem((slots, column), BF16),
            vmem((slots, column), F32),
            vmem((channels, slots), BF16),
            vmem((slots, channels), BF16),
            vmem((slots, channels), BF16),
            vmem((slots, channels), F32),
            vmem((channels, width), BF16),
            vmem((slots, slots), BF16),
            vmem((3, n_lev, 3 * portion, slots), BF16),
            vmem((3, 2, half, slots), BF16),
            vmem((3, 2, half, slots), BF16),
            vmem((3, 4, half, slots), BF16),
            vmem((3, 3 * portion, slots), BF16),
            vmem((portion, cells + cols), F32),
            vmem((portion, cells), F32),
            vmem((portion, cells + cols), F32),
            vmem((2, chans, cols), BF16),
            vmem((2, chans, cols), BF16),
            vmem((128, chans), BF16),
            vmem((128, chans), BF16),
            vmem((n_lev, portion, 3 * cols), BF16),
            vmem((n_lev - 1, portion, 3 * cols), BF16),
            dma((4,)),
            dma((10,)),
            dma((8,)),
            dma((8,)),
            dma((2, n_lev - 1)),
            dma((2, n_lev - 1)),
            dma((3, 2)),
            dma((3, 2)),
            dma((3, 4)),
            dma((3, 4)),
            dma((8,)),
            dma((8,)),
            dma((n_lev - 1,)),
            dma((n_lev - 1,)),
        ],
        compiler_params=pltpu.CompilerParams(
            collective_id=0, has_side_effects=True, vmem_limit_bytes=50 * 1024 * 1024
        ),
        name="slots_step",
    )(*operands, obs_count)
    mine = lax.dynamic_slice_in_dim(latent, lax.axis_index("lev") * portion, portion, 0)
    return mine.astype(F32) + grad.reshape(portion, rows, cols)


def solution(mesh):
    return jax.shard_map(
        per_device,
        mesh=mesh,
        in_specs=(
            P(None, "lat", "lon"),
            P("lev", None, None, None),
            P("lev", None, None),
            P("lev", None, None),
            P(),
            P(),
            P("lat", "lon", None, None),
            P(),
            P("lat", "lon", None),
            P("lat", "lon"),
        ),
        out_specs=P("lev", "lat", "lon"),
        check_vma=False,
    )
```

```python
import functools

import jax
import jax.numpy as jnp
from jax import lax
from jax.experimental import pallas as pl
from jax.experimental.pallas import tpu as pltpu
from jax.sharding import PartitionSpec as P

KAPPA = 0.7978845608028654
CUBIC = 0.044715
F32 = jnp.float32
BF16 = jnp.bfloat16
MESH = pl.DeviceIdType.MESH


def gelu_slope(pre):
    tanh_v = jnp.tanh(KAPPA * (pre + CUBIC * pre * pre * pre))
    half = 0.5 * (1.0 + tanh_v)
    value = pre * half
    slope = half + 0.5 * pre * (1.0 - tanh_v * tanh_v) * (KAPPA + 3.0 * KAPPA * CUBIC * pre * pre)
    return (value, slope)


def dot_nn(x, y):
    return lax.dot_general(x, y, (((1,), (0,)), ((), ())), preferred_element_type=F32)


def dot_nt(x, y):
    return lax.dot_general(x, y, (((1,), (1,)), ((), ())), preferred_element_type=F32)


def iota(shape, dim):
    return lax.broadcasted_iota(jnp.int32, shape, dim)


def loop(count, body, unroll=1):
    def step(i, carry):
        body(i)
        return carry

    lax.fori_loop(0, count, step, 0, unroll=unroll)


def kernel(
    latent_hbm,
    conv_hbm,
    mid_hbm,
    out_hbm,
    inner_hbm,
    outer_hbm,
    obs_hbm,
    weight_hbm,
    index_hbm,
    count_hbm,
    grad_ref,
    raw,
    conv,
    mid_ref,
    out_ref,
    inner,
    outer,
    obs,
    weight_ref,
    index_ref,
    count_ref,
    index_smem,
    slab,
    table,
    patch,
    patches,
    conv_t,
    pick,
    edge,
    side_pick,
    side_send,
    side,
    row_out,
    north,
    south,
    pre,
    act,
    slope_one,
    slope_two,
    act_col,
    slope_col,
    fields,
    fields_t,
    cast,
    misfit,
    out_pad,
    eye,
    taps,
    relay_in,
    relay_out,
    taps_in,
    summed,
    up_part,
    mid_part,
    down_part,
    row_send,
    row_in,
    side_out,
    side_in,
    strips,
    strips_in,
    first_sem,
    load_sem,
    halo_send,
    halo_recv,
    field_send,
    field_recv,
    relay_send,
    relay_recv,
    taps_send,
    taps_recv,
    back_send,
    back_recv,
    strip_send,
    strip_recv,
):
    lev, lat, lon = lax.axis_index("lev"), lax.axis_index("lat"), lax.axis_index("lon")
    n_lev, n_lat, n_lon = lax.axis_size("lev"), lax.axis_size("lat"), lax.axis_size("lon")
    slots = pick.shape[1]
    cells = pick.shape[2]
    chans = slab.shape[1]
    rows = cells // 128
    groups, hidden = mid_ref.shape[:2]
    levels = out_ref.shape[1]
    own = groups * levels
    portion = chans // n_lev
    pitch = table.shape[0] // (rows + 2)

    pairs = (
        (index_hbm, index_smem),
        (index_hbm, index_ref),
        (count_hbm, count_ref),
        (conv_hbm, conv),
        (mid_hbm, mid_ref),
        (out_hbm, out_ref),
        (inner_hbm, inner),
        (outer_hbm, outer),
        (obs_hbm, obs),
        (weight_hbm, weight_ref.at[0]),
    )
    loads = [pltpu.make_async_copy(src, dst, load_sem.at[n]) for n, (src, dst) in enumerate(pairs)]
    pieces = 4
    first_loads = []
    for n in range(pieces):
        part = pl.ds(n * (raw.shape[0] // pieces), raw.shape[0] // pieces)
        first_loads.append(pltpu.make_async_copy(latent_hbm.at[part], raw.at[part], first_sem.at[n]))
    for load in first_loads + loads[:3]:
        load.start()

    def tile(dlat, dlon):
        return (lev, lax.rem(lat + dlat + n_lat, n_lat), lax.rem(lon + dlon + n_lon, n_lon))

    def peer(d):
        return (lax.rem(lev + d, n_lev), lat, lon)

    around = [(x, y) for x in (-1, 0, 1) for y in (-1, 0, 1) if (x, y) != (0, 0)]
    barrier = pltpu.get_barrier_semaphore()
    for x, y in around:
        pl.semaphore_signal(barrier, inc=1, device_id=tile(x, y), device_id_type=MESH)
    for d in range(1, n_lev):
        pl.semaphore_signal(barrier, inc=1, device_id=peer(d), device_id_type=MESH)

    square = iota((slots, slots), 0) == iota((slots, slots), 1)
    eye[...] = jnp.where(square, 1.0, 0.0).astype(BF16)
    order = iota((slots, 1), 0)
    order = lax.bitwise_and(order, 7) * rows + lax.shift_right_logical(order, 3)
    order = jnp.where(iota((slots, slots), 1) == order, 1.0, 0.0).astype(BF16)

    def relayout(i):
        start = i * 16 * rows
        parts = [
            dot_nn(order, raw[pl.ds(start + h * 8 * rows, 8 * rows), :]).reshape(rows, 8, 128) for h in range(2)
        ]
        slab[:, pl.ds(i * 16, 16), :] = jnp.concatenate(parts, axis=1).astype(BF16)

    for n, load in enumerate(first_loads):
        load.wait()
        if n == pieces - 1:
            for later in loads[3:]:
                later.start()
        for i in range(chans // 16 // pieces):
            relayout(n * (chans // 16 // pieces) + i)

    def put_row(line, value):
        start = line * pitch + 2
        table[pl.ds(start, 128, stride=2), :] = value[:, 0:128]
        table[pl.ds(start + 1, 128, stride=2), :] = value[:, 128:256]

    def table_row(r):
        put_row(r + 1, dot_nt(eye[0:128, 0:128], slab[r]))

    loop(rows, table_row, rows)

    for n, line in ((0, 0), (1, rows - 1)):
        row_out[n] = dot_nt(eye[0:128, 0:128], slab[line]).astype(BF16)
    for h in range(2):
        part = slice(h * 128, (h + 1) * 128)
        side_send[0:rows, part] = table[pl.ds(pitch + 256 + h, rows, stride=pitch), :]
        side_send[rows : 2 * rows, part] = table[pl.ds(pitch + 2 + h, rows, stride=pitch), :]
        for n, at in enumerate(
            (rows * pitch + 256, rows * pitch + 2, pitch + 256, pitch + 2)
        ):
            first = 2 * rows + 8 * n
            side_send[first : first + 8, part] = jnp.broadcast_to(table[at + h : at + h + 1, :], (8, 128))

    pl.semaphore_wait(barrier, len(around) + n_lev - 1)
    halo = [(row_out.at[0], south, (-1, 0)), (row_out.at[1], north, (1, 0))]
    sides = [(0, 32, (0, 1)), (32, 32, (0, -1)), (64, 8, (1, 1)), (72, 8, (1, -1)), (80, 8, (-1, 1)), (88, 8, (-1, -1))]
    for first, length, where in sides:
        halo.append((side_send.at[pl.ds(first, length)], side.at[pl.ds(first, length)], where))
    halo = [
        pltpu.make_async_remote_copy(
            src_ref=src,
            dst_ref=dst,
            send_sem=halo_send.at[n],
            recv_sem=halo_recv.at[n],
            device_id=tile(*where),
            device_id_type=MESH,
        )
        for n, (src, dst, where) in enumerate(halo)
    ]
    for copy in halo:
        copy.start()

    out_pad[...] = jnp.zeros(out_pad.shape, BF16)
    for load in loads[:6]:
        load.wait()
    for g in range(groups):
        part = pl.ds(pl.multiple_of(lev * own + g * levels, 16), levels)
        out_pad[part, g * hidden : (g + 1) * hidden] = out_ref[g]

    for copy in halo:
        copy.wait_recv()
    has_north = jnp.where(lat > 0, 1.0, 0.0)
    has_south = jnp.where(lat < n_lat - 1, 1.0, 0.0)
    put_row(0, north[...].astype(F32) * has_north)
    put_row(rows + 1, south[...].astype(F32) * has_south)
    for h in range(2):
        part = slice(h * 128, (h + 1) * 128)
        table[pl.ds(pitch + h, rows, stride=pitch), :] = side[0:rows, part]
        table[pl.ds(pitch + 258 + h, rows, stride=pitch), :] = side[rows : 2 * rows, part]
        low = (rows + 1) * pitch
        for n, (at, scale) in enumerate(((0, has_north), (258, has_north), (low, has_south), (low + 258, has_south))):
            first = 2 * rows + 8 * n
            table[at + h : at + h + 1, :] = side[first : first + 1, part] * scale

    def slot_patch(k):
        where = index_smem[0, k]
        start = lax.shift_right_logical(where, 7) * pitch + lax.bitwise_and(where, 127) * 2
        for a in range(3):
            patch[pl.ds(pl.multiple_of(k * 24 + a * 8, 8), 8), :] = table[pl.ds(start + a * pitch, 8), :]

    loop(slots, slot_patch, 8)

    step = 32
    sets = 2
    per_set = groups // sets

    def field_copy(p, d, source):
        part = pl.ds(pl.multiple_of(source * own + p * (own // sets), 16), own // sets)
        return pltpu.make_async_remote_copy(
            src_ref=fields.at[part],
            dst_ref=fields.at[part],
            send_sem=field_send.at[p, d - 1],
            recv_sem=field_recv.at[p, d - 1],
            device_id=peer(d),
            device_id_type=MESH,
        )

    field_out = []
    for p in range(sets):
        span = slice(p * per_set * hidden, (p + 1) * per_set * hidden)
        first = p * per_set
        total = None
        for t in range(9):
            if p == 0:
                parts = [patch[pl.ds((t // 3) * 8 + (t % 3) * 2 + h, slots, stride=24), :] for h in range(2)]
                patches[t] = jnp.concatenate(parts, axis=1).astype(BF16)
            kernel_t = conv[first : first + per_set, t].reshape(per_set * hidden, chans)
            part = dot_nt(patches[t], kernel_t)
            total = part if total is None else total + part
        pre[:, span] = total

        def gelu_one(i, span=span):
            part = pl.ds(pl.multiple_of(i * step, step), step)
            value, slope = gelu_slope(pre[part, span])
            act[part, span] = value.astype(BF16)
            slope_one[part, span] = slope

        def gelu_two(i, span=span):
            part = pl.ds(pl.multiple_of(i * step, step), step)
            value, slope = gelu_slope(pre[part, span])
            act[part, span] = value.astype(BF16)
            slope_two[part, span] = slope

        loop(slots // step, gelu_one, 4)
        for g in range(first, first + per_set):
            part = slice(g * hidden, (g + 1) * hidden)
            pre[:, part] = dot_nt(act[:, part], mid_ref[g])
        loop(slots // step, gelu_two, 4)
        for g in range(first, first + per_set):
            part = slice(g * hidden, (g + 1) * hidden)
            fields[pl.ds(pl.multiple_of(lev * own + g * levels, 16), levels), :] = dot_nt(
                out_ref[g], act[:, part]
            ).astype(BF16)
        for d in (1, 3) if p == 0 else (2, 1, 3):
            copy = field_copy(p, d, lev)
            copy.start()
            field_out.append(copy)

    spread = jnp.broadcast_to(index_ref[...].astype(F32), (slots, slots))
    index = jnp.sum(jnp.where(square, spread, 0.0), axis=1, keepdims=True).astype(jnp.int32)
    row = lax.shift_right_logical(index, 7)
    col = lax.bitwise_and(index, 127)
    live = jnp.where(iota((slots, 1), 0) < count_ref[...], 1.0, 0.0)
    row_wide = jnp.broadcast_to(row, (slots, 128))
    lane_wide = iota((slots, 128), 1)
    last = (rows - 1) * 128
    for b in range(3):
        cast[:, b * 128 : (b + 1) * 128] = jnp.where(lane_wide == col + (b - 1), 1.0, 0.0).astype(BF16)

    def pick_row(r):
        hit = row_wide == r
        for b in range(3):
            column_b = cast[:, b * 128 : (b + 1) * 128].astype(F32)
            pick[b, :, pl.ds(pl.multiple_of(r * 128, 128), 128)] = jnp.where(hit, column_b, 0.0).astype(BF16)

    loop(rows, pick_row)

    for a in range(3):
        line = row + (a - 1)
        above = (line < 0) & (lat > 0)
        below = (line >= rows) & (lat < n_lat - 1)
        inside = (line >= 0) & (line < rows)
        for n, b in enumerate((0, 2)):
            first, upper, lower = (0, 64, 96) if b == 0 else (32, 80, 112)
            out = (col == 0) if b == 0 else (col == 127)
            target = jnp.where(inside, first + line, jnp.where(above, upper, jnp.where(below, lower, -1)))
            target = jnp.where(out, target, -1)
            side_pick[n * 3 + a] = jnp.where(lane_wide == target, 1.0, 0.0).astype(BF16)

    j = iota((128, 1), 0)
    spot = jnp.where(j < 32, j * 128 + 127, (j - 32) * 128)
    for at, cell in ((64, last + 127), (80, last), (96, 127), (112, 0)):
        spot = jnp.where(j == at, cell, jnp.where(j > at, -1, spot))

    def edge_block(i):
        start = pl.multiple_of(i * 512, 512)
        edge[:, pl.ds(start, 512)] = jnp.where(iota((128, 512), 1) + start == spot, 1.0, 0.0).astype(BF16)

    loop(cells // 512, edge_block)

    field_copy(0, 3, lax.rem(lev + 1, n_lev)).wait_recv()
    part = pl.ds(pl.multiple_of(lax.rem(lev + 1, n_lev) * own, 16), own // sets)
    onward = pltpu.make_async_remote_copy(
        src_ref=fields.at[part],
        dst_ref=fields.at[part],
        send_sem=field_send.at[0, 1],
        recv_sem=field_recv.at[0, 1],
        device_id=peer(3),
        device_id_type=MESH,
    )
    onward.start()
    field_out.append(onward)

    def turn(t):
        conv_t[t] = dot_nt(eye[...], conv[:, t].reshape(groups * hidden, chans)).astype(BF16)

    loop(9, turn, 3)
    for load in loads[6:]:
        load.wait()
    for p in range(sets):
        for d in range(1, n_lev):
            if (p, d) != (0, 3):
                field_copy(p, d, lax.rem(lev + n_lev - d, n_lev)).wait_recv()

    blocks = fields.shape[0] // 256
    for i in range(blocks):
        part = slice(i * 256, (i + 1) * 256)
        fields_t[:, part] = dot_nt(eye[...], fields[part, :]).astype(BF16)

    def column(i):
        part = pl.ds(pl.multiple_of(i * 256, 256), 256)
        value, slope = gelu_slope(dot_nt(fields_t[...], inner[part, :]))
        slope_col[:, part] = slope
        act_col[:, part] = value.astype(BF16)

    loop(inner.shape[0] // 256, column, 4)

    def compare(i):
        part = pl.ds(pl.multiple_of(i * 256, 256), 256)
        forecast = fields_t[:, part].astype(F32) + dot_nt(act_col[...], outer[part, :])
        value = (forecast - obs[:, part]) * live * weight_ref[:, part]
        misfit[:, part] = value
        cast[:, part] = value.astype(BF16)

    loop(blocks, compare, 3)

    def column_back(i):
        part = pl.ds(pl.multiple_of(i * 256, 256), 256)
        act_col[:, part] = (dot_nn(cast[...], outer[:, part]) * slope_col[:, part]).astype(BF16)

    loop(inner.shape[0] // 256, column_back, 4)

    def fields_back(i):
        part = pl.ds(pl.multiple_of(i * 256, 256), 256)
        fields_t[:, part] = (misfit[:, part] + dot_nn(act_col[...], inner[:, part])).astype(BF16)

    loop(blocks, fields_back, 3)
    act[...] = (dot_nn(fields_t[...], out_pad[...]) * slope_two[...]).astype(BF16)
    for g in range(groups):
        part = slice(g * hidden, (g + 1) * hidden)
        slope_one[:, part] = slope_one[:, part] * dot_nn(act[:, part], mid_ref[g])
    act[...] = slope_one[...].astype(BF16)

    above_lev, below_lev, across = lax.rem(lev + 1, n_lev), lax.rem(lev + 3, n_lev), lax.rem(lev + 2, n_lev)
    half = 3 * portion // 2
    low_half, high_half = pl.ds(0, half), pl.ds(half, half)

    def send(src, dst, sems, device):
        return pltpu.make_async_remote_copy(
            src_ref=src,
            dst_ref=dst,
            send_sem=sems[0],
            recv_sem=sems[1],
            device_id=(device, lat, lon),
            device_id_type=MESH,
        )

    def relay_copies(b):
        return [
            send(taps.at[b, across, low_half], relay_in.at[b, 0], (relay_send.at[b, 0], relay_recv.at[b, 0]), above_lev),
            send(taps.at[b, across, high_half], relay_in.at[b, 1], (relay_send.at[b, 1], relay_recv.at[b, 1]), below_lev),
        ]

    def taps_copies(b):
        sources = (
            (relay_out.at[b, 0], above_lev),
            (taps.at[b, above_lev, high_half], above_lev),
            (taps.at[b, below_lev, low_half], below_lev),
            (relay_out.at[b, 1], below_lev),
        )
        return [
            send(src, taps_in.at[b, n], (taps_send.at[b, n], taps_recv.at[b, n]), device)
            for n, (src, device) in enumerate(sources)
        ]

    relays = [relay_copies(b) for b in range(3)]
    shares = [taps_copies(b) for b in range(3)]
    for b in range(3):

        def back(a, b=b):
            part = dot_nt(conv_t[a * 3 + b], act[...]).astype(BF16)
            for d in range(n_lev):
                taps[b, d, pl.ds(pl.multiple_of(a * portion, 16), portion), :] = part[
                    d * portion : (d + 1) * portion
                ]

        loop(3, back, 3)
        for copy in relays[b]:
            copy.start()
    for b in range(3):
        shares[b][1].start()
        shares[b][2].start()

    upper = jnp.zeros((chans, 128), F32)
    lower = jnp.zeros((chans, 128), F32)
    beside = jnp.zeros((chans, 128), F32)
    for b in range(3):
        tap_b = [taps[b, :, a * portion : (a + 1) * portion, :].reshape(chans, slots) for a in range(3)]
        upper = upper + dot_nn(tap_b[0], pick[b, :, 0:128])
        lower = lower + dot_nn(tap_b[2], pick[b, :, last : last + 128])
        if b != 1:
            for a in range(3):
                beside = beside + dot_nn(tap_b[a], side_pick[(b // 2) * 3 + a])
    row_send[0] = (upper * has_north).astype(BF16)
    row_send[1] = (lower * has_south).astype(BF16)
    side_out[...] = dot_nt(eye[0:128, 0:128], beside.astype(BF16)).astype(BF16)
    back_copies = [(row_send.at[0], row_in.at[0], (-1, 0)), (row_send.at[1], row_in.at[1], (1, 0))]
    back_sides = [(0, 32, (0, -1)), (32, 32, (0, 1)), (64, 16, (-1, -1)), (80, 16, (-1, 1)), (96, 16, (1, -1)), (112, 16, (1, 1))]
    for first, length, where in back_sides:
        back_copies.append((side_out.at[pl.ds(first, length)], side_in.at[pl.ds(first, length)], where))
    back_copies = [
        pltpu.make_async_remote_copy(
            src_ref=src,
            dst_ref=dst,
            send_sem=back_send.at[n],
            recv_sem=back_recv.at[n],
            device_id=tile(*where),
            device_id_type=MESH,
        )
        for n, (src, dst, where) in enumerate(back_copies)
    ]
    for copy in back_copies:
        copy.start()

    for b in range(3):
        for copy in relays[b]:
            copy.wait_recv()
        for n, (device, part) in enumerate(((above_lev, low_half), (below_lev, high_half))):
            mine = taps[b, device, part, :].astype(F32)
            relay_out[b, n] = (mine + relay_in[b, n].astype(F32)).astype(BF16)
        shares[b][0].start()
        shares[b][3].start()

    for copy in back_copies:
        copy.wait_recv()
    for n in range(2):
        strips[:, :, n * 128 : (n + 1) * 128] = row_in[n].reshape(n_lev, portion, 128)
    strips[:, :, 256:384] = dot_nt(eye[...], side_in[...]).astype(BF16).reshape(n_lev, portion, 128)
    strip_copies = [
        send(strips.at[lax.rem(lev + d, n_lev)], strips_in.at[d - 1], (strip_send.at[d - 1], strip_recv.at[d - 1]), lax.rem(lev + d, n_lev))
        for d in (2, 1, 3)
    ]
    for copy in strip_copies:
        copy.start()

    for b in range(3):
        for copy in shares[b]:
            copy.wait_recv()
        halves = []
        for part, first, second in ((low_half, 0, 2), (high_half, 1, 3)):
            total = taps[b, lev, part, :].astype(F32)
            halves.append(total + taps_in[b, first].astype(F32) + taps_in[b, second].astype(F32))
        summed[b] = jnp.concatenate(halves, axis=0).astype(BF16)

        def scatter(i, b=b):
            here = pl.ds(pl.multiple_of(i * 512, 512), 512)
            after = pl.ds(pl.multiple_of(i * 512 + 128, 128), 512)
            part = dot_nn(summed[b], pick[b, :, here])
            if b == 0:
                up_part[:, here] = part[0:portion]
                mid_part[:, here] = part[portion : 2 * portion]
                down_part[:, after] = part[2 * portion :]
            else:
                up_part[:, here] += part[0:portion]
                mid_part[:, here] += part[portion : 2 * portion]
                down_part[:, after] += part[2 * portion :]

        loop(cells // 512, scatter, 4)

    for copy in strip_copies:
        copy.wait_recv()
    strip = strips[lev].astype(F32)
    for d in range(1, n_lev):
        strip = strip + strips_in[d - 1].astype(F32)
    up_part[:, cells : cells + 128] = strip[:, 0:128]
    down_part[:, 0:128] = strip[:, 128:256]
    block = strip[:, 256:384].astype(BF16)

    def finish(i):
        start = i * 1024
        here = pl.ds(pl.multiple_of(start, 1024), 1024)
        below = pl.ds(pl.multiple_of(start + 128, 128), 1024)
        total = up_part[:, below] + mid_part[:, here] + down_part[:, here] + dot_nn(block, edge[:, here])
        for n in range(8):
            grad_ref[pl.ds(i * 8 + n, portion, stride=rows), :] = total[:, n * 128 : (n + 1) * 128]

    loop(rows // 8, finish, 4)
    for copy in halo + field_out + sum(relays, []) + sum(shares, []) + back_copies + strip_copies:
        copy.wait_send()


def per_device(
    latent,
    conv_weight,
    mid_weight,
    out_weight,
    vertical_inner_matrix,
    vertical_outer_matrix,
    obs_values,
    obs_weight,
    obs_index,
    obs_count,
):
    chans, rows, cols = latent.shape
    groups, hidden = conv_weight.shape[:2]
    slots, channels = obs_values.shape[2:]
    n_lev = lax.axis_size("lev")
    cells = rows * cols
    portion = chans // n_lev
    width = groups * hidden
    column = vertical_inner_matrix.shape[0]
    conv = conv_weight.transpose(0, 2, 1, 3)
    half = 3 * portion // 2
    vmem = pltpu.VMEM
    dma = pltpu.SemaphoreType.DMA
    operands = [
        latent.reshape(chans * rows, cols),
        conv,
        mid_weight,
        out_weight,
        vertical_inner_matrix,
        vertical_outer_matrix,
        obs_values.reshape(slots, channels),
        obs_weight,
        obs_index.reshape(1, slots),
    ]
    operands = [pltpu.with_memory_space_constraint(x, pltpu.HBM) for x in operands]
    grad = pl.pallas_call(
        kernel,
        out_shape=jax.ShapeDtypeStruct((portion * rows, cols), F32),
        in_specs=[pl.BlockSpec(memory_space=pl.ANY)] * 10,
        out_specs=pl.BlockSpec(memory_space=pltpu.VMEM),
        scratch_shapes=[
            vmem((chans * rows, cols), BF16),
            vmem(conv.shape, BF16),
            vmem(mid_weight.shape, BF16),
            vmem(out_weight.shape, BF16),
            vmem(vertical_inner_matrix.shape, BF16),
            vmem(vertical_outer_matrix.shape, BF16),
            vmem((slots, channels), F32),
            vmem((1, channels), F32),
            vmem((1, slots), jnp.int32),
            vmem((1, 1), jnp.int32),
            pltpu.SMEM((1, slots), jnp.int32),
            vmem((rows, chans, cols), BF16),
            vmem(((rows + 2) * 2 * (cols + 8), 128), F32),
            vmem((slots * 24, 128), F32),
            vmem((9, slots, chans), BF16),
            vmem((9, chans, width), BF16),
            vmem((3, slots, cells), BF16),
            vmem((128, cells), BF16),
            vmem((6, slots, 128), BF16),
            vmem((2 * rows + 32, chans), F32),
            vmem((2 * rows + 32, chans), F32),
            vmem((2, cols, chans), BF16),
            vmem((cols, chans), BF16),
            vmem((cols, chans), BF16),
            vmem((slots, width), F32),
            vmem((slots, width), BF16),
            vmem((slots, width), F32),
            vmem((slots, width), F32),
            vmem((slots, column), BF16),
            vmem((slots, column), F32),
            vmem((channels, slots), BF16),
            vmem((slots, channels), BF16),
            vmem((slots, channels), BF16),
            vmem((slots, channels), F32),
            vmem((channels, width), BF16),
            vmem((slots, slots), BF16),
            vmem((3, n_lev, 3 * portion, slots), BF16),
            vmem((3, 2, half, slots), BF16),
            vmem((3, 2, half, slots), BF16),
            vmem((3, 4, half, slots), BF16),
            vmem((3, 3 * portion, slots), BF16),
            vmem((portion, cells + cols), F32),
            vmem((portion, cells), F32),
            vmem((portion, cells + cols), F32),
            vmem((2, chans, cols), BF16),
            vmem((2, chans, cols), BF16),
            vmem((128, chans), BF16),
            vmem((128, chans), BF16),
            vmem((n_lev, portion, 3 * cols), BF16),
            vmem((n_lev - 1, portion, 3 * cols), BF16),
            dma((4,)),
            dma((10,)),
            dma((8,)),
            dma((8,)),
            dma((2, n_lev - 1)),
            dma((2, n_lev - 1)),
            dma((3, 2)),
            dma((3, 2)),
            dma((3, 4)),
            dma((3, 4)),
            dma((8,)),
            dma((8,)),
            dma((n_lev - 1,)),
            dma((n_lev - 1,)),
        ],
        compiler_params=pltpu.CompilerParams(
            collective_id=0, has_side_effects=True, vmem_limit_bytes=50 * 1024 * 1024
        ),
        name="slots_step",
    )(*operands, obs_count)
    mine = lax.dynamic_slice_in_dim(latent, lax.axis_index("lev") * portion, portion, 0)
    return mine.astype(F32) + grad.reshape(portion, rows, cols)


def solution(mesh):
    return jax.shard_map(
        per_device,
        mesh=mesh,
        in_specs=(
            P(None, "lat", "lon"),
            P("lev", None, None, None),
            P("lev", None, None),
            P("lev", None, None),
            P(),
            P(),
            P("lat", "lon", None, None),
            P(),
            P("lat", "lon", None),
            P("lat", "lon"),
        ),
        out_specs=P("lev", "lat", "lon"),
        check_vma=False,
    )
```

```python
import functools

import jax
import jax.numpy as jnp
from jax import lax
from jax.experimental import pallas as pl
from jax.experimental.pallas import tpu as pltpu
from jax.sharding import PartitionSpec as P

KAPPA = 0.7978845608028654
CUBIC = 0.044715
F32 = jnp.float32
BF16 = jnp.bfloat16
MESH = pl.DeviceIdType.MESH


def gelu_slope(pre):
    tanh_v = jnp.tanh(KAPPA * (pre + CUBIC * pre * pre * pre))
    half = 0.5 * (1.0 + tanh_v)
    value = pre * half
    slope = half + 0.5 * pre * (1.0 - tanh_v * tanh_v) * (KAPPA + 3.0 * KAPPA * CUBIC * pre * pre)
    return (value, slope)


def dot_nn(x, y):
    return lax.dot_general(x, y, (((1,), (0,)), ((), ())), preferred_element_type=F32)


def dot_nt(x, y):
    return lax.dot_general(x, y, (((1,), (1,)), ((), ())), preferred_element_type=F32)


def iota(shape, dim):
    return lax.broadcasted_iota(jnp.int32, shape, dim)


def loop(count, body, unroll=1):
    def step(i, carry):
        body(i)
        return carry

    lax.fori_loop(0, count, step, 0, unroll=unroll)


def kernel(
    latent_hbm,
    conv_hbm,
    mid_hbm,
    out_hbm,
    inner_hbm,
    outer_hbm,
    obs_hbm,
    weight_hbm,
    index_hbm,
    count_hbm,
    grad_ref,
    raw,
    conv,
    mid_ref,
    out_ref,
    inner,
    outer,
    obs,
    weight_ref,
    index_ref,
    count_ref,
    index_smem,
    slab,
    table,
    patch,
    patches,
    conv_t,
    pick,
    edge,
    side_pick,
    side_send,
    side,
    row_out,
    north,
    south,
    pre,
    act,
    slope_one,
    slope_two,
    act_col,
    slope_col,
    fields,
    fields_t,
    cast,
    misfit,
    out_pad,
    eye,
    taps,
    relay_in,
    relay_out,
    taps_in,
    summed,
    up_part,
    mid_part,
    down_part,
    row_send,
    row_in,
    side_out,
    side_in,
    strips,
    strips_in,
    first_sem,
    load_sem,
    halo_send,
    halo_recv,
    field_send,
    field_recv,
    relay_send,
    relay_recv,
    taps_send,
    taps_recv,
    back_send,
    back_recv,
    strip_send,
    strip_recv,
):
    lev, lat, lon = lax.axis_index("lev"), lax.axis_index("lat"), lax.axis_index("lon")
    n_lev, n_lat, n_lon = lax.axis_size("lev"), lax.axis_size("lat"), lax.axis_size("lon")
    slots = pick.shape[1]
    cells = pick.shape[2]
    chans = slab.shape[1]
    rows = cells // 128
    groups, hidden = mid_ref.shape[:2]
    levels = out_ref.shape[1]
    own = groups * levels
    portion = chans // n_lev
    pitch = table.shape[0] // (rows + 2)

    pairs = (
        (index_hbm, index_smem),
        (index_hbm, index_ref),
        (count_hbm, count_ref),
        (conv_hbm, conv),
        (mid_hbm, mid_ref),
        (out_hbm, out_ref),
        (inner_hbm, inner),
        (outer_hbm, outer),
        (obs_hbm, obs),
        (weight_hbm, weight_ref.at[0]),
    )
    loads = [pltpu.make_async_copy(src, dst, load_sem.at[n]) for n, (src, dst) in enumerate(pairs)]
    pieces = 4
    first_loads = []
    for n in range(pieces):
        part = pl.ds(n * (raw.shape[0] // pieces), raw.shape[0] // pieces)
        first_loads.append(pltpu.make_async_copy(latent_hbm.at[part], raw.at[part], first_sem.at[n]))
    for load in first_loads + loads[:3]:
        load.start()

    def tile(dlat, dlon):
        return (lev, lax.rem(lat + dlat + n_lat, n_lat), lax.rem(lon + dlon + n_lon, n_lon))

    def peer(d):
        return (lax.rem(lev + d, n_lev), lat, lon)

    around = [(x, y) for x in (-1, 0, 1) for y in (-1, 0, 1) if (x, y) != (0, 0)]
    barrier = pltpu.get_barrier_semaphore()
    for x, y in around:
        pl.semaphore_signal(barrier, inc=1, device_id=tile(x, y), device_id_type=MESH)
    for d in range(1, n_lev):
        pl.semaphore_signal(barrier, inc=1, device_id=peer(d), device_id_type=MESH)

    square = iota((slots, slots), 0) == iota((slots, slots), 1)
    eye[...] = jnp.where(square, 1.0, 0.0).astype(BF16)
    order = iota((slots, 1), 0)
    order = lax.bitwise_and(order, 7) * rows + lax.shift_right_logical(order, 3)
    order = jnp.where(iota((slots, slots), 1) == order, 1.0, 0.0).astype(BF16)

    def relayout(i):
        start = i * 16 * rows
        parts = [
            dot_nn(order, raw[pl.ds(start + h * 8 * rows, 8 * rows), :]).reshape(rows, 8, 128) for h in range(2)
        ]
        slab[:, pl.ds(i * 16, 16), :] = jnp.concatenate(parts, axis=1).astype(BF16)

    for n, load in enumerate(first_loads):
        load.wait()
        if n == pieces - 1:
            for later in loads[3:]:
                later.start()
        for i in range(chans // 16 // pieces):
            relayout(n * (chans // 16 // pieces) + i)

    def put_row(line, value):
        start = line * pitch + 2
        table[pl.ds(start, 128, stride=2), :] = value[:, 0:128]
        table[pl.ds(start + 1, 128, stride=2), :] = value[:, 128:256]

    def table_row(r):
        put_row(r + 1, dot_nt(eye[0:128, 0:128], slab[r]))

    loop(rows, table_row, rows)

    for n, line in ((0, 0), (1, rows - 1)):
        row_out[n] = dot_nt(eye[0:128, 0:128], slab[line]).astype(BF16)
    for h in range(2):
        part = slice(h * 128, (h + 1) * 128)
        side_send[0:rows, part] = table[pl.ds(pitch + 256 + h, rows, stride=pitch), :]
        side_send[rows : 2 * rows, part] = table[pl.ds(pitch + 2 + h, rows, stride=pitch), :]
        for n, at in enumerate(
            (rows * pitch + 256, rows * pitch + 2, pitch + 256, pitch + 2)
        ):
            first = 2 * rows + 8 * n
            side_send[first : first + 8, part] = jnp.broadcast_to(table[at + h : at + h + 1, :], (8, 128))

    pl.semaphore_wait(barrier, len(around) + n_lev - 1)
    halo = [(row_out.at[0], south, (-1, 0)), (row_out.at[1], north, (1, 0))]
    sides = [(0, 32, (0, 1)), (32, 32, (0, -1)), (64, 8, (1, 1)), (72, 8, (1, -1)), (80, 8, (-1, 1)), (88, 8, (-1, -1))]
    for first, length, where in sides:
        halo.append((side_send.at[pl.ds(first, length)], side.at[pl.ds(first, length)], where))
    halo = [
        pltpu.make_async_remote_copy(
            src_ref=src,
            dst_ref=dst,
            send_sem=halo_send.at[n],
            recv_sem=halo_recv.at[n],
            device_id=tile(*where),
            device_id_type=MESH,
        )
        for n, (src, dst, where) in enumerate(halo)
    ]
    for copy in halo:
        copy.start()

    out_pad[...] = jnp.zeros(out_pad.shape, BF16)
    for load in loads[:6]:
        load.wait()
    for g in range(groups):
        part = pl.ds(pl.multiple_of(lev * own + g * levels, 16), levels)
        out_pad[part, g * hidden : (g + 1) * hidden] = out_ref[g]

    for copy in halo:
        copy.wait_recv()
    has_north = jnp.where(lat > 0, 1.0, 0.0)
    has_south = jnp.where(lat < n_lat - 1, 1.0, 0.0)
    put_row(0, north[...].astype(F32) * has_north)
    put_row(rows + 1, south[...].astype(F32) * has_south)
    for h in range(2):
        part = slice(h * 128, (h + 1) * 128)
        table[pl.ds(pitch + h, rows, stride=pitch), :] = side[0:rows, part]
        table[pl.ds(pitch + 258 + h, rows, stride=pitch), :] = side[rows : 2 * rows, part]
        low = (rows + 1) * pitch
        for n, (at, scale) in enumerate(((0, has_north), (258, has_north), (low, has_south), (low + 258, has_south))):
            first = 2 * rows + 8 * n
            table[at + h : at + h + 1, :] = side[first : first + 1, part] * scale

    def slot_patch(k):
        where = index_smem[0, k]
        start = lax.shift_right_logical(where, 7) * pitch + lax.bitwise_and(where, 127) * 2
        for a in range(3):
            patch[pl.ds(pl.multiple_of(k * 24 + a * 8, 8), 8), :] = table[pl.ds(start + a * pitch, 8), :]

    loop(slots, slot_patch, 32)

    step = 32
    sets = 2
    per_set = groups // sets

    def field_copy(p, d, source):
        part = pl.ds(pl.multiple_of(source * own + p * (own // sets), 16), own // sets)
        return pltpu.make_async_remote_copy(
            src_ref=fields.at[part],
            dst_ref=fields.at[part],
            send_sem=field_send.at[p, d - 1],
            recv_sem=field_recv.at[p, d - 1],
            device_id=peer(d),
            device_id_type=MESH,
        )

    field_out = []
    for p in range(sets):
        span = slice(p * per_set * hidden, (p + 1) * per_set * hidden)
        first = p * per_set
        total = None
        for t in range(9):
            if p == 0:
                parts = [patch[pl.ds((t // 3) * 8 + (t % 3) * 2 + h, slots, stride=24), :] for h in range(2)]
                patches[t] = jnp.concatenate(parts, axis=1).astype(BF16)
            kernel_t = conv[first : first + per_set, t].reshape(per_set * hidden, chans)
            part = dot_nt(patches[t], kernel_t)
            total = part if total is None else total + part
        pre[:, span] = total

        def gelu_one(i, span=span):
            part = pl.ds(pl.multiple_of(i * step, step), step)
            value, slope = gelu_slope(pre[part, span])
            act[part, span] = value.astype(BF16)
            slope_one[part, span] = slope

        def gelu_two(i, span=span):
            part = pl.ds(pl.multiple_of(i * step, step), step)
            value, slope = gelu_slope(pre[part, span])
            act[part, span] = value.astype(BF16)
            slope_two[part, span] = slope

        loop(slots // step, gelu_one, 8)
        for g in range(first, first + per_set):
            part = slice(g * hidden, (g + 1) * hidden)
            pre[:, part] = dot_nt(act[:, part], mid_ref[g])
        loop(slots // step, gelu_two, 8)
        for g in range(first, first + per_set):
            part = slice(g * hidden, (g + 1) * hidden)
            fields[pl.ds(pl.multiple_of(lev * own + g * levels, 16), levels), :] = dot_nt(
                out_ref[g], act[:, part]
            ).astype(BF16)
        for d in (1, 3) if p == 0 else (2, 1, 3):
            copy = field_copy(p, d, lev)
            copy.start()
            field_out.append(copy)

    spread = jnp.broadcast_to(index_ref[...].astype(F32), (slots, slots))
    index = jnp.sum(jnp.where(square, spread, 0.0), axis=1, keepdims=True).astype(jnp.int32)
    row = lax.shift_right_logical(index, 7)
    col = lax.bitwise_and(index, 127)
    live = jnp.where(iota((slots, 1), 0) < count_ref[...], 1.0, 0.0)
    row_wide = jnp.broadcast_to(row, (slots, 128))
    lane_wide = iota((slots, 128), 1)
    last = (rows - 1) * 128
    for b in range(3):
        cast[:, b * 128 : (b + 1) * 128] = jnp.where(lane_wide == col + (b - 1), 1.0, 0.0).astype(BF16)

    def pick_row(r):
        hit = row_wide == r
        for b in range(3):
            column_b = cast[:, b * 128 : (b + 1) * 128].astype(F32)
            pick[b, :, pl.ds(pl.multiple_of(r * 128, 128), 128)] = jnp.where(hit, column_b, 0.0).astype(BF16)

    loop(rows, pick_row)

    for a in range(3):
        line = row + (a - 1)
        above = (line < 0) & (lat > 0)
        below = (line >= rows) & (lat < n_lat - 1)
        inside = (line >= 0) & (line < rows)
        for n, b in enumerate((0, 2)):
            first, upper, lower = (0, 64, 96) if b == 0 else (32, 80, 112)
            out = (col == 0) if b == 0 else (col == 127)
            target = jnp.where(inside, first + line, jnp.where(above, upper, jnp.where(below, lower, -1)))
            target = jnp.where(out, target, -1)
            side_pick[n * 3 + a] = jnp.where(lane_wide == target, 1.0, 0.0).astype(BF16)

    j = iota((128, 1), 0)
    spot = jnp.where(j < 32, j * 128 + 127, (j - 32) * 128)
    for at, cell in ((64, last + 127), (80, last), (96, 127), (112, 0)):
        spot = jnp.where(j == at, cell, jnp.where(j > at, -1, spot))

    def edge_block(i):
        start = pl.multiple_of(i * 512, 512)
        edge[:, pl.ds(start, 512)] = jnp.where(iota((128, 512), 1) + start == spot, 1.0, 0.0).astype(BF16)

    loop(cells // 512, edge_block)

    field_copy(0, 3, lax.rem(lev + 1, n_lev)).wait_recv()
    part = pl.ds(pl.multiple_of(lax.rem(lev + 1, n_lev) * own, 16), own // sets)
    onward = pltpu.make_async_remote_copy(
        src_ref=fields.at[part],
        dst_ref=fields.at[part],
        send_sem=field_send.at[0, 1],
        recv_sem=field_recv.at[0, 1],
        device_id=peer(3),
        device_id_type=MESH,
    )
    onward.start()
    field_out.append(onward)

    def turn(t):
        conv_t[t] = dot_nt(eye[...], conv[:, t].reshape(groups * hidden, chans)).astype(BF16)

    loop(9, turn, 3)
    for load in loads[6:]:
        load.wait()
    for p in range(sets):
        for d in range(1, n_lev):
            if (p, d) != (0, 3):
                field_copy(p, d, lax.rem(lev + n_lev - d, n_lev)).wait_recv()

    blocks = fields.shape[0] // 256
    for i in range(blocks):
        part = slice(i * 256, (i + 1) * 256)
        fields_t[:, part] = dot_nt(eye[...], fields[part, :]).astype(BF16)

    def column(i):
        part = pl.ds(pl.multiple_of(i * 256, 256), 256)
        value, slope = gelu_slope(dot_nt(fields_t[...], inner[part, :]))
        slope_col[:, part] = slope
        act_col[:, part] = value.astype(BF16)

    loop(inner.shape[0] // 256, column, 4)

    def compare(i):
        part = pl.ds(pl.multiple_of(i * 256, 256), 256)
        forecast = fields_t[:, part].astype(F32) + dot_nt(act_col[...], outer[part, :])
        value = (forecast - obs[:, part]) * live * weight_ref[:, part]
        misfit[:, part] = value
        cast[:, part] = value.astype(BF16)

    loop(blocks, compare, 3)

    def column_back(i):
        part = pl.ds(pl.multiple_of(i * 256, 256), 256)
        act_col[:, part] = (dot_nn(cast[...], outer[:, part]) * slope_col[:, part]).astype(BF16)

    loop(inner.shape[0] // 256, column_back, 4)

    def fields_back(i):
        part = pl.ds(pl.multiple_of(i * 256, 256), 256)
        fields_t[:, part] = (misfit[:, part] + dot_nn(act_col[...], inner[:, part])).astype(BF16)

    loop(blocks, fields_back, 3)
    act[...] = (dot_nn(fields_t[...], out_pad[...]) * slope_two[...]).astype(BF16)
    for g in range(groups):
        part = slice(g * hidden, (g + 1) * hidden)
        slope_one[:, part] = slope_one[:, part] * dot_nn(act[:, part], mid_ref[g])
    act[...] = slope_one[...].astype(BF16)

    above_lev, below_lev, across = lax.rem(lev + 1, n_lev), lax.rem(lev + 3, n_lev), lax.rem(lev + 2, n_lev)
    half = 3 * portion // 2
    low_half, high_half = pl.ds(0, half), pl.ds(half, half)

    def send(src, dst, sems, device):
        return pltpu.make_async_remote_copy(
            src_ref=src,
            dst_ref=dst,
            send_sem=sems[0],
            recv_sem=sems[1],
            device_id=(device, lat, lon),
            device_id_type=MESH,
        )

    def relay_copies(b):
        return [
            send(taps.at[b, across, low_half], relay_in.at[b, 0], (relay_send.at[b, 0], relay_recv.at[b, 0]), above_lev),
            send(taps.at[b, across, high_half], relay_in.at[b, 1], (relay_send.at[b, 1], relay_recv.at[b, 1]), below_lev),
        ]

    def taps_copies(b):
        sources = (
            (relay_out.at[b, 0], above_lev),
            (taps.at[b, above_lev, high_half], above_lev),
            (taps.at[b, below_lev, low_half], below_lev),
            (relay_out.at[b, 1], below_lev),
        )
        return [
            send(src, taps_in.at[b, n], (taps_send.at[b, n], taps_recv.at[b, n]), device)
            for n, (src, device) in enumerate(sources)
        ]

    relays = [relay_copies(b) for b in range(3)]
    shares = [taps_copies(b) for b in range(3)]
    for b in range(3):

        def back(a, b=b):
            part = dot_nt(conv_t[a * 3 + b], act[...]).astype(BF16)
            for d in range(n_lev):
                taps[b, d, pl.ds(pl.multiple_of(a * portion, 16), portion), :] = part[
                    d * portion : (d + 1) * portion
                ]

        loop(3, back, 3)
        for copy in relays[b]:
            copy.start()
    for b in range(3):
        shares[b][1].start()
        shares[b][2].start()

    upper = jnp.zeros((chans, 128), F32)
    lower = jnp.zeros((chans, 128), F32)
    beside = jnp.zeros((chans, 128), F32)
    for b in range(3):
        tap_b = [taps[b, :, a * portion : (a + 1) * portion, :].reshape(chans, slots) for a in range(3)]
        upper = upper + dot_nn(tap_b[0], pick[b, :, 0:128])
        lower = lower + dot_nn(tap_b[2], pick[b, :, last : last + 128])
        if b != 1:
            for a in range(3):
                beside = beside + dot_nn(tap_b[a], side_pick[(b // 2) * 3 + a])
    row_send[0] = (upper * has_north).astype(BF16)
    row_send[1] = (lower * has_south).astype(BF16)
    side_out[...] = dot_nt(eye[0:128, 0:128], beside.astype(BF16)).astype(BF16)
    back_copies = [(row_send.at[0], row_in.at[0], (-1, 0)), (row_send.at[1], row_in.at[1], (1, 0))]
    back_sides = [(0, 32, (0, -1)), (32, 32, (0, 1)), (64, 16, (-1, -1)), (80, 16, (-1, 1)), (96, 16, (1, -1)), (112, 16, (1, 1))]
    for first, length, where in back_sides:
        back_copies.append((side_out.at[pl.ds(first, length)], side_in.at[pl.ds(first, length)], where))
    back_copies = [
        pltpu.make_async_remote_copy(
            src_ref=src,
            dst_ref=dst,
            send_sem=back_send.at[n],
            recv_sem=back_recv.at[n],
            device_id=tile(*where),
            device_id_type=MESH,
        )
        for n, (src, dst, where) in enumerate(back_copies)
    ]
    for copy in back_copies:
        copy.start()

    for b in range(3):
        for copy in relays[b]:
            copy.wait_recv()
        for n, (device, part) in enumerate(((above_lev, low_half), (below_lev, high_half))):
            mine = taps[b, device, part, :].astype(F32)
            relay_out[b, n] = (mine + relay_in[b, n].astype(F32)).astype(BF16)
        shares[b][0].start()
        shares[b][3].start()

    for copy in back_copies:
        copy.wait_recv()
    for n in range(2):
        strips[:, :, n * 128 : (n + 1) * 128] = row_in[n].reshape(n_lev, portion, 128)
    strips[:, :, 256:384] = dot_nt(eye[...], side_in[...]).astype(BF16).reshape(n_lev, portion, 128)
    strip_copies = [
        send(strips.at[lax.rem(lev + d, n_lev)], strips_in.at[d - 1], (strip_send.at[d - 1], strip_recv.at[d - 1]), lax.rem(lev + d, n_lev))
        for d in (2, 1, 3)
    ]
    for copy in strip_copies:
        copy.start()

    for b in range(3):
        for copy in shares[b]:
            copy.wait_recv()
        halves = []
        for part, first, second in ((low_half, 0, 2), (high_half, 1, 3)):
            total = taps[b, lev, part, :].astype(F32)
            halves.append(total + taps_in[b, first].astype(F32) + taps_in[b, second].astype(F32))
        summed[b] = jnp.concatenate(halves, axis=0).astype(BF16)

        def scatter(i, b=b):
            here = pl.ds(pl.multiple_of(i * 512, 512), 512)
            after = pl.ds(pl.multiple_of(i * 512 + 128, 128), 512)
            part = dot_nn(summed[b], pick[b, :, here])
            if b == 0:
                up_part[:, here] = part[0:portion]
                mid_part[:, here] = part[portion : 2 * portion]
                down_part[:, after] = part[2 * portion :]
            else:
                up_part[:, here] += part[0:portion]
                mid_part[:, here] += part[portion : 2 * portion]
                down_part[:, after] += part[2 * portion :]

        loop(cells // 512, scatter, 8)

    for copy in strip_copies:
        copy.wait_recv()
    strip = strips[lev].astype(F32)
    for d in range(1, n_lev):
        strip = strip + strips_in[d - 1].astype(F32)
    up_part[:, cells : cells + 128] = strip[:, 0:128]
    down_part[:, 0:128] = strip[:, 128:256]
    block = strip[:, 256:384].astype(BF16)

    def finish(i):
        start = i * 1024
        here = pl.ds(pl.multiple_of(start, 1024), 1024)
        below = pl.ds(pl.multiple_of(start + 128, 128), 1024)
        total = up_part[:, below] + mid_part[:, here] + down_part[:, here] + dot_nn(block, edge[:, here])
        for n in range(8):
            mine = slab[i * 8 + n, pl.ds(pl.multiple_of(lev * portion, 16), portion), :].astype(F32)
            grad_ref[pl.ds(i * 8 + n, portion, stride=rows), :] = mine + total[:, n * 128 : (n + 1) * 128]

    loop(rows // 8, finish, 4)
    for copy in halo + field_out + sum(relays, []) + sum(shares, []) + back_copies + strip_copies:
        copy.wait_send()


def per_device(
    latent,
    conv_weight,
    mid_weight,
    out_weight,
    vertical_inner_matrix,
    vertical_outer_matrix,
    obs_values,
    obs_weight,
    obs_index,
    obs_count,
):
    chans, rows, cols = latent.shape
    groups, hidden = conv_weight.shape[:2]
    slots, channels = obs_values.shape[2:]
    n_lev = lax.axis_size("lev")
    cells = rows * cols
    portion = chans // n_lev
    width = groups * hidden
    column = vertical_inner_matrix.shape[0]
    conv = conv_weight.transpose(0, 2, 1, 3)
    half = 3 * portion // 2
    vmem = pltpu.VMEM
    dma = pltpu.SemaphoreType.DMA
    operands = [
        latent.reshape(chans * rows, cols),
        conv,
        mid_weight,
        out_weight,
        vertical_inner_matrix,
        vertical_outer_matrix,
        obs_values.reshape(slots, channels),
        obs_weight,
        obs_index.reshape(1, slots),
    ]
    operands = [pltpu.with_memory_space_constraint(x, pltpu.HBM) for x in operands]
    grad = pl.pallas_call(
        kernel,
        out_shape=jax.ShapeDtypeStruct((portion * rows, cols), F32),
        in_specs=[pl.BlockSpec(memory_space=pl.ANY)] * 10,
        out_specs=pl.BlockSpec(memory_space=pltpu.VMEM),
        scratch_shapes=[
            vmem((chans * rows, cols), BF16),
            vmem(conv.shape, BF16),
            vmem(mid_weight.shape, BF16),
            vmem(out_weight.shape, BF16),
            vmem(vertical_inner_matrix.shape, BF16),
            vmem(vertical_outer_matrix.shape, BF16),
            vmem((slots, channels), F32),
            vmem((1, channels), F32),
            vmem((1, slots), jnp.int32),
            vmem((1, 1), jnp.int32),
            pltpu.SMEM((1, slots), jnp.int32),
            vmem((rows, chans, cols), BF16),
            vmem(((rows + 2) * 2 * (cols + 8), 128), F32),
            vmem((slots * 24, 128), F32),
            vmem((9, slots, chans), BF16),
            vmem((9, chans, width), BF16),
            vmem((3, slots, cells), BF16),
            vmem((128, cells), BF16),
            vmem((6, slots, 128), BF16),
            vmem((2 * rows + 32, chans), F32),
            vmem((2 * rows + 32, chans), F32),
            vmem((2, cols, chans), BF16),
            vmem((cols, chans), BF16),
            vmem((cols, chans), BF16),
            vmem((slots, width), F32),
            vmem((slots, width), BF16),
            vmem((slots, width), F32),
            vmem((slots, width), F32),
            vmem((slots, column), BF16),
            vmem((slots, column), F32),
            vmem((channels, slots), BF16),
            vmem((slots, channels), BF16),
            vmem((slots, channels), BF16),
            vmem((slots, channels), F32),
            vmem((channels, width), BF16),
            vmem((slots, slots), BF16),
            vmem((3, n_lev, 3 * portion, slots), BF16),
            vmem((3, 2, half, slots), BF16),
            vmem((3, 2, half, slots), BF16),
            vmem((3, 4, half, slots), BF16),
            vmem((3, 3 * portion, slots), BF16),
            vmem((portion, cells + cols), F32),
            vmem((portion, cells), F32),
            vmem((portion, cells + cols), F32),
            vmem((2, chans, cols), BF16),
            vmem((2, chans, cols), BF16),
            vmem((128, chans), BF16),
            vmem((128, chans), BF16),
            vmem((n_lev, portion, 3 * cols), BF16),
            vmem((n_lev - 1, portion, 3 * cols), BF16),
            dma((4,)),
            dma((10,)),
            dma((8,)),
            dma((8,)),
            dma((2, n_lev - 1)),
            dma((2, n_lev - 1)),
            dma((3, 2)),
            dma((3, 2)),
            dma((3, 4)),
            dma((3, 4)),
            dma((8,)),
            dma((8,)),
            dma((n_lev - 1,)),
            dma((n_lev - 1,)),
        ],
        compiler_params=pltpu.CompilerParams(
            collective_id=0, has_side_effects=True, vmem_limit_bytes=50 * 1024 * 1024
        ),
        name="slots_step",
    )(*operands, obs_count)
    return grad.reshape(portion, rows, cols)


def solution(mesh):
    return jax.shard_map(
        per_device,
        mesh=mesh,
        in_specs=(
            P(None, "lat", "lon"),
            P("lev", None, None, None),
            P("lev", None, None),
            P("lev", None, None),
            P(),
            P(),
            P("lat", "lon", None, None),
            P(),
            P("lat", "lon", None),
            P("lat", "lon"),
        ),
        out_specs=P("lev", "lat", "lon"),
        check_vma=False,
    )
```

```python
import functools

import jax
import jax.numpy as jnp
from jax import lax
from jax.experimental import pallas as pl
from jax.experimental.pallas import tpu as pltpu
from jax.sharding import PartitionSpec as P

KAPPA = 0.7978845608028654
CUBIC = 0.044715
F32 = jnp.float32
BF16 = jnp.bfloat16
MESH = pl.DeviceIdType.MESH


def gelu_slope(pre):
    square = pre * pre
    half = 0.5 + 0.5 * jnp.tanh(pre * (KAPPA + KAPPA * CUBIC * square))
    value = pre * half
    slope = half + value * (1.0 - half) * (2.0 * KAPPA + 6.0 * KAPPA * CUBIC * square)
    return (value, slope)


def dot_nn(x, y):
    return lax.dot_general(x, y, (((1,), (0,)), ((), ())), preferred_element_type=F32)


def dot_nt(x, y):
    return lax.dot_general(x, y, (((1,), (1,)), ((), ())), preferred_element_type=F32)


def iota(shape, dim):
    return lax.broadcasted_iota(jnp.int32, shape, dim)


def loop(count, body, unroll=1):
    def step(i, carry):
        body(i)
        return carry

    lax.fori_loop(0, count, step, 0, unroll=unroll)


def kernel(
    latent_hbm,
    conv_hbm,
    mid_hbm,
    out_hbm,
    inner_hbm,
    outer_hbm,
    obs_hbm,
    weight_hbm,
    index_hbm,
    count_hbm,
    grad_ref,
    raw,
    conv,
    mid_ref,
    out_ref,
    inner,
    outer,
    obs,
    weight_ref,
    index_ref,
    count_ref,
    index_smem,
    slab,
    table,
    patch,
    patches,
    conv_t,
    pick,
    edge,
    side_pick,
    side_send,
    side,
    row_out,
    north,
    south,
    pre,
    act,
    slope_one,
    slope_two,
    act_col,
    slope_col,
    fields,
    fields_t,
    cast,
    misfit,
    out_pad,
    eye,
    taps,
    relay_in,
    relay_out,
    taps_in,
    summed,
    up_part,
    mid_part,
    down_part,
    row_send,
    row_in,
    side_out,
    side_in,
    strips,
    strips_in,
    first_sem,
    load_sem,
    halo_send,
    halo_recv,
    field_send,
    field_recv,
    relay_send,
    relay_recv,
    taps_send,
    taps_recv,
    back_send,
    back_recv,
    strip_send,
    strip_recv,
):
    lev, lat, lon = lax.axis_index("lev"), lax.axis_index("lat"), lax.axis_index("lon")
    n_lev, n_lat, n_lon = lax.axis_size("lev"), lax.axis_size("lat"), lax.axis_size("lon")
    slots = pick.shape[1]
    cells = pick.shape[2]
    chans = slab.shape[1]
    rows = cells // 128
    groups, hidden = mid_ref.shape[:2]
    levels = out_ref.shape[1]
    own = groups * levels
    portion = chans // n_lev
    pitch = table.shape[0] // (rows + 2)

    pairs = (
        (index_hbm, index_smem),
        (index_hbm, index_ref),
        (count_hbm, count_ref),
        (conv_hbm, conv),
        (mid_hbm, mid_ref),
        (out_hbm, out_ref),
        (inner_hbm, inner),
        (outer_hbm, outer),
        (obs_hbm, obs),
        (weight_hbm, weight_ref.at[0]),
    )
    loads = [pltpu.make_async_copy(src, dst, load_sem.at[n]) for n, (src, dst) in enumerate(pairs)]
    pieces = 4
    first_loads = []
    for n in range(pieces):
        part = pl.ds(n * (raw.shape[0] // pieces), raw.shape[0] // pieces)
        first_loads.append(pltpu.make_async_copy(latent_hbm.at[part], raw.at[part], first_sem.at[n]))
    for load in first_loads + loads[:3]:
        load.start()

    def tile(dlat, dlon):
        return (lev, lax.rem(lat + dlat + n_lat, n_lat), lax.rem(lon + dlon + n_lon, n_lon))

    def peer(d):
        return (lax.rem(lev + d, n_lev), lat, lon)

    around = [(x, y) for x in (-1, 0, 1) for y in (-1, 0, 1) if (x, y) != (0, 0)]
    barrier = pltpu.get_barrier_semaphore()
    for x, y in around:
        pl.semaphore_signal(barrier, inc=1, device_id=tile(x, y), device_id_type=MESH)
    for d in range(1, n_lev):
        pl.semaphore_signal(barrier, inc=1, device_id=peer(d), device_id_type=MESH)

    square = iota((slots, slots), 0) == iota((slots, slots), 1)
    eye[...] = jnp.where(square, 1.0, 0.0).astype(BF16)
    order = iota((slots, 1), 0)
    order = lax.bitwise_and(order, 7) * rows + lax.shift_right_logical(order, 3)
    order = jnp.where(iota((slots, slots), 1) == order, 1.0, 0.0).astype(BF16)

    def relayout(i):
        start = i * 16 * rows
        parts = [
            dot_nn(order, raw[pl.ds(start + h * 8 * rows, 8 * rows), :]).reshape(rows, 8, 128) for h in range(2)
        ]
        slab[:, pl.ds(i * 16, 16), :] = jnp.concatenate(parts, axis=1).astype(BF16)

    for n, load in enumerate(first_loads):
        load.wait()
        if n == pieces - 1:
            for later in loads[3:]:
                later.start()
        for i in range(chans // 16 // pieces):
            relayout(n * (chans // 16 // pieces) + i)

    def put_row(line, value):
        start = line * pitch + 2
        table[pl.ds(start, 128, stride=2), :] = value[:, 0:128]
        table[pl.ds(start + 1, 128, stride=2), :] = value[:, 128:256]

    def table_row(r):
        put_row(r + 1, dot_nt(eye[0:128, 0:128], slab[r]))

    loop(rows, table_row, rows)

    for n, line in ((0, 0), (1, rows - 1)):
        row_out[n] = dot_nt(eye[0:128, 0:128], slab[line]).astype(BF16)
    for h in range(2):
        part = slice(h * 128, (h + 1) * 128)
        side_send[0:rows, part] = table[pl.ds(pitch + 256 + h, rows, stride=pitch), :]
        side_send[rows : 2 * rows, part] = table[pl.ds(pitch + 2 + h, rows, stride=pitch), :]
        for n, at in enumerate(
            (rows * pitch + 256, rows * pitch + 2, pitch + 256, pitch + 2)
        ):
            first = 2 * rows + 8 * n
            side_send[first : first + 8, part] = jnp.broadcast_to(table[at + h : at + h + 1, :], (8, 128))

    pl.semaphore_wait(barrier, len(around) + n_lev - 1)
    halo = [(row_out.at[0], south, (-1, 0)), (row_out.at[1], north, (1, 0))]
    sides = [(0, 32, (0, 1)), (32, 32, (0, -1)), (64, 8, (1, 1)), (72, 8, (1, -1)), (80, 8, (-1, 1)), (88, 8, (-1, -1))]
    for first, length, where in sides:
        halo.append((side_send.at[pl.ds(first, length)], side.at[pl.ds(first, length)], where))
    halo = [
        pltpu.make_async_remote_copy(
            src_ref=src,
            dst_ref=dst,
            send_sem=halo_send.at[n],
            recv_sem=halo_recv.at[n],
            device_id=tile(*where),
            device_id_type=MESH,
        )
        for n, (src, dst, where) in enumerate(halo)
    ]
    for copy in halo:
        copy.start()

    out_pad[...] = jnp.zeros(out_pad.shape, BF16)
    for load in loads[:6]:
        load.wait()
    for g in range(groups):
        part = pl.ds(pl.multiple_of(lev * own + g * levels, 16), levels)
        out_pad[part, g * hidden : (g + 1) * hidden] = out_ref[g]

    for copy in halo:
        copy.wait_recv()
    has_north = jnp.where(lat > 0, 1.0, 0.0)
    has_south = jnp.where(lat < n_lat - 1, 1.0, 0.0)
    put_row(0, north[...].astype(F32) * has_north)
    put_row(rows + 1, south[...].astype(F32) * has_south)
    for h in range(2):
        part = slice(h * 128, (h + 1) * 128)
        table[pl.ds(pitch + h, rows, stride=pitch), :] = side[0:rows, part]
        table[pl.ds(pitch + 258 + h, rows, stride=pitch), :] = side[rows : 2 * rows, part]
        low = (rows + 1) * pitch
        for n, (at, scale) in enumerate(((0, has_north), (258, has_north), (low, has_south), (low + 258, has_south))):
            first = 2 * rows + 8 * n
            table[at + h : at + h + 1, :] = side[first : first + 1, part] * scale

    def slot_patch(k):
        where = index_smem[0, k]
        start = lax.shift_right_logical(where, 7) * pitch + lax.bitwise_and(where, 127) * 2
        for a in range(3):
            patch[pl.ds(pl.multiple_of(k * 24 + a * 8, 8), 8), :] = table[pl.ds(start + a * pitch, 8), :]

    loop(slots, slot_patch, 64)

    step = 64
    sets = 2
    per_set = groups // sets

    def field_copy(p, d, source):
        part = pl.ds(pl.multiple_of(source * own + p * (own // sets), 16), own // sets)
        return pltpu.make_async_remote_copy(
            src_ref=fields.at[part],
            dst_ref=fields.at[part],
            send_sem=field_send.at[p, d - 1],
            recv_sem=field_recv.at[p, d - 1],
            device_id=peer(d),
            device_id_type=MESH,
        )

    field_out = []
    for p in range(sets):
        span = slice(p * per_set * hidden, (p + 1) * per_set * hidden)
        first = p * per_set
        total = None
        for t in range(9):
            if p == 0:
                parts = [patch[pl.ds((t // 3) * 8 + (t % 3) * 2 + h, slots, stride=24), :] for h in range(2)]
                patches[t] = jnp.concatenate(parts, axis=1).astype(BF16)
            kernel_t = conv[first : first + per_set, t].reshape(per_set * hidden, chans)
            part = dot_nt(patches[t], kernel_t)
            total = part if total is None else total + part
        pre[:, span] = total

        def gelu_one(i, span=span):
            part = pl.ds(pl.multiple_of(i * step, step), step)
            value, slope = gelu_slope(pre[part, span])
            act[part, span] = value.astype(BF16)
            slope_one[part, span] = slope

        def gelu_two(i, span=span):
            part = pl.ds(pl.multiple_of(i * step, step), step)
            value, slope = gelu_slope(pre[part, span])
            act[part, span] = value.astype(BF16)
            slope_two[part, span] = slope

        loop(slots // step, gelu_one, 4)
        for g in range(first, first + per_set):
            part = slice(g * hidden, (g + 1) * hidden)
            pre[:, part] = dot_nt(act[:, part], mid_ref[g])
        loop(slots // step, gelu_two, 4)
        for g in range(first, first + per_set):
            part = slice(g * hidden, (g + 1) * hidden)
            fields[pl.ds(pl.multiple_of(lev * own + g * levels, 16), levels), :] = dot_nt(
                out_ref[g], act[:, part]
            ).astype(BF16)
        for d in (1, 3) if p == 0 else (2, 1, 3):
            copy = field_copy(p, d, lev)
            copy.start()
            field_out.append(copy)

    spread = jnp.broadcast_to(index_ref[...].astype(F32), (slots, slots))
    index = jnp.sum(jnp.where(square, spread, 0.0), axis=1, keepdims=True).astype(jnp.int32)
    row = lax.shift_right_logical(index, 7)
    col = lax.bitwise_and(index, 127)
    live = jnp.where(iota((slots, 1), 0) < count_ref[...], 1.0, 0.0)
    row_wide = jnp.broadcast_to(row, (slots, 128))
    lane_wide = iota((slots, 128), 1)
    last = (rows - 1) * 128
    for b in range(3):
        cast[:, b * 128 : (b + 1) * 128] = jnp.where(lane_wide == col + (b - 1), 1.0, 0.0).astype(BF16)

    def pick_row(r):
        hit = row_wide == r
        for b in range(3):
            column_b = cast[:, b * 128 : (b + 1) * 128].astype(F32)
            pick[b, :, pl.ds(pl.multiple_of(r * 128, 128), 128)] = jnp.where(hit, column_b, 0.0).astype(BF16)

    loop(rows, pick_row)

    for a in range(3):
        line = row + (a - 1)
        above = (line < 0) & (lat > 0)
        below = (line >= rows) & (lat < n_lat - 1)
        inside = (line >= 0) & (line < rows)
        for n, b in enumerate((0, 2)):
            first, upper, lower = (0, 64, 96) if b == 0 else (32, 80, 112)
            out = (col == 0) if b == 0 else (col == 127)
            target = jnp.where(inside, first + line, jnp.where(above, upper, jnp.where(below, lower, -1)))
            target = jnp.where(out, target, -1)
            side_pick[n * 3 + a] = jnp.where(lane_wide == target, 1.0, 0.0).astype(BF16)

    j = iota((128, 1), 0)
    spot = jnp.where(j < 32, j * 128 + 127, (j - 32) * 128)
    for at, cell in ((64, last + 127), (80, last), (96, 127), (112, 0)):
        spot = jnp.where(j == at, cell, jnp.where(j > at, -1, spot))

    def edge_block(i):
        start = pl.multiple_of(i * 512, 512)
        edge[:, pl.ds(start, 512)] = jnp.where(iota((128, 512), 1) + start == spot, 1.0, 0.0).astype(BF16)

    loop(cells // 512, edge_block)

    field_copy(0, 3, lax.rem(lev + 1, n_lev)).wait_recv()
    part = pl.ds(pl.multiple_of(lax.rem(lev + 1, n_lev) * own, 16), own // sets)
    onward = pltpu.make_async_remote_copy(
        src_ref=fields.at[part],
        dst_ref=fields.at[part],
        send_sem=field_send.at[0, 1],
        recv_sem=field_recv.at[0, 1],
        device_id=peer(3),
        device_id_type=MESH,
    )
    onward.start()
    field_out.append(onward)

    def turn(t):
        conv_t[t] = dot_nt(eye[...], conv[:, t].reshape(groups * hidden, chans)).astype(BF16)

    loop(9, turn, 3)
    for load in loads[6:]:
        load.wait()
    for p in range(sets):
        for d in range(1, n_lev):
            if (p, d) != (0, 3):
                field_copy(p, d, lax.rem(lev + n_lev - d, n_lev)).wait_recv()

    blocks = fields.shape[0] // 256
    for i in range(blocks):
        part = slice(i * 256, (i + 1) * 256)
        fields_t[:, part] = dot_nt(eye[...], fields[part, :]).astype(BF16)

    def column(i):
        part = pl.ds(pl.multiple_of(i * 256, 256), 256)
        value, slope = gelu_slope(dot_nt(fields_t[...], inner[part, :]))
        slope_col[:, part] = slope
        act_col[:, part] = value.astype(BF16)

    loop(inner.shape[0] // 256, column, 4)

    def compare(i):
        part = pl.ds(pl.multiple_of(i * 256, 256), 256)
        forecast = fields_t[:, part].astype(F32) + dot_nt(act_col[...], outer[part, :])
        value = (forecast - obs[:, part]) * live * weight_ref[:, part]
        misfit[:, part] = value
        cast[:, part] = value.astype(BF16)

    loop(blocks, compare, 3)

    def column_back(i):
        part = pl.ds(pl.multiple_of(i * 256, 256), 256)
        act_col[:, part] = (dot_nn(cast[...], outer[:, part]) * slope_col[:, part]).astype(BF16)

    loop(inner.shape[0] // 256, column_back, 4)

    def fields_back(i):
        part = pl.ds(pl.multiple_of(i * 256, 256), 256)
        fields_t[:, part] = (misfit[:, part] + dot_nn(act_col[...], inner[:, part])).astype(BF16)

    loop(blocks, fields_back, 3)
    act[...] = (dot_nn(fields_t[...], out_pad[...]) * slope_two[...]).astype(BF16)
    for g in range(groups):
        part = slice(g * hidden, (g + 1) * hidden)
        slope_one[:, part] = slope_one[:, part] * dot_nn(act[:, part], mid_ref[g])
    act[...] = slope_one[...].astype(BF16)

    above_lev, below_lev, across = lax.rem(lev + 1, n_lev), lax.rem(lev + 3, n_lev), lax.rem(lev + 2, n_lev)
    half = 3 * portion // 2
    low_half, high_half = pl.ds(0, half), pl.ds(half, half)

    def send(src, dst, sems, device):
        return pltpu.make_async_remote_copy(
            src_ref=src,
            dst_ref=dst,
            send_sem=sems[0],
            recv_sem=sems[1],
            device_id=(device, lat, lon),
            device_id_type=MESH,
        )

    def relay_copies(b):
        return [
            send(taps.at[b, across, low_half], relay_in.at[b, 0], (relay_send.at[b, 0], relay_recv.at[b, 0]), above_lev),
            send(taps.at[b, across, high_half], relay_in.at[b, 1], (relay_send.at[b, 1], relay_recv.at[b, 1]), below_lev),
        ]

    def taps_copies(b):
        sources = (
            (relay_out.at[b, 0], above_lev),
            (taps.at[b, above_lev, high_half], above_lev),
            (taps.at[b, below_lev, low_half], below_lev),
            (relay_out.at[b, 1], below_lev),
        )
        return [
            send(src, taps_in.at[b, n], (taps_send.at[b, n], taps_recv.at[b, n]), device)
            for n, (src, device) in enumerate(sources)
        ]

    relays = [relay_copies(b) for b in range(3)]
    shares = [taps_copies(b) for b in range(3)]
    for b in range(3):

        def back(a, b=b):
            part = dot_nt(conv_t[a * 3 + b], act[...]).astype(BF16)
            for d in range(n_lev):
                taps[b, d, pl.ds(pl.multiple_of(a * portion, 16), portion), :] = part[
                    d * portion : (d + 1) * portion
                ]

        loop(3, back, 3)
        for copy in relays[b]:
            copy.start()

    upper = jnp.zeros((chans, 128), F32)
    lower = jnp.zeros((chans, 128), F32)
    beside = jnp.zeros((chans, 128), F32)
    for b in range(3):
        tap_b = [taps[b, :, a * portion : (a + 1) * portion, :].reshape(chans, slots) for a in range(3)]
        upper = upper + dot_nn(tap_b[0], pick[b, :, 0:128])
        lower = lower + dot_nn(tap_b[2], pick[b, :, last : last + 128])
        if b != 1:
            for a in range(3):
                beside = beside + dot_nn(tap_b[a], side_pick[(b // 2) * 3 + a])
    row_send[0] = (upper * has_north).astype(BF16)
    row_send[1] = (lower * has_south).astype(BF16)
    side_out[...] = dot_nt(eye[0:128, 0:128], beside.astype(BF16)).astype(BF16)
    back_copies = [(row_send.at[0], row_in.at[0], (-1, 0)), (row_send.at[1], row_in.at[1], (1, 0))]
    back_sides = [(0, 32, (0, -1)), (32, 32, (0, 1)), (64, 16, (-1, -1)), (80, 16, (-1, 1)), (96, 16, (1, -1)), (112, 16, (1, 1))]
    for first, length, where in back_sides:
        back_copies.append((side_out.at[pl.ds(first, length)], side_in.at[pl.ds(first, length)], where))
    back_copies = [
        pltpu.make_async_remote_copy(
            src_ref=src,
            dst_ref=dst,
            send_sem=back_send.at[n],
            recv_sem=back_recv.at[n],
            device_id=tile(*where),
            device_id_type=MESH,
        )
        for n, (src, dst, where) in enumerate(back_copies)
    ]
    for copy in back_copies:
        copy.start()
    for b in range(3):
        shares[b][1].start()
        shares[b][2].start()

    for b in range(3):
        for n, (device, part) in enumerate(((above_lev, low_half), (below_lev, high_half))):
            relays[b][n].wait_recv()
            mine = taps[b, device, part, :].astype(F32)
            relay_out[b, n] = (mine + relay_in[b, n].astype(F32)).astype(BF16)
            shares[b][3 * n].start()

    for copy in back_copies:
        copy.wait_recv()
    for n in range(2):
        strips[:, :, n * 128 : (n + 1) * 128] = row_in[n].reshape(n_lev, portion, 128)
    strips[:, :, 256:384] = dot_nt(eye[...], side_in[...]).astype(BF16).reshape(n_lev, portion, 128)
    strip_copies = [
        send(strips.at[lax.rem(lev + d, n_lev)], strips_in.at[d - 1], (strip_send.at[d - 1], strip_recv.at[d - 1]), lax.rem(lev + d, n_lev))
        for d in (2, 1, 3)
    ]
    for copy in strip_copies:
        copy.start()

    for b in range(3):
        for copy in shares[b]:
            copy.wait_recv()
        halves = []
        for part, first, second in ((low_half, 0, 2), (high_half, 1, 3)):
            total = taps[b, lev, part, :].astype(F32)
            halves.append(total + taps_in[b, first].astype(F32) + taps_in[b, second].astype(F32))
        summed[b] = jnp.concatenate(halves, axis=0).astype(BF16)

        def scatter(i, b=b):
            here = pl.ds(pl.multiple_of(i * 512, 512), 512)
            after = pl.ds(pl.multiple_of(i * 512 + 128, 128), 512)
            part = dot_nn(summed[b], pick[b, :, here])
            if b == 0:
                up_part[:, here] = part[0:portion]
                mid_part[:, here] = part[portion : 2 * portion]
                down_part[:, after] = part[2 * portion :]
            else:
                up_part[:, here] += part[0:portion]
                mid_part[:, here] += part[portion : 2 * portion]
                down_part[:, after] += part[2 * portion :]

        loop(cells // 512, scatter, 8)

    for copy in strip_copies:
        copy.wait_recv()
    strip = strips[lev].astype(F32)
    for d in range(1, n_lev):
        strip = strip + strips_in[d - 1].astype(F32)
    up_part[:, cells : cells + 128] = strip[:, 0:128]
    down_part[:, 0:128] = strip[:, 128:256]
    block = strip[:, 256:384].astype(BF16)

    def finish(i):
        start = i * 1024
        here = pl.ds(pl.multiple_of(start, 1024), 1024)
        below = pl.ds(pl.multiple_of(start + 128, 128), 1024)
        total = up_part[:, below] + mid_part[:, here] + down_part[:, here] + dot_nn(block, edge[:, here])
        for n in range(8):
            mine = slab[i * 8 + n, pl.ds(pl.multiple_of(lev * portion, 16), portion), :].astype(F32)
            grad_ref[pl.ds(i * 8 + n, portion, stride=rows), :] = mine + total[:, n * 128 : (n + 1) * 128]

    loop(rows // 8, finish, 4)
    for copy in halo + field_out + sum(relays, []) + sum(shares, []) + back_copies + strip_copies:
        copy.wait_send()


def per_device(
    latent,
    conv_weight,
    mid_weight,
    out_weight,
    vertical_inner_matrix,
    vertical_outer_matrix,
    obs_values,
    obs_weight,
    obs_index,
    obs_count,
):
    chans, rows, cols = latent.shape
    groups, hidden = conv_weight.shape[:2]
    slots, channels = obs_values.shape[2:]
    n_lev = lax.axis_size("lev")
    cells = rows * cols
    portion = chans // n_lev
    width = groups * hidden
    column = vertical_inner_matrix.shape[0]
    conv = conv_weight.transpose(0, 2, 1, 3)
    half = 3 * portion // 2
    vmem = pltpu.VMEM
    dma = pltpu.SemaphoreType.DMA
    operands = [
        latent.reshape(chans * rows, cols),
        conv,
        mid_weight,
        out_weight,
        vertical_inner_matrix,
        vertical_outer_matrix,
        obs_values.reshape(slots, channels),
        obs_weight,
        obs_index.reshape(1, slots),
    ]
    operands = [pltpu.with_memory_space_constraint(x, pltpu.HBM) for x in operands]
    grad = pl.pallas_call(
        kernel,
        out_shape=jax.ShapeDtypeStruct((portion * rows, cols), F32),
        in_specs=[pl.BlockSpec(memory_space=pl.ANY)] * 10,
        out_specs=pl.BlockSpec(memory_space=pltpu.VMEM),
        scratch_shapes=[
            vmem((chans * rows, cols), BF16),
            vmem(conv.shape, BF16),
            vmem(mid_weight.shape, BF16),
            vmem(out_weight.shape, BF16),
            vmem(vertical_inner_matrix.shape, BF16),
            vmem(vertical_outer_matrix.shape, BF16),
            vmem((slots, channels), F32),
            vmem((1, channels), F32),
            vmem((1, slots), jnp.int32),
            vmem((1, 1), jnp.int32),
            pltpu.SMEM((1, slots), jnp.int32),
            vmem((rows, chans, cols), BF16),
            vmem(((rows + 2) * 2 * (cols + 8), 128), F32),
            vmem((slots * 24, 128), F32),
            vmem((9, slots, chans), BF16),
            vmem((9, chans, width), BF16),
            vmem((3, slots, cells), BF16),
            vmem((128, cells), BF16),
            vmem((6, slots, 128), BF16),
            vmem((2 * rows + 32, chans), F32),
            vmem((2 * rows + 32, chans), F32),
            vmem((2, cols, chans), BF16),
            vmem((cols, chans), BF16),
            vmem((cols, chans), BF16),
            vmem((slots, width), F32),
            vmem((slots, width), BF16),
            vmem((slots, width), F32),
            vmem((slots, width), F32),
            vmem((slots, column), BF16),
            vmem((slots, column), F32),
            vmem((channels, slots), BF16),
            vmem((slots, channels), BF16),
            vmem((slots, channels), BF16),
            vmem((slots, channels), F32),
            vmem((channels, width), BF16),
            vmem((slots, slots), BF16),
            vmem((3, n_lev, 3 * portion, slots), BF16),
            vmem((3, 2, half, slots), BF16),
            vmem((3, 2, half, slots), BF16),
            vmem((3, 4, half, slots), BF16),
            vmem((3, 3 * portion, slots), BF16),
            vmem((portion, cells + cols), F32),
            vmem((portion, cells), F32),
            vmem((portion, cells + cols), F32),
            vmem((2, chans, cols), BF16),
            vmem((2, chans, cols), BF16),
            vmem((128, chans), BF16),
            vmem((128, chans), BF16),
            vmem((n_lev, portion, 3 * cols), BF16),
            vmem((n_lev - 1, portion, 3 * cols), BF16),
            dma((4,)),
            dma((10,)),
            dma((8,)),
            dma((8,)),
            dma((2, n_lev - 1)),
            dma((2, n_lev - 1)),
            dma((3, 2)),
            dma((3, 2)),
            dma((3, 4)),
            dma((3, 4)),
            dma((8,)),
            dma((8,)),
            dma((n_lev - 1,)),
            dma((n_lev - 1,)),
        ],
        compiler_params=pltpu.CompilerParams(
            collective_id=0, has_side_effects=True, vmem_limit_bytes=50 * 1024 * 1024
        ),
        name="slots_step",
    )(*operands, obs_count)
    return grad.reshape(portion, rows, cols)


def solution(mesh):
    return jax.shard_map(
        per_device,
        mesh=mesh,
        in_specs=(
            P(None, "lat", "lon"),
            P("lev", None, None, None),
            P("lev", None, None),
            P("lev", None, None),
            P(),
            P(),
            P("lat", "lon", None, None),
            P(),
            P("lat", "lon", None),
            P("lat", "lon"),
        ),
        out_specs=P("lev", "lat", "lon"),
        check_vma=False,
    )
```
